32 devices in a mesh: dp: 16 (over z, y, core), seq: 2 (over x).
Axes of the slice: x: 2, y: 2, z: 4, core: 2. Of those that a mesh axis runs over, the one named last changes fastest.
Arguments:
- clip_tokens: bfloat16 [16, 1024, 1024], P('dp', 'seq'), may hold values from -6 to 6
- adapter_index: int32 [16], P('dp'), may hold values from 0 to 7
- ln1_gain: float32 [1024], replicated, may hold values from 0.25 to 1.75
- ln1_bias: float32 [1024], replicated, may hold values from -1.8 to 1.8
- qkv_weight: bfloat16 [1024, 3072], replicated, may hold values from -0.1875 to 0.1875
- qkv_bias: float32 [3072], replicated, may hold values from -1.8 to 1.8
- qkv_down: bfloat16 [8, 16, 1024], replicated, may hold values from -0.1875 to 0.1875
- qkv_up: bfloat16 [8, 16, 3072], replicated, may hold values from -1.5 to 1.5
- out_weight: bfloat16 [1024, 1024], replicated, may hold values from -3 to 3
- out_bias: float32 [1024], replicated, may hold values from -1.8 to 1.8
- out_down: bfloat16 [8, 16, 1024], replicated, may hold values from -3 to 3
- out_up: bfloat16 [8, 16, 1024], replicated, may hold values from -1.5 to 1.5
- ln2_gain: float32 [1024], replicated, may hold values from 0.25 to 1.75
- ln2_bias: float32 [1024], replicated, may hold values from -1.8 to 1.8
- fc1_weight: bfloat16 [1024, 4096], replicated, may hold values from -0.1875 to 0.1875
- fc1_bias: float32 [4096], replicated, may hold values from -1.8 to 1.8
- fc1_down: bfloat16 [8, 16, 1024], replicated, may hold values from -0.1875 to 0.1875
- fc1_up: bfloat16 [8, 16, 4096], replicated, may hold values from -1.5 to 1.5
- fc2_weight: bfloat16 [4096, 1024], replicated, may hold values from -0.09375 to 0.09375
- fc2_bias: float32 [1024], replicated, may hold values from -1.8 to 1.8
- fc2_down: bfloat16 [8, 16, 4096], replicated, may hold values from -0.09375 to 0.09375
- fc2_up: bfloat16 [8, 16, 1024], replicated, may hold values from -1.5 to 1.5
- cotangent: bfloat16 [16, 1024, 1024], P('dp', 'seq'), may hold values from -6 to 6
Outputs:
- block_output: bfloat16 [16, 1024, 1024], P('dp', 'seq')
- input_grad: float32 [16, 1024, 1024], P('dp', 'seq')
- grad_qkv_down: float32 [8, 16, 1024], replicated
- grad_qkv_up: float32 [8, 16, 3072], replicated
- grad_out_down: float32 [8, 16, 1024], replicated
- grad_out_up: float32 [8, 16, 1024], replicated
- grad_fc1_down: float32 [8, 16, 1024], replicated
- grad_fc1_up: float32 [8, 16, 4096], replicated
- grad_fc2_down: float32 [8, 16, 4096], replicated
- grad_fc2_up: float32 [8, 16, 1024], replicated
The draws below stay inside these ranges and needn't reach their ends.
All inputs are finite; a program needn't handle non-finite values.
Results may differ from the reference program's by a relative error of at most 0.023.
Values may be sent and summed in bfloat16 or wider, within the bound.
No kernel may reach another device: no remote copies, remote signals or barrier semaphores. Data moves between devices by JAX's collectives and lax.ppermute only.
A program may use at most 192 MiB of HBM per device.

```python
import jax
import jax.numpy as jnp
from jax import lax

D = 1024
HEADS = 16
HD = 64
FF = 4096
RANK = 16
NADAPT = 8
GRID = 16
LENGTH = 1024
CLIPS = 16


def plant(array, own_key, smallest, top_value):
    dims = array.shape
    spot = [jax.random.randint(jax.random.fold_in(own_key, axis), (), 0, dims[axis]) for axis in range(len(dims))]
    array = array.at[tuple(spot)].set(smallest)
    longest = dims.index(max(dims))
    spot[longest] = (spot[longest] + 1) % dims[longest]
    return array.at[tuple(spot)].set(top_value)


def levels(rng, dims, split, least, high):
    def one(dim, blocks):
        heights = jax.random.uniform(jax.random.fold_in(jax.random.fold_in(rng, 6), dim), (blocks,), jnp.float32, least / len(split), high / len(split))
        return jnp.repeat(jnp.exp(heights), dims[dim] // blocks).reshape((-1,) + (1,) * (len(dims) - dim - 1))

    level = one(*split[0])
    for cut in split[1:]:
        level = level * one(*cut)
    return level


def bell_draw(key, extent, width, limit, shards=(), kind=jnp.bfloat16):
    level = levels(key, extent, shards, -0.22, 0.18) if shards else 1.0
    drawn = jax.random.normal(key, extent, jnp.float32) * width * level
    return jnp.minimum(jnp.maximum(drawn, -limit), limit).astype(kind)


def setup_inputs(seed: int = 0) -> dict:
    keys = jax.random.split(jax.random.key(seed), 24)
    return {
        "clip_tokens": bell_draw(keys[0], (CLIPS, LENGTH, D), 1.0, 6.0, ((0, 16), (1, 2))),
        "adapter_index": plant(jax.random.randint(keys[1], (CLIPS,), 0, NADAPT), jax.random.fold_in(keys[1], 1), 0, NADAPT - 1).astype(jnp.int32),
        "ln1_gain": jnp.clip(1.0 + 0.15 * jax.random.normal(keys[2], (D,), jnp.float32), 0.25, 1.75),
        "ln1_bias": bell_draw(keys[3], (D,), 0.3, 1.8, (), jnp.float32),
        "qkv_weight": bell_draw(keys[4], (D, 3 * D), D ** -0.5, 0.1875),
        "qkv_bias": bell_draw(keys[5], (3 * D,), 0.3, 1.8, (), jnp.float32),
        "qkv_down": bell_draw(keys[6], (NADAPT, RANK, D), D ** -0.5, 0.1875),
        "qkv_up": bell_draw(keys[7], (NADAPT, RANK, 3 * D), RANK ** -0.5, 1.5),
        "out_weight": bell_draw(keys[8], (D, D), (max(1, 4 * D // LENGTH)) ** -0.5, 3.0),
        "out_bias": bell_draw(keys[9], (D,), 0.3, 1.8, (), jnp.float32),
        "out_down": bell_draw(keys[10], (NADAPT, RANK, D), (max(1, 4 * D // LENGTH)) ** -0.5, 3.0),
        "out_up": bell_draw(keys[11], (NADAPT, RANK, D), RANK ** -0.5, 1.5),
        "ln2_gain": jnp.clip(1.0 + 0.15 * jax.random.normal(keys[12], (D,), jnp.float32), 0.25, 1.75),
        "ln2_bias": bell_draw(keys[13], (D,), 0.3, 1.8, (), jnp.float32),
        "fc1_weight": bell_draw(keys[14], (D, FF), D ** -0.5, 0.1875),
        "fc1_bias": bell_draw(keys[15], (FF,), 0.3, 1.8, (), jnp.float32),
        "fc1_down": bell_draw(keys[16], (NADAPT, RANK, D), D ** -0.5, 0.1875),
        "fc1_up": bell_draw(keys[17], (NADAPT, RANK, FF), RANK ** -0.5, 1.5),
        "fc2_weight": bell_draw(keys[18], (FF, D), FF ** -0.5, 0.09375),
        "fc2_bias": bell_draw(keys[19], (D,), 0.3, 1.8, (), jnp.float32),
        "fc2_down": bell_draw(keys[20], (NADAPT, RANK, FF), FF ** -0.5, 0.09375),
        "fc2_up": bell_draw(keys[21], (NADAPT, RANK, D), RANK ** -0.5, 1.5),
        "cotangent": bell_draw(keys[22], (CLIPS, LENGTH, D), 1.0, 6.0, ((0, 16), (1, 2))),
    }


@jax.custom_vjp
def low(v):
    return lax.optimization_barrier(v.astype(jnp.bfloat16)).astype(jnp.float32)

@jax.custom_vjp
def low_back(v):
    return v

def low_keep(v):
    return (low(v), None)

def low_pass(kept, grad):
    return (grad,)

def back_keep(v):
    return (v, None)

def back_low(kept, grad):
    return (low(grad),)
low.defvjp(low_keep, low_pass)
low_back.defvjp(back_keep, back_low)
EPSILON = 1e-06

def matmul(left, right):
    return jnp.dot(left, right, precision=lax.Precision.HIGHEST, preferred_element_type=jnp.float32)

def layer_norm(values, gain, shift):
    centre = values - lax.optimization_barrier(jnp.mean(values, axis=-1, keepdims=True))
    spread = lax.rsqrt(lax.optimization_barrier(jnp.mean(centre * centre, axis=-1, keepdims=True)) + EPSILON)
    return centre * spread * gain + shift

def rotary_tables(first_token, count_rows, head_size, grid_side):
    half_size = head_size // 2
    side_pairs = half_size // 3
    lead_pairs = half_size - 2 * side_pairs
    token_index = first_token + jnp.arange(count_rows, dtype=jnp.int32)
    frame = token_index // (grid_side * grid_side)
    row_pos = token_index // grid_side % grid_side
    col_pos = token_index % grid_side
    pair_index = jnp.arange(half_size, dtype=jnp.int32)
    axis_pick = jnp.where(pair_index < lead_pairs, 0, jnp.where(pair_index < lead_pairs + side_pairs, 1, 2))
    local_pair = jnp.where(axis_pick == 0, pair_index, jnp.where(axis_pick == 1, pair_index - lead_pairs, pair_index - lead_pairs - side_pairs))
    total_pairs = jnp.where(axis_pick == 0, lead_pairs, side_pairs)
    frequency = jnp.power(10000.0, -local_pair.astype(jnp.float32) / total_pairs.astype(jnp.float32))
    position = jnp.where(axis_pick[None, :] == 0, frame[:, None], jnp.where(axis_pick[None, :] == 1, row_pos[:, None], col_pos[:, None])).astype(jnp.float32)
    angles = position * frequency[None, :]
    return (jnp.cos(angles), jnp.sin(angles))

def rotate(values, cosine, sine):
    half_size = values.shape[-1] // 2
    first_half = values[..., :half_size]
    second_half = values[..., half_size:]
    cos_rows = cosine[:, None, :]
    sin_rows = sine[:, None, :]
    return jnp.concatenate([first_half * cos_rows - second_half * sin_rows, first_half * sin_rows + second_half * cos_rows], axis=-1)

def project(inputs, weight, bias_row, down_table, up_table):
    low_rank = low(low_back(matmul(inputs, down_table.T)))
    return matmul(inputs, weight) + bias_row + matmul(low_rank, up_table)

def attend(queries, key_rows, value_rows):
    length = queries.shape[0]
    block_size = min(length, 512)
    score_scale = HD ** (-0.5)

    def query_block(query_part):
        scores = low_back(jnp.einsum('qhd,khd->hqk', query_part, key_rows, precision=lax.Precision.HIGHEST) * score_scale)
        row_max = lax.optimization_barrier(jnp.max(scores, axis=-1, keepdims=True))
        weights = jnp.exp(scores - row_max)
        attn_prob = low(weights / lax.optimization_barrier(jnp.sum(weights, axis=-1, keepdims=True)))
        return jnp.einsum('hqk,khd->qhd', attn_prob, value_rows, precision=lax.Precision.HIGHEST)
    parts = queries.reshape(length // block_size, block_size, queries.shape[1], queries.shape[2])
    return lax.map(jax.checkpoint(query_block), parts).reshape(length, queries.shape[1] * queries.shape[2])

def clip_forward(inputs, clip_index, frozen, tables):
    ln1_gain, ln1_bias, qkv_weight, qkv_bias, out_weight, out_bias, ln2_gain, ln2_bias, fc1_weight, fc1_bias, fc2_weight, fc2_bias = frozen
    qkv_down, qkv_up, out_down, out_up, fc1_down, fc1_up, fc2_down, fc2_up = tables

    def select(table_rows):
        return lax.dynamic_index_in_dim(table_rows, clip_index, 0, keepdims=False)
    length = inputs.shape[0]
    model_width = inputs.shape[1]
    first_in = low(layer_norm(inputs, ln1_gain, ln1_bias))
    qkv = low_back(project(first_in, qkv_weight, qkv_bias, select(qkv_down), select(qkv_up)))
    cosine, sine = rotary_tables(0, length, HD, GRID)
    queries = low(rotate(qkv[:, :model_width].reshape(length, HEADS, HD), cosine, sine))
    key_rows = low(rotate(qkv[:, model_width:2 * model_width].reshape(length, HEADS, HD), cosine, sine))
    value_rows = low(qkv[:, 2 * model_width:].reshape(length, HEADS, HD))
    mixed_heads = low(low_back(attend(queries, key_rows, value_rows)))
    branch = low_back(project(mixed_heads, out_weight, out_bias, select(out_down), select(out_up)))
    middle = inputs + branch
    second_in = low(layer_norm(middle, ln2_gain, ln2_bias))
    hidden = low_back(project(second_in, fc1_weight, fc1_bias, select(fc1_down), select(fc1_up)))
    active = low(jax.nn.gelu(hidden, approximate=False))
    return middle + low_back(project(active, fc2_weight, fc2_bias, select(fc2_down), select(fc2_up)))

def reference(clip_tokens, adapter_index, ln1_gain, ln1_bias, qkv_weight, qkv_bias, qkv_down, qkv_up, out_weight, out_bias, out_down, out_up, ln2_gain, ln2_bias, fc1_weight, fc1_bias, fc1_down, fc1_up, fc2_weight, fc2_bias, fc2_down, fc2_up, cotangent):
    frozen = tuple((entry.astype(jnp.float32) for entry in (ln1_gain, ln1_bias, qkv_weight, qkv_bias, out_weight, out_bias, ln2_gain, ln2_bias, fc1_weight, fc1_bias, fc2_weight, fc2_bias)))
    tables = tuple((entry.astype(jnp.float32) for entry in (qkv_down, qkv_up, out_down, out_up, fc1_down, fc1_up, fc2_down, fc2_up)))

    def run(inputs, table_set):

        def clip_step(carried, clip_item):
            return (carried, clip_forward(clip_item[0], clip_item[1], frozen, table_set))
        unused, outputs = lax.scan(jax.checkpoint(clip_step), jnp.zeros((), jnp.float32), (inputs, adapter_index))
        return outputs
    outputs, pull_back = jax.vjp(run, clip_tokens.astype(jnp.float32), tables)
    grad_in, grad_tables = pull_back(cotangent.astype(jnp.float32))
    return (outputs.astype(jnp.bfloat16), grad_in, grad_tables[0], grad_tables[1], grad_tables[2], grad_tables[3], grad_tables[4], grad_tables[5], grad_tables[6], grad_tables[7])
```

```python
import functools

import jax
import jax.numpy as jnp
import numpy as np
from jax import lax
from jax.experimental import pallas as pl
from jax.experimental.pallas import tpu as pltpu
from jax.sharding import PartitionSpec as P

HEADS = 16
HD = 64
GRID = 16
NADAPT = 8
RANK = 16
EPSILON = 1e-06
LANES = 128
EXTRA = 48

F32 = jnp.float32
BF16 = jnp.bfloat16
NN = (((1,), (0,)), ((), ()))
NT = (((1,), (1,)), ((), ()))

ERFC = (
    0.16918800211151383,
    0.1707152747822528,
    0.14833885959986734,
    0.21492717178376733,
    -0.09465313901935662,
    0.5477232747113128,
    -0.5122807406271995,
    0.48556441585520754,
    -0.1295231387829952,
)


def dot(a, b, dims=NN):
    return lax.dot_general(a, b, dims, preferred_element_type=F32)


def params(steps=1):
    return pltpu.CompilerParams(
        dimension_semantics=("arbitrary",) * steps, vmem_limit_bytes=60 << 20
    )


def cost(flops, moved, exps=0):
    return pl.CostEstimate(flops=int(flops), bytes_accessed=int(moved), transcendentals=int(exps))


def norm_rows(values):
    centre = values - jnp.mean(values, axis=-1, keepdims=True)
    spread = lax.rsqrt(jnp.mean(centre * centre, axis=-1, keepdims=True) + EPSILON)
    return centre * spread, spread


def norm_back(grad_rows, normed, spread, gain):
    scaled = grad_rows * gain
    first = jnp.mean(scaled, axis=-1, keepdims=True)
    second = jnp.mean(scaled * normed, axis=-1, keepdims=True)
    return spread * (scaled - first - normed * second)


def rotary_tables(length):
    half = HD // 2
    side = half // 3
    lead = half - 2 * side
    token = np.arange(length)
    pair = np.arange(half)
    kind = np.where(pair < lead, 0, np.where(pair < lead + side, 1, 2))
    local = np.where(kind == 0, pair, np.where(kind == 1, pair - lead, pair - lead - side))
    total = np.where(kind == 0, lead, side)
    frequency = np.power(
        np.float32(10000.0), -local.astype(np.float32) / total.astype(np.float32)
    ).astype(np.float32)
    place = np.where(
        kind[None] == 0,
        (token // (GRID * GRID))[:, None],
        np.where(kind[None] == 1, (token // GRID % GRID)[:, None], (token % GRID)[:, None]),
    ).astype(np.float32)
    angle = place * frequency[None]
    cosine, sine = np.cos(angle), np.sin(angle)
    cos_rows = np.concatenate([cosine] * 4, axis=1).astype(np.float32)
    sin_rows = np.concatenate([-sine, sine, -sine, sine], axis=1).astype(np.float32)
    return cos_rows, sin_rows


def swap_halves(values):
    lane = lax.broadcasted_iota(jnp.int32, values.shape, 1)
    low = lax.rem(lane, HD) < HD // 2
    return jnp.where(
        low, pltpu.roll(values, LANES - HD // 2, 1), pltpu.roll(values, HD // 2, 1)
    )


def head_mask(values, head):
    lane = lax.broadcasted_iota(jnp.int32, (1, LANES), 1)
    keep = (lane < HD) if head == 0 else (lane >= HD)
    return jnp.where(keep, values, jnp.zeros_like(values))


def whole(shape):
    return pl.BlockSpec(shape, lambda *_: (0,) * len(shape))


def chosen(shape):
    return pl.BlockSpec((1,) + shape, lambda j, at: (at[0], 0, 0))


def qkv_kernel(at, x, gain, shift, w, bias, down, up, cos, sin, qkv, low, h1, *, tile, width):
    j = pl.program_id(0)

    @pl.when(j == 0)
    def _():
        normed, _s = norm_rows(x[...].astype(F32))
        rows = (normed * gain[...] + shift[...]).astype(BF16)
        h1[...] = rows
        low[...] = dot(rows, down[0], NT).astype(BF16)

    out = dot(h1[...], w[...]) + bias[...] + dot(low[...], up[0])
    rotated = 2 * width // tile

    @pl.when(j < rotated)
    def _():
        scale = jnp.where(j < rotated // 2, HD**-0.5, 1.0).astype(F32)
        c = cos[...] * scale
        s = sin[...] * scale
        for g in range(tile // LANES):
            part = out[:, g * LANES : (g + 1) * LANES]
            qkv[:, g * LANES : (g + 1) * LANES] = (part * c + swap_halves(part) * s).astype(BF16)

    @pl.when(j >= rotated)
    def _():
        qkv[...] = out.astype(BF16)


def qkv_rows(at, x, gain, shift, w, bias, down, up, cos, sin):
    rows, width = x.shape
    cols = w.shape[1]
    tile = 512
    return pl.pallas_call(
        functools.partial(qkv_kernel, tile=tile, width=width),
        grid_spec=pltpu.PrefetchScalarGridSpec(
            num_scalar_prefetch=1,
            grid=(cols // tile,),
            in_specs=[
                whole((rows, width)),
                whole((1, width)),
                whole((1, width)),
                pl.BlockSpec((width, tile), lambda j, at: (0, j)),
                pl.BlockSpec((1, tile), lambda j, at: (0, j)),
                chosen((RANK, width)),
                pl.BlockSpec((1, RANK, tile), lambda j, at: (at[0], 0, j)),
                whole((rows, LANES)),
                whole((rows, LANES)),
            ],
            out_specs=[
                pl.BlockSpec((rows, tile), lambda j, at: (0, j)),
                whole((rows, RANK)),
            ],
            scratch_shapes=[pltpu.VMEM((rows, width), BF16)],
        ),
        out_shape=[
            jax.ShapeDtypeStruct((rows, cols), BF16),
            jax.ShapeDtypeStruct((rows, RANK), BF16),
        ],
        compiler_params=params(),
        cost_estimate=cost(2 * rows * width * cols, 2 * width * cols + 2 * rows * (width + cols)),
        name="qkv_rows",
    )(at, x, gain, shift, w, bias, down, up, cos, sin)


def attend_kernel(q, k0, v0, k1, v1, out, lse):
    i = pl.program_id(0)
    rows, wide = q.shape
    keys = jnp.concatenate([k0[...], k1[...]], axis=0)
    values_t = jnp.concatenate([v0[...], v1[...]], axis=0).T

    def scores(item):
        pair, head = item
        cut = slice(pair * LANES, (pair + 1) * LANES)
        return dot(keys[:, cut], head_mask(q[:, cut], head), NT)

    items = [(pair, head) for pair in range(wide // LANES) for head in range(2)]
    held = []
    now = scores(items[0])
    for n, (pair, head) in enumerate(items):
        later = scores(items[n + 1]) if n + 1 < len(items) else None
        top = jnp.max(now, axis=0, keepdims=True)
        weights = jnp.exp(now - top)
        total = jnp.sum(weights, axis=0, keepdims=True)
        first = pair * LANES + head * HD
        mixed = dot(values_t[first : first + HD], weights.astype(BF16))
        held.append(mixed * (1.0 / total))
        lse[pl.ds(i * (wide // HD) + n, 1), :] = top + jnp.log(total)
        if head == 1:
            both = jnp.concatenate(held, axis=0).T
            out[:, pair * LANES : (pair + 1) * LANES] = both.astype(BF16)
            held = []
        now = later


def attend(own, peer):
    rows = own.shape[0]
    width = own.shape[1] // 3
    others = peer.shape[0]
    wide = 2 * LANES
    steps = width // wide

    def part(count, which):
        return pl.BlockSpec((count, wide), lambda i: (0, i + which * steps))

    return pl.pallas_call(
        attend_kernel,
        grid=(steps,),
        in_specs=[part(rows, 0), part(rows, 1), part(rows, 2), part(others, 1), part(others, 2)],
        out_specs=[
            pl.BlockSpec((rows, wide), lambda i: (0, i)),
            whole((HEADS, rows)),
        ],
        out_shape=[
            jax.ShapeDtypeStruct((rows, width), BF16),
            jax.ShapeDtypeStruct((HEADS, rows), F32),
        ],
        compiler_params=params(),
        cost_estimate=cost(
            16 * rows * (rows + others) * width, 4 * width * (rows + others), rows * HEADS * others
        ),
        name="attend",
    )(own, own, own, peer, peer)


def gelu_both(f):
    z = jnp.abs(f) * (0.5**0.5)
    t = 1.0 / (1.0 + 0.3 * z)
    poly = ERFC[-1]
    for c in ERFC[-2::-1]:
        poly = poly * t + c
    bell = jnp.exp(f * f * -0.5)
    tail = (0.5 * poly) * t * bell
    phi = jnp.where(f < 0, tail, 1.0 - tail)
    return f * phi, phi + f * (bell * 0.3989422804014327)


def put_pieces(ref, slot, first, tile, code, spread):
    for p in range(tile.shape[1] // LANES):
        ref[(first + p) ^ code, slot] = tile[:, p * LANES : (p + 1) * LANES].astype(BF16)


def block_kernel(
    at,
    x, o, cot, lse, w_out, b_out, out_down, out_up, gain, shift,
    w1, b1, down1, up1, w2, b2, down2, up2,
    y_out, dx1_out, go_out, delta_out, pieces,
    x1, h2, y, dh2, low_o, low1, low1_t, grad2, grad2_t, low2, grad1,
    *, tile,
):
    j = pl.program_id(0)
    last = pl.num_programs(0) - 1
    code = at[1]
    rows, width = x.shape

    @pl.when(j == 0)
    def _():
        low = dot(o[...], out_down[0], NT).astype(BF16)
        low_o[...] = low
        mid = x[...].astype(F32) + (dot(o[...], w_out[...]) + b_out[...] + dot(low, out_up[0]))
        x1[...] = mid
        normed, _s = norm_rows(mid)
        rows2 = (normed * gain[...] + shift[...]).astype(BF16)
        h2[...] = rows2
        low_1 = dot(rows2, down1[0], NT).astype(BF16)
        low1[...] = low_1
        low1_t[...] = low_1.T
        g2 = dot(cot[...], up2[0], NT).astype(BF16)
        grad2[...] = g2
        grad2_t[...] = g2.T
        y[...] = jnp.zeros_like(y)
        dh2[...] = jnp.zeros_like(dh2)
        low2[...] = jnp.zeros_like(low2)
        grad1[...] = jnp.zeros_like(grad1)

    f = dot(h2[...], w1[...]) + b1[...] + dot(low1[...], up1[0])
    back = dot(cot[...], w2[...], NT) + dot(grad2[...], down2[0])
    act, slope = gelu_both(f)
    act = act.astype(BF16)
    df = (back * slope).astype(BF16)
    y[...] += dot(act, w2[...])
    dh2[...] += dot(df, w1[...], NT)
    low2[...] += dot(act, down2[0], NT)
    grad1[...] += dot(df, up1[0], NT)
    first = j * (tile // LANES)
    up1_grad = dot(low1_t[...], df)
    down2_grad = dot(grad2_t[...], act)
    for p in range(tile // LANES):
        cut = slice(p * LANES, (p + 1) * LANES)
        pieces[(first + p) ^ code, 0] = up1_grad[:, cut].astype(BF16)
        pieces[(first + p) ^ code, 1] = down2_grad[:, cut].astype(BF16)

    @pl.when(j == last)
    def _():
        low_2 = low2[...].astype(BF16)
        total = x1[...] + (y[...] + b2[...] + dot(low_2, up2[0]))
        y_out[...] = total.astype(BF16)
        up2_grad = dot(low_2.T, cot[...])
        g1 = grad1[...].astype(BF16)
        back2 = dh2[...] + dot(g1, down1[0])
        down1_grad = dot(g1.T, h2[...])
        normed, spread = norm_rows(x1[...])
        dx1 = cot[...].astype(F32) + norm_back(back2, normed, spread, gain[...])
        dx1_out[...] = dx1
        da = dx1.astype(BF16)
        g_o = dot(da, out_up[0], NT).astype(BF16)
        go = (dot(da, w_out[...], NT) + dot(g_o, out_down[0])).astype(BF16)
        go_out[EXTRA : EXTRA + rows, :] = go
        up_o_grad = dot(low_o[...].T, da)
        down_o_grad = dot(g_o.T, o[...])
        for slot, grad in enumerate((up2_grad, down1_grad, up_o_grad, down_o_grad)):
            for p in range(width // LANES):
                cut = slice(p * LANES, (p + 1) * LANES)
                pieces[(slot * (width // LANES) + p) ^ code, 2] = grad[:, cut].astype(BF16)
        product = go.astype(F32) * o[...].astype(F32)
        high = product.astype(BF16)
        rest = (product - high.astype(F32)).astype(BF16)
        lane = lax.broadcasted_iota(jnp.int32, (HEADS, width), 1)
        head = lax.broadcasted_iota(jnp.int32, (HEADS, width), 0)
        pick = (lane // HD == head).astype(BF16)
        delta = dot(pick, high, NT) + dot(pick, rest, NT)
        delta_out[...] = delta
        if rows < width // 2:
            go_out[0:EXTRA, :] = jnp.zeros((EXTRA, width), BF16)
        for side, stat in enumerate((lse[...], delta)):
            left = stat
            for n in range(3):
                part = left.astype(BF16)
                go_out[16 * n : 16 * n + 16, side * (width // 2) : side * (width // 2) + rows] = part
                left = left - part.astype(F32)


def block_rows(at, x, o, cot, lse, out_set, norm_set, fc1_set, fc2_set, groups):
    rows, width = x.shape
    w_out, b_out, out_down, out_up = out_set
    w1, b1, down1, up1 = fc1_set
    w2, b2, down2, up2 = fc2_set
    ff = w1.shape[1]
    tile = 512
    row_block = whole((rows, width))
    return pl.pallas_call(
        functools.partial(block_kernel, tile=tile),
        grid_spec=pltpu.PrefetchScalarGridSpec(
            num_scalar_prefetch=1,
            grid=(ff // tile,),
            in_specs=[
                row_block,
                row_block,
                row_block,
                whole((HEADS, rows)),
                whole((width, width)),
                whole((1, width)),
                chosen((RANK, width)),
                chosen((RANK, width)),
                whole((1, width)),
                whole((1, width)),
                pl.BlockSpec((width, tile), lambda j, at: (0, j)),
                pl.BlockSpec((1, tile), lambda j, at: (0, j)),
                chosen((RANK, width)),
                pl.BlockSpec((1, RANK, tile), lambda j, at: (at[0], 0, j)),
                pl.BlockSpec((tile, width), lambda j, at: (j, 0)),
                whole((1, width)),
                pl.BlockSpec((1, RANK, tile), lambda j, at: (at[0], 0, j)),
                chosen((RANK, width)),
            ],
            out_specs=[
                row_block,
                row_block,
                whole((EXTRA + rows, width)),
                whole((HEADS, rows)),
                whole((groups, 3, RANK, LANES)),
            ],
            scratch_shapes=[
                pltpu.VMEM((rows, width), F32),
                pltpu.VMEM((rows, width), BF16),
                pltpu.VMEM((rows, width), F32),
                pltpu.VMEM((rows, width), F32),
                pltpu.VMEM((rows, RANK), BF16),
                pltpu.VMEM((rows, RANK), BF16),
                pltpu.VMEM((RANK, rows), BF16),
                pltpu.VMEM((rows, RANK), BF16),
                pltpu.VMEM((RANK, rows), BF16),
                pltpu.VMEM((rows, RANK), F32),
                pltpu.VMEM((rows, RANK), F32),
            ],
        ),
        out_shape=[
            jax.ShapeDtypeStruct((rows, width), BF16),
            jax.ShapeDtypeStruct((rows, width), F32),
            jax.ShapeDtypeStruct((EXTRA + rows, width), BF16),
            jax.ShapeDtypeStruct((HEADS, rows), F32),
            jax.ShapeDtypeStruct((groups, 3, RANK, LANES), BF16),
        ],
        compiler_params=params(),
        cost_estimate=cost(
            8 * rows * width * ff + 4 * rows * width * width, 4 * width * ff, rows * ff
        ),
        name="block_rows",
    )(
        at, x, o, cot, lse, w_out, b_out, out_down, out_up, *norm_set,
        w1, b1, down1, up1, w2, b2, down2, up2,
    )


def attend_back_kernel(
    q0, k0, v0, q1, k1, v1, go, gp, stats, lse0, delta0, cos, sin, out, lse1, delta1
):
    i = pl.program_id(0)
    rows = q0.shape[0]
    peers = gp.shape[0]
    half = stats.shape[2] // 2

    @pl.when(i == 0)
    def _():
        for n in range(peers):
            for side, ref in enumerate((lse1, delta1)):
                cut = slice(side * half, side * half + rows)
                ref[n] = (
                    stats[n, 0:16, cut].astype(F32)
                    + stats[n, 16:32, cut].astype(F32)
                    + stats[n, 32:48, cut].astype(F32)
                )

    keys = jnp.concatenate([k0[...], k1[...]], axis=0)
    values = jnp.concatenate([v0[...], v1[...]], axis=0)
    keys_t = keys.T

    def first(item):
        head, peer = item
        if peer is None:
            q = head_mask(q0[...], head)
            g = head_mask(go[EXTRA : EXTRA + rows, :], head)
            return dot(keys, q, NT), dot(values, g, NT), q, g
        q = head_mask(q1[peer * rows : (peer + 1) * rows, :], head)
        g = head_mask(gp[peer, EXTRA : EXTRA + rows, :], head)
        return dot(k0[...], q, NT), dot(v0[...], g, NT), q, g

    items = [(head, None) for head in range(2)]
    items += [(head, peer) for peer in range(peers) for head in range(2)]
    grad_k = grad_v = None
    grad_q = []
    now = first(items[0])
    for n, (head, peer) in enumerate(items):
        later = first(items[n + 1]) if n + 1 < len(items) else None
        s, dp, q, g = now
        row = pl.ds(2 * i + head, 1)
        lse = lse0[row, :] if peer is None else lse1[peer, row, :]
        delta = delta0[row, :] if peer is None else delta1[peer, row, :]
        prob = jnp.exp(s - lse)
        ds = (prob * (dp - delta)).astype(BF16)
        prob = prob.astype(BF16)
        if peer is None:
            grad_q.append(dot(keys_t[head * HD : (head + 1) * HD], ds))
        more_v = dot(prob[:rows], g)
        more_k = dot(ds[:rows], q)
        grad_v = more_v if grad_v is None else grad_v + more_v
        grad_k = more_k if grad_k is None else grad_k + more_k
        now = later

    def unrotate(values):
        return values * cos[...] - swap_halves(values) * sin[...]

    out[0] = unrotate(jnp.concatenate(grad_q, axis=0).T * (HD**-0.5)).astype(BF16)
    out[1] = unrotate(grad_k).astype(BF16)
    out[2] = grad_v.astype(BF16)


def attend_back(own, peer, go, gp, lse, delta, cos, sin):
    rows = own.shape[0]
    width = own.shape[1] // 3
    others = peer.shape[0]
    peers = gp.shape[0]
    steps = width // LANES

    def part(count, which):
        return pl.BlockSpec((count, LANES), lambda i: (0, i + which * steps))

    return pl.pallas_call(
        attend_back_kernel,
        grid=(steps,),
        in_specs=[
            part(rows, 0), part(rows, 1), part(rows, 2),
            part(others, 0), part(others, 1), part(others, 2),
            part(rows + EXTRA, 0),
            pl.BlockSpec((peers, rows + EXTRA, LANES), lambda i: (0, 0, i)),
            whole((peers, EXTRA, width)),
            whole((HEADS, rows)),
            whole((HEADS, rows)),
            whole((rows, LANES)),
            whole((rows, LANES)),
        ],
        out_specs=pl.BlockSpec((3, rows, LANES), lambda i: (0, 0, i)),
        out_shape=jax.ShapeDtypeStruct((3, rows, width), BF16),
        scratch_shapes=[
            pltpu.VMEM((peers, HEADS, rows), F32),
            pltpu.VMEM((peers, HEADS, rows), F32),
        ],
        compiler_params=params(),
        cost_estimate=cost(
            12 * 2 * rows * (rows + others) * width, 8 * width * (rows + others), rows * others
        ),
        name="attend_back",
    )(own, own, own, peer, peer, peer, go, gp, gp, lse, delta, cos, sin)


def qkv_grad_kernel(at, g, low, x, gain, shift, up, pieces, rank_grad):
    code = at[1]
    width = x.shape[1]
    low_t = low[...].T
    total = None
    for n in range(3):
        grad = dot(low_t, g[n])
        for p in range(width // LANES):
            piece = n * (width // LANES) + p
            pieces[piece ^ code, 0] = grad[:, p * LANES : (p + 1) * LANES].astype(BF16)
        more = dot(g[n], up[0, :, n * width : (n + 1) * width], NT)
        total = more if total is None else total + more
    rank = total.astype(BF16)
    rank_grad[...] = rank
    normed, _s = norm_rows(x[...].astype(F32))
    h1 = (normed * gain[...] + shift[...]).astype(BF16)
    grad = dot(rank.T, h1)
    for p in range(width // LANES):
        piece = 3 * (width // LANES) + p
        pieces[piece ^ code, 0] = grad[:, p * LANES : (p + 1) * LANES].astype(BF16)


def qkv_grad(at, g, low, x, gain, shift, up, groups):
    rows, width = x.shape
    return pl.pallas_call(
        qkv_grad_kernel,
        grid_spec=pltpu.PrefetchScalarGridSpec(
            num_scalar_prefetch=1,
            grid=(1,),
            in_specs=[
                whole((3, rows, width)),
                whole((rows, RANK)),
                whole((rows, width)),
                whole((1, width)),
                whole((1, width)),
                chosen((RANK, 3 * width)),
            ],
            out_specs=[whole((groups, 1, RANK, LANES)), whole((rows, RANK))],
        ),
        out_shape=[
            jax.ShapeDtypeStruct((groups, 1, RANK, LANES), BF16),
            jax.ShapeDtypeStruct((rows, RANK), BF16),
        ],
        compiler_params=params(),
        cost_estimate=cost(2 * rows * 16 * 3 * width * 4, 8 * rows * width),
        name="qkv_grad",
    )(at, g, low, x, gain, shift, up)


def input_grad_kernel(at, g, w, rank_grad, down, x, gain, dx1, out, total):
    j = pl.program_id(0)

    @pl.when(j == 0)
    def _():
        total[...] = dot(rank_grad[...], down[0])

    total[...] += dot(g[0], w[...], NT)

    @pl.when(j == pl.num_programs(0) - 1)
    def _():
        normed, spread = norm_rows(x[...].astype(F32))
        out[...] = dx1[...] + norm_back(total[...], normed, spread, gain[...])


def input_grad(at, g, w, rank_grad, down, x, gain, dx1):
    rows, width = x.shape
    tile = 512
    per = width // tile
    return pl.pallas_call(
        input_grad_kernel,
        grid_spec=pltpu.PrefetchScalarGridSpec(
            num_scalar_prefetch=1,
            grid=(3 * per,),
            in_specs=[
                pl.BlockSpec((1, rows, tile), lambda j, at: (j // per, 0, j % per)),
                pl.BlockSpec((width, tile), lambda j, at: (0, j)),
                whole((rows, RANK)),
                chosen((RANK, width)),
                whole((rows, width)),
                whole((1, width)),
                whole((rows, width)),
            ],
            out_specs=whole((rows, width)),
            scratch_shapes=[pltpu.VMEM((rows, width), F32)],
        ),
        out_shape=jax.ShapeDtypeStruct((rows, width), F32),
        compiler_params=params(),
        cost_estimate=cost(6 * rows * width * width, 6 * width * width + 16 * rows * width),
        name="input_grad",
    )(at, g, w, rank_grad, down, x, gain, dx1)


def flip(values, axis, bit):
    size = lax.axis_size(axis)
    return lax.ppermute(values, axis, [(n, n ^ bit) for n in range(size)])


def swap_order(groups):
    bits = [("dp", 1)]
    n = 1
    while n < lax.axis_size("seq"):
        bits.append(("seq", n))
        n *= 2
    n = 2
    while n < lax.axis_size("dp"):
        bits.append(("dp", n))
        n *= 2
    count = groups.bit_length() - 1
    return bits[:count], bits[count:]


def place_code(groups):
    halves, _rest = swap_order(groups)
    code = jnp.int32(0)
    for n, (axis, bit) in enumerate(halves):
        on = (lax.axis_index(axis) & bit) != 0
        code = code + jnp.where(on, groups >> (n + 1), 0).astype(jnp.int32)
    return code


def sum_pieces(pieces, index_all, groups):
    halves, rest = swap_order(groups)
    held = pieces[None]
    slots = [0]
    for axis, bit in halves:
        half = held.shape[1] // 2
        arrived = flip(held[:, half:], axis, bit)
        kept = held[:, :half]
        if axis == "seq":
            held = (kept.astype(F32) + arrived.astype(F32)).astype(BF16)
        else:
            held = jnp.concatenate([kept, arrived], axis=0)
            slots = slots + [slot ^ bit for slot in slots]
    place = lax.axis_index("dp")
    owners = jnp.stack([index_all[place ^ slot] for slot in slots])
    onehot = (jnp.arange(NADAPT, dtype=jnp.int32)[:, None] == owners[None, :]).astype(F32)
    total = jnp.sum(
        onehot[:, :, None, None, None, None] * held.astype(F32)[None], axis=1
    )
    total = jnp.transpose(total, (1, 2, 0, 3, 4)).astype(BF16)
    for axis, bit in rest:
        total = (total.astype(F32) + flip(total, axis, bit).astype(F32)).astype(BF16)
    for axis, bit in halves[::-1]:
        total = jnp.concatenate([total, flip(total, axis, bit)], axis=0)
    return total


def spread_kernel(at, pieces, *outs, plan):
    code = at[1]
    for ref, part, first, count in zip(outs, *plan):
        for p in range(count):
            ref[:, :, p * LANES : (p + 1) * LANES] = pieces[(first + p) ^ code, part].astype(F32)


def spread(at, pieces, plan):
    parts, firsts, counts = plan
    shapes = [(NADAPT, RANK, count * LANES) for count in counts]
    return pl.pallas_call(
        functools.partial(spread_kernel, plan=plan),
        grid_spec=pltpu.PrefetchScalarGridSpec(
            num_scalar_prefetch=1,
            grid=(1,),
            in_specs=[whole(pieces.shape)],
            out_specs=[whole(shape) for shape in shapes],
        ),
        out_shape=[jax.ShapeDtypeStruct(shape, F32) for shape in shapes],
        compiler_params=params(),
        cost_estimate=cost(1, 6 * pieces.size),
        name="spread",
    )(at, pieces)


def body(
    clip_tokens, adapter_index, ln1_gain, ln1_bias, qkv_weight, qkv_bias, qkv_down, qkv_up,
    out_weight, out_bias, out_down, out_up, ln2_gain, ln2_bias, fc1_weight, fc1_bias, fc1_down,
    fc1_up, fc2_weight, fc2_bias, fc2_down, fc2_up, cotangent,
):
    _one, rows, width = clip_tokens.shape
    devices = lax.axis_size("seq")
    here = lax.axis_index("seq")
    groups = 32
    row = lambda v: v.reshape(1, -1)
    x = clip_tokens[0]
    cot = cotangent[0]
    at = jnp.stack([adapter_index[0], place_code(groups)])
    index_all = lax.all_gather(adapter_index, "dp", axis=0, tiled=True)

    def from_peer(values, shift):
        return lax.ppermute(
            values, "seq", [((n + shift) % devices, n) for n in range(devices)]
        )

    cos_all, sin_all = (jnp.asarray(t) for t in rotary_tables(rows * devices))

    def tables(place):
        return tuple(
            lax.dynamic_slice_in_dim(t, place * rows, rows, 0) for t in (cos_all, sin_all)
        )

    cos, sin = tables(here)
    peers = range(1, devices)
    x_peer = jnp.concatenate([from_peer(x, n) for n in peers], axis=0)
    peer_tables = [tables((here + n) % devices) for n in peers]
    cos_peer = jnp.concatenate([t[0] for t in peer_tables], axis=0)
    sin_peer = jnp.concatenate([t[1] for t in peer_tables], axis=0)
    first_set = (row(ln1_gain), row(ln1_bias), qkv_weight, row(qkv_bias), qkv_down, qkv_up)
    own, low_qkv = qkv_rows(at, x, *first_set, cos, sin)
    peer, _low = qkv_rows(at, x_peer, *first_set, cos_peer, sin_peer)
    mixed, lse = attend(own, peer)
    block_output, dx1, go, delta, pieces_a = block_rows(
        at, x, mixed, cot, lse,
        (out_weight, row(out_bias), out_down, out_up),
        (row(ln2_gain), row(ln2_bias)),
        (fc1_weight, row(fc1_bias), fc1_down, fc1_up),
        (fc2_weight, row(fc2_bias), fc2_down, fc2_up),
        groups,
    )
    go_peer = jnp.stack([from_peer(go, n) for n in peers])
    grad_qkv = attend_back(own, peer, go, go_peer, lse, delta, cos, sin)
    pieces_b, rank_grad = qkv_grad(
        at, grad_qkv, low_qkv, x, row(ln1_gain), row(ln1_bias), qkv_up, groups
    )
    grad_in = input_grad(at, grad_qkv, qkv_weight, rank_grad, qkv_down, x, row(ln1_gain), dx1)
    sums_a = sum_pieces(pieces_a, index_all, groups)
    sums_b = sum_pieces(pieces_b, index_all, groups)
    per = width // LANES
    up1, down2, up2, down1, up_o, down_o = spread(
        at, sums_a, ((0, 1, 2, 2, 2, 2), (0, 0, 0, per, 2 * per, 3 * per), (32, 32, per, per, per, per))
    )
    up_qkv, down_qkv = spread(at, sums_b, ((0, 0), (0, 3 * per), (3 * per, per)))
    return (
        block_output[None], grad_in[None], down_qkv, up_qkv, down_o, up_o, down1, up1, down2, up2,
    )


def solution(mesh):
    split = P("dp", "seq", None)
    return jax.shard_map(
        body,
        mesh=mesh,
        in_specs=(split, P("dp")) + (P(),) * 20 + (split,),
        out_specs=(split, split) + (P(),) * 8,
        check_vma=False,
    )
```

```python
import functools

import jax
import jax.numpy as jnp
import numpy as np
from jax import lax
from jax.experimental import pallas as pl
from jax.experimental.pallas import tpu as pltpu
from jax.sharding import PartitionSpec as P

HEADS = 16
HD = 64
GRID = 16
NADAPT = 8
RANK = 16
EPSILON = 1e-06
LANES = 128
EXTRA = 48

F32 = jnp.float32
BF16 = jnp.bfloat16
NN = (((1,), (0,)), ((), ()))
NT = (((1,), (1,)), ((), ()))

ERFC = (
    0.16918800211151383,
    0.1707152747822528,
    0.14833885959986734,
    0.21492717178376733,
    -0.09465313901935662,
    0.5477232747113128,
    -0.5122807406271995,
    0.48556441585520754,
    -0.1295231387829952,
)


def dot(a, b, dims=NN):
    return lax.dot_general(a, b, dims, preferred_element_type=F32)


def params(steps=1):
    return pltpu.CompilerParams(
        dimension_semantics=("arbitrary",) * steps, vmem_limit_bytes=60 << 20
    )


def cost(flops, moved, exps=0):
    return pl.CostEstimate(flops=int(flops), bytes_accessed=int(moved), transcendentals=int(exps))


def norm_rows(values):
    centre = values - jnp.mean(values, axis=-1, keepdims=True)
    spread = lax.rsqrt(jnp.mean(centre * centre, axis=-1, keepdims=True) + EPSILON)
    return centre * spread, spread


def norm_back(grad_rows, normed, spread, gain):
    scaled = grad_rows * gain
    first = jnp.mean(scaled, axis=-1, keepdims=True)
    second = jnp.mean(scaled * normed, axis=-1, keepdims=True)
    return spread * (scaled - first - normed * second)


def rotary_tables(length):
    half = HD // 2
    side = half // 3
    lead = half - 2 * side
    token = np.arange(length)
    pair = np.arange(half)
    kind = np.where(pair < lead, 0, np.where(pair < lead + side, 1, 2))
    local = np.where(kind == 0, pair, np.where(kind == 1, pair - lead, pair - lead - side))
    total = np.where(kind == 0, lead, side)
    frequency = np.power(
        np.float32(10000.0), -local.astype(np.float32) / total.astype(np.float32)
    ).astype(np.float32)
    place = np.where(
        kind[None] == 0,
        (token // (GRID * GRID))[:, None],
        np.where(kind[None] == 1, (token // GRID % GRID)[:, None], (token % GRID)[:, None]),
    ).astype(np.float32)
    angle = place * frequency[None]
    cosine, sine = np.cos(angle), np.sin(angle)
    cos_rows = np.concatenate([cosine] * 4, axis=1).astype(np.float32)
    sin_rows = np.concatenate([-sine, sine, -sine, sine], axis=1).astype(np.float32)
    return cos_rows, sin_rows


def swap_halves(values):
    lane = lax.broadcasted_iota(jnp.int32, (1, LANES), 1)
    low = (lane & (HD // 2)) == 0
    return jnp.where(
        low, pltpu.roll(values, LANES - HD // 2, 1), pltpu.roll(values, HD // 2, 1)
    )


def head_mask(values, head):
    lane = lax.broadcasted_iota(jnp.int32, (1, LANES), 1)
    keep = (lane < HD) if head == 0 else (lane >= HD)
    return jnp.where(keep, values, jnp.zeros_like(values))


def whole(shape):
    return pl.BlockSpec(shape, lambda *_: (0,) * len(shape))


def chosen(shape):
    return pl.BlockSpec((1,) + shape, lambda *ids: (ids[-1][0], 0, 0))


def position(piece, at):
    top = (piece >> 4) ^ at[1]
    return 16 * top + ((piece & 15) ^ jnp.where(top == 0, at[2], at[3]))


def qkv_kernel(at, x, gain, shift, w, bias, down, up, cos, sin, qkv, low, h1, *, tile, width):
    j = pl.program_id(0)
    p = pl.program_id(1)

    @pl.when(j == 0)
    def _():
        normed, _s = norm_rows(x[...].astype(F32))
        rows = (normed * gain[...] + shift[...]).astype(BF16)
        h1[p] = rows
        low[p] = dot(rows, down[0], NT).astype(BF16)

    out = dot(h1[p], w[...]) + bias[...] + dot(low[p], up[0])
    rotated = 2 * width // tile

    @pl.when(j < rotated)
    def _():
        scale = jnp.where(j < rotated // 2, HD**-0.5, 1.0).astype(F32)
        c = cos[...] * scale
        s = sin[...] * scale
        for g in range(tile // LANES):
            part = out[:, g * LANES : (g + 1) * LANES]
            qkv[:, g * LANES : (g + 1) * LANES] = (part * c + swap_halves(part) * s).astype(BF16)

    @pl.when(j >= rotated)
    def _():
        qkv[...] = out.astype(BF16)


def qkv_rows(at, x, gain, shift, w, bias, down, up, cos, sin, rows):
    blocks = x.shape[0] // rows
    width = x.shape[1]
    cols = w.shape[1]
    tile = 1024
    table = pl.BlockSpec((rows, LANES), lambda j, p, at: (at[1 + p], 0))
    return pl.pallas_call(
        functools.partial(qkv_kernel, tile=tile, width=width),
        grid_spec=pltpu.PrefetchScalarGridSpec(
            num_scalar_prefetch=1,
            grid=(cols // tile, blocks),
            in_specs=[
                pl.BlockSpec((rows, width), lambda j, p, at: (jnp.where(j == 0, p, blocks - 1), 0)),
                whole((1, width)),
                whole((1, width)),
                pl.BlockSpec((width, tile), lambda j, p, at: (0, j)),
                pl.BlockSpec((1, tile), lambda j, p, at: (0, j)),
                chosen((RANK, width)),
                pl.BlockSpec((1, RANK, tile), lambda j, p, at: (at[0], 0, j)),
                table,
                table,
            ],
            out_specs=[
                pl.BlockSpec((rows, tile), lambda j, p, at: (p, j)),
                whole((blocks, rows, RANK)),
            ],
            scratch_shapes=[pltpu.VMEM((blocks, rows, width), BF16)],
        ),
        out_shape=[
            jax.ShapeDtypeStruct((blocks * rows, cols), BF16),
            jax.ShapeDtypeStruct((blocks, rows, RANK), BF16),
        ],
        compiler_params=params(2),
        cost_estimate=cost(
            2 * blocks * rows * width * cols, 2 * width * cols + 2 * blocks * rows * (width + cols)
        ),
        name="qkv_rows",
    )(at, x, gain, shift, w, bias, down, up, cos, sin)


def attend_kernel(*refs, ahead):
    if ahead:
        q, k, v, mixed_out, top_out, total_out = refs
    else:
        q, k, v, mixed_in, top_in, total_in, out, lse = refs
    wide = q.shape[1]
    keys = k[...]
    values_t = [v[:, n * LANES : (n + 1) * LANES].T for n in range(wide // LANES)]

    def scores(item):
        pair, head = item
        cut = slice(pair * LANES, (pair + 1) * LANES)
        return dot(keys[:, cut], head_mask(q[:, cut], head), NT)

    items = [(pair, head) for pair in range(wide // LANES) for head in range(2)]
    held = []
    now = scores(items[0])
    for n, (pair, head) in enumerate(items):
        later = scores(items[n + 1]) if n + 1 < len(items) else None
        row = slice(n, n + 1)
        cut = slice(pair * LANES + head * HD, pair * LANES + (head + 1) * HD)
        top = jnp.max(now, axis=0, keepdims=True)
        if not ahead:
            before = top_in[row, :]
            top = jnp.maximum(top, before)
            scale = jnp.exp(before - top)
        weights = jnp.exp(now - top)
        total = jnp.sum(weights, axis=0, keepdims=True)
        mixed = dot(values_t[pair][head * HD : (head + 1) * HD], weights.astype(BF16))
        if ahead:
            mixed_out[cut, :] = mixed
            top_out[row, :] = top
            total_out[row, :] = total
        else:
            total = total + scale * total_in[row, :]
            mixed = mixed + scale * mixed_in[cut, :]
            held.append(mixed * (1.0 / total))
            lse[row, :] = top + jnp.log(total)
            if head == 1:
                both = jnp.concatenate(held, axis=0).T
                out[:, pair * LANES : (pair + 1) * LANES] = both.astype(BF16)
                held = []
        now = later


def attend(own, keyed, state=None):
    rows = own.shape[0]
    width = own.shape[1] // 3
    count = keyed.shape[0]
    wide = 4 * LANES
    steps = width // wide

    def part(length, which):
        return pl.BlockSpec((length, wide), lambda i: (0, i + which * steps))

    turned = pl.BlockSpec((wide, rows), lambda i: (i, 0))
    stat = pl.BlockSpec((wide // HD, rows), lambda i: (i, 0))
    stat_shape = jax.ShapeDtypeStruct((HEADS, rows), F32)
    if state is None:
        more_specs, more = [], ()
        out_specs = [turned, stat, stat]
        out_shape = [jax.ShapeDtypeStruct((width, rows), F32), stat_shape, stat_shape]
    else:
        more_specs, more = [turned, stat, stat], state
        out_specs = [pl.BlockSpec((rows, wide), lambda i: (0, i)), stat]
        out_shape = [jax.ShapeDtypeStruct((rows, width), BF16), stat_shape]
    return pl.pallas_call(
        functools.partial(attend_kernel, ahead=state is None),
        grid=(steps,),
        in_specs=[part(rows, 0), part(count, 1), part(count, 2)] + more_specs,
        out_specs=out_specs,
        out_shape=out_shape,
        compiler_params=params(),
        cost_estimate=cost(16 * rows * count * width, 8 * width * (rows + count), rows * HEADS * count),
        name="attend",
    )(own, keyed, keyed, *more)


def gelu_both(f):
    z = jnp.abs(f) * (0.5**0.5)
    t = 1.0 / (1.0 + 0.3 * z)
    poly = ERFC[-1]
    for c in ERFC[-2::-1]:
        poly = poly * t + c
    bell = jnp.exp(f * f * -0.5)
    tail = (0.5 * poly) * t * bell
    phi = jnp.where(f < 0, tail, 1.0 - tail)
    return f * phi, phi + f * (bell * 0.3989422804014327)


def back_kernel(at, cot, w2, down2, up2, back, grad2):
    j = pl.program_id(0)

    @pl.when(j == 0)
    def _():
        grad2[...] = dot(cot[...], up2[0], NT).astype(BF16)

    back[...] = dot(cot[...], w2[...], NT) + dot(grad2[...], down2[0])


def back_rows(at, cot, w2, down2, up2):
    rows, width = cot.shape
    ff = w2.shape[0]
    tile = 1024
    return pl.pallas_call(
        back_kernel,
        grid_spec=pltpu.PrefetchScalarGridSpec(
            num_scalar_prefetch=1,
            grid=(ff // tile,),
            in_specs=[
                whole((rows, width)),
                pl.BlockSpec((tile, width), lambda j, at: (j, 0)),
                pl.BlockSpec((1, RANK, tile), lambda j, at: (at[0], 0, j)),
                chosen((RANK, width)),
            ],
            out_specs=[pl.BlockSpec((rows, tile), lambda j, at: (0, j)), whole((rows, RANK))],
        ),
        out_shape=[
            jax.ShapeDtypeStruct((rows, ff), F32),
            jax.ShapeDtypeStruct((rows, RANK), BF16),
        ],
        compiler_params=params(),
        cost_estimate=cost(2 * rows * width * ff, 2 * width * ff + 4 * rows * ff),
        name="back_rows",
    )(at, cot, w2, down2, up2)


def block_kernel(
    at,
    x, o, cot, lse, back, grad2, w_out, b_out, out_down, out_up, gain, shift,
    w1, b1, down1, up1, down2,
    act_out, x1, low2_out, dx1_out, go_out, delta_out, pieces,
    h2, dh2, low_o, low1, low1_t, grad2_t, low2, grad1,
):
    j = pl.program_id(0)
    last = pl.num_programs(0) - 1
    rows, width = x.shape
    tile = w1.shape[1]

    def put(first, slot, grad):
        for p in range(grad.shape[1] // LANES):
            cut = slice(p * LANES, (p + 1) * LANES)
            pieces[position(first + p, at), slot] = grad[:, cut].astype(BF16)

    @pl.when(j == 0)
    def _():
        low = dot(o[...], out_down[0], NT).astype(BF16)
        low_o[...] = low
        mid = x[...].astype(F32) + (dot(o[...], w_out[...]) + b_out[...] + dot(low, out_up[0]))
        x1[...] = mid
        normed, _s = norm_rows(mid)
        rows2 = (normed * gain[...] + shift[...]).astype(BF16)
        h2[...] = rows2
        low_1 = dot(rows2, down1[0], NT).astype(BF16)
        low1[...] = low_1
        low1_t[...] = low_1.T
        grad2_t[...] = grad2[...].T
        dh2[...] = jnp.zeros_like(dh2)
        low2[...] = jnp.zeros_like(low2)
        grad1[...] = jnp.zeros_like(grad1)

    f = dot(h2[...], w1[...]) + b1[...] + dot(low1[...], up1[0])
    act, slope = gelu_both(f)
    act = act.astype(BF16)
    df = (back[...] * slope).astype(BF16)
    act_out[...] = act
    dh2[...] += dot(df, w1[...], NT)
    low2[...] += dot(act, down2[0], NT)
    grad1[...] += dot(df, up1[0], NT)
    put(j * (tile // LANES), 0, dot(low1_t[...], df))
    put(j * (tile // LANES), 1, dot(grad2_t[...], act))

    @pl.when(j == last)
    def _():
        low_2 = low2[...].astype(BF16)
        low2_out[...] = low_2
        g1 = grad1[...].astype(BF16)
        back2 = dh2[...] + dot(g1, down1[0])
        normed, spread = norm_rows(x1[...])
        dx1 = cot[...].astype(F32) + norm_back(back2, normed, spread, gain[...])
        dx1_out[...] = dx1
        da = dx1.astype(BF16)
        g_o = dot(da, out_up[0], NT).astype(BF16)
        go = (dot(da, w_out[...], NT) + dot(g_o, out_down[0])).astype(BF16)
        go_out[EXTRA : EXTRA + rows, :] = go
        per = width // LANES
        put(0, 2, dot(low_2.T, cot[...]))
        put(per, 2, dot(g1.T, h2[...]))
        put(2 * per, 2, dot(low_o[...].T, da))
        put(3 * per, 2, dot(g_o.T, o[...]))
        product = go.astype(F32) * o[...].astype(F32)
        high = product.astype(BF16)
        rest = (product - high.astype(F32)).astype(BF16)
        lane = lax.broadcasted_iota(jnp.int32, (HEADS, width), 1)
        head = lax.broadcasted_iota(jnp.int32, (HEADS, width), 0)
        pick = (lane // HD == head).astype(BF16)
        delta = dot(pick, high, NT) + dot(pick, rest, NT)
        delta_out[...] = delta
        if rows < width // 2:
            go_out[0:EXTRA, :] = jnp.zeros((EXTRA, width), BF16)
        for side, stat in enumerate((lse[...], delta)):
            left = stat
            for n in range(3):
                part = left.astype(BF16)
                go_out[16 * n : 16 * n + 16, side * (width // 2) : side * (width // 2) + rows] = part
                left = left - part.astype(F32)


def block_rows(at, x, o, cot, lse, back, grad2, out_set, norm_set, fc1_set, down2, groups):
    rows, width = x.shape
    w1 = fc1_set[0]
    ff = w1.shape[1]
    tile = 512
    row_block = whole((rows, width))
    return pl.pallas_call(
        block_kernel,
        grid_spec=pltpu.PrefetchScalarGridSpec(
            num_scalar_prefetch=1,
            grid=(ff // tile,),
            in_specs=[
                row_block,
                row_block,
                row_block,
                whole((HEADS, rows)),
                pl.BlockSpec((rows, tile), lambda j, at: (0, j)),
                whole((rows, RANK)),
                whole((width, width)),
                whole((1, width)),
                chosen((RANK, width)),
                chosen((RANK, width)),
                whole((1, width)),
                whole((1, width)),
                pl.BlockSpec((width, tile), lambda j, at: (0, j)),
                pl.BlockSpec((1, tile), lambda j, at: (0, j)),
                chosen((RANK, width)),
                pl.BlockSpec((1, RANK, tile), lambda j, at: (at[0], 0, j)),
                pl.BlockSpec((1, RANK, tile), lambda j, at: (at[0], 0, j)),
            ],
            out_specs=[
                pl.BlockSpec((rows, tile), lambda j, at: (0, j)),
                row_block,
                whole((rows, RANK)),
                row_block,
                whole((EXTRA + rows, width)),
                whole((HEADS, rows)),
                whole((groups, 3, RANK, LANES)),
            ],
            scratch_shapes=[
                pltpu.VMEM((rows, width), BF16),
                pltpu.VMEM((rows, width), F32),
                pltpu.VMEM((rows, RANK), BF16),
                pltpu.VMEM((rows, RANK), BF16),
                pltpu.VMEM((RANK, rows), BF16),
                pltpu.VMEM((RANK, rows), BF16),
                pltpu.VMEM((rows, RANK), F32),
                pltpu.VMEM((rows, RANK), F32),
            ],
        ),
        out_shape=[
            jax.ShapeDtypeStruct((rows, ff), BF16),
            jax.ShapeDtypeStruct((rows, width), F32),
            jax.ShapeDtypeStruct((rows, RANK), BF16),
            jax.ShapeDtypeStruct((rows, width), F32),
            jax.ShapeDtypeStruct((EXTRA + rows, width), BF16),
            jax.ShapeDtypeStruct((HEADS, rows), F32),
            jax.ShapeDtypeStruct((groups, 3, RANK, LANES), BF16),
        ],
        compiler_params=params(),
        cost_estimate=cost(
            4 * rows * width * ff + 4 * rows * width * width, 4 * width * ff, rows * ff
        ),
        name="block_rows",
    )(at, x, o, cot, lse, back, grad2, *out_set, *norm_set, *fc1_set, down2)


def output_kernel(at, act, w2, x1, b2, low2, up2, out, y):
    j = pl.program_id(0)

    @pl.when(j == 0)
    def _():
        y[...] = x1[...] + (b2[...] + dot(low2[...], up2[0]))

    y[...] += dot(act[...], w2[...])

    @pl.when(j == pl.num_programs(0) - 1)
    def _():
        out[...] = y[...].astype(BF16)


def output_rows(at, act, w2, x1, b2, low2, up2):
    rows, ff = act.shape
    width = x1.shape[1]
    tile = 1024
    return pl.pallas_call(
        output_kernel,
        grid_spec=pltpu.PrefetchScalarGridSpec(
            num_scalar_prefetch=1,
            grid=(ff // tile,),
            in_specs=[
                pl.BlockSpec((rows, tile), lambda j, at: (0, j)),
                pl.BlockSpec((tile, width), lambda j, at: (j, 0)),
                whole((rows, width)),
                whole((1, width)),
                whole((rows, RANK)),
                chosen((RANK, width)),
            ],
            out_specs=whole((rows, width)),
            scratch_shapes=[pltpu.VMEM((rows, width), F32)],
        ),
        out_shape=jax.ShapeDtypeStruct((rows, width), BF16),
        compiler_params=params(),
        cost_estimate=cost(2 * rows * width * ff, 2 * width * ff + 2 * rows * ff),
        name="output_rows",
    )(at, act, w2, x1, b2, low2, up2)


def unrotate(values, cos, sin):
    return values * cos[...] - swap_halves(values) * sin[...]


def score_grads(s, dp, lse, delta):
    prob = jnp.exp(s - lse)
    return prob.astype(BF16), (prob * (dp - delta)).astype(BF16)


def own_back_kernel(at, q0, k0, v0, k1, v1, go, lse0, delta0, cos, sin, *refs, first_pair):
    dq, dk, dv = refs[-3:]
    i = pl.program_id(0) + first_pair
    rows = q0.shape[0]
    keys = jnp.concatenate([k0[...], k1[...]], axis=0)
    values = jnp.concatenate([v0[...], v1[...]], axis=0)
    keys_t = keys.T

    def first(head):
        q = head_mask(q0[...], head)
        g = head_mask(go[EXTRA : EXTRA + rows, :], head)
        return dot(keys, q, NT), dot(values, g, NT), q, g

    grad_q = []
    now = first(0)
    for head in range(2):
        later = first(1) if head == 0 else None
        s, dp, q, g = now
        row = pl.ds(2 * i + head, 1)
        prob, ds = score_grads(s, dp, lse0[row, :], delta0[row, :])
        grad_q.append(dot(keys_t[head * HD : (head + 1) * HD], ds))
        more_v = dot(prob[:rows], g)
        more_k = dot(ds[:rows], q)
        if head == 0:
            dv[...] = more_v
            dk[...] = more_k
        else:
            dv[...] += more_v
            dk[...] += more_k
        now = later
    dq[...] = unrotate(jnp.concatenate(grad_q, axis=0).T * (HD**-0.5), cos, sin).astype(BF16)


def peer_back_kernel(
    at, q1, k0, v0, gp, stats, cos, sin, dk_in, dv_in, *refs, first_pair
):
    dk, dv, lse1, delta1 = refs[-4:]
    i = pl.program_id(0) + first_pair
    rows = k0.shape[0]
    peers = gp.shape[0]
    half = stats.shape[2] // 2

    @pl.when(i == first_pair)
    def _():
        for n in range(peers):
            for side, ref in enumerate((lse1, delta1)):
                cut = slice(side * half, side * half + rows)
                ref[n] = (
                    stats[n, 0:16, cut].astype(F32)
                    + stats[n, 16:32, cut].astype(F32)
                    + stats[n, 32:48, cut].astype(F32)
                )

    def first(item):
        head, peer = item
        q = head_mask(q1[peer * rows : (peer + 1) * rows, :], head)
        g = head_mask(gp[peer, EXTRA : EXTRA + rows, :], head)
        return dot(k0[...], q, NT), dot(v0[...], g, NT), q, g

    items = [(head, peer) for peer in range(peers) for head in range(2)]
    grad_k, grad_v = dk_in[...], dv_in[...]
    now = first(items[0])
    for n, (head, peer) in enumerate(items):
        later = first(items[n + 1]) if n + 1 < len(items) else None
        s, dp, q, g = now
        row = pl.ds(2 * i + head, 1)
        prob, ds = score_grads(s, dp, lse1[peer, row, :], delta1[peer, row, :])
        grad_v = grad_v + dot(prob, g)
        grad_k = grad_k + dot(ds, q)
        now = later
    dk[...] = unrotate(grad_k, cos, sin).astype(BF16)
    dv[...] = grad_v.astype(BF16)


def attend_back(kernel, at, args, specs, outs, before, pairs, scratch, flops, name):
    first, count = pairs
    before = () if before is None else tuple(before)
    steps = HEADS // 2
    return pl.pallas_call(
        functools.partial(kernel, first_pair=first),
        grid_spec=pltpu.PrefetchScalarGridSpec(
            num_scalar_prefetch=1,
            grid=(count,),
            in_specs=specs + [pl.BlockSpec(memory_space=pl.ANY)] * len(before),
            out_specs=[
                pl.BlockSpec((o.shape[0], LANES), lambda i, at: (0, i + first)) for o in outs
            ],
            scratch_shapes=scratch,
        ),
        out_shape=outs,
        input_output_aliases={1 + len(args) + n: n for n in range(len(before))},
        compiler_params=params(),
        cost_estimate=cost(
            flops * count // steps,
            4 * sum(a.size for a in args[:4]) * count // steps,
            flops * count // steps // 512,
        ),
        name=name,
    )(at, *args, *before)


def head_part(count, which, steps, first):
    return pl.BlockSpec((count, LANES), lambda i, at: (0, i + first + which * steps))


def table_part(rows):
    return pl.BlockSpec((rows, LANES), lambda i, at: (at[1], 0))


def own_back(at, own, peer, go, lse, delta, cos, sin, pairs, before):
    rows, others = own.shape[0], peer.shape[0]
    width = own.shape[1] // 3
    part = functools.partial(head_part, steps=width // LANES, first=pairs[0])
    stat = whole((HEADS, rows))
    return attend_back(
        own_back_kernel,
        at,
        (own, own, own, peer, peer, go, lse, delta, cos, sin),
        [part(rows, 0), part(rows, 1), part(rows, 2), part(others, 1), part(others, 2)]
        + [part(rows + EXTRA, 0), stat, stat, table_part(rows), table_part(rows)],
        [jax.ShapeDtypeStruct((rows, width), t) for t in (BF16, F32, F32)],
        before,
        pairs,
        [],
        2 * rows * width * 4 * (3 * (rows + others) + 2 * rows),
        "own_back",
    )


def peer_back(at, own, peer, gp, cos, sin, dk, dv, pairs, before):
    rows, others = own.shape[0], peer.shape[0]
    width = own.shape[1] // 3
    peers = gp.shape[0]
    first = pairs[0]
    part = functools.partial(head_part, steps=width // LANES, first=first)
    return attend_back(
        peer_back_kernel,
        at,
        (peer, own, own, gp, gp, cos, sin, dk, dv),
        [
            part(others, 0), part(rows, 1), part(rows, 2),
            pl.BlockSpec((peers, rows + EXTRA, LANES), lambda i, at: (0, 0, i + first)),
            whole((peers, EXTRA, width)),
            table_part(rows), table_part(rows), part(rows, 0), part(rows, 0),
        ],
        [jax.ShapeDtypeStruct((rows, width), BF16)] * 2,
        before,
        pairs,
        [pltpu.VMEM((peers, HEADS, rows), F32), pltpu.VMEM((peers, HEADS, rows), F32)],
        2 * rows * width * 4 * 4 * others,
        "peer_back",
    )


def qkv_grad_kernel(at, gq, gk, gv, low, x, gain, shift, up, pieces, rank_grad):
    width = x.shape[1]
    low_t = low[...].T
    total = None
    def put(first, grad):
        for p in range(width // LANES):
            cut = slice(p * LANES, (p + 1) * LANES)
            pieces[position(jnp.int32(first + p), at), 0] = grad[:, cut].astype(BF16)

    for n, g in enumerate((gq, gk, gv)):
        put(n * (width // LANES), dot(low_t, g[...]))
        more = dot(g[...], up[0, :, n * width : (n + 1) * width], NT)
        total = more if total is None else total + more
    rank = total.astype(BF16)
    rank_grad[...] = rank
    normed, _s = norm_rows(x[...].astype(F32))
    h1 = (normed * gain[...] + shift[...]).astype(BF16)
    put(3 * (width // LANES), dot(rank.T, h1))


def qkv_grad(at, g, low, x, gain, shift, up, groups):
    rows, width = x.shape
    return pl.pallas_call(
        qkv_grad_kernel,
        grid_spec=pltpu.PrefetchScalarGridSpec(
            num_scalar_prefetch=1,
            grid=(1,),
            in_specs=[
                whole((rows, width)),
                whole((rows, width)),
                whole((rows, width)),
                whole((rows, RANK)),
                whole((rows, width)),
                whole((1, width)),
                whole((1, width)),
                chosen((RANK, 3 * width)),
            ],
            out_specs=[whole((groups, 1, RANK, LANES)), whole((rows, RANK))],
        ),
        out_shape=[
            jax.ShapeDtypeStruct((groups, 1, RANK, LANES), BF16),
            jax.ShapeDtypeStruct((rows, RANK), BF16),
        ],
        compiler_params=params(),
        cost_estimate=cost(2 * rows * 16 * 3 * width * 4, 8 * rows * width),
        name="qkv_grad",
    )(at, *g, low, x, gain, shift, up)


def input_grad_kernel(at, gq, gk, gv, w, rank_grad, down, x, gain, dx1, out, total):
    j = pl.program_id(0)

    @pl.when(j == 0)
    def _():
        total[...] = dot(rank_grad[...], down[0]) + dot(gq[...], w[...], NT)

    @pl.when(j == 1)
    def _():
        total[...] += dot(gk[...], w[...], NT)

    @pl.when(j == 2)
    def _():
        grad = total[...] + dot(gv[...], w[...], NT)
        normed, spread = norm_rows(x[...].astype(F32))
        out[...] = dx1[...] + norm_back(grad, normed, spread, gain[...])


def input_grad(at, g, w, rank_grad, down, x, gain, dx1):
    rows, width = x.shape
    block = whole((rows, width))
    return pl.pallas_call(
        input_grad_kernel,
        grid_spec=pltpu.PrefetchScalarGridSpec(
            num_scalar_prefetch=1,
            grid=(3,),
            in_specs=[
                block,
                block,
                block,
                pl.BlockSpec((width, width), lambda j, at: (0, j)),
                whole((rows, RANK)),
                chosen((RANK, width)),
                block,
                whole((1, width)),
                block,
            ],
            out_specs=block,
            scratch_shapes=[pltpu.VMEM((rows, width), F32)],
        ),
        out_shape=jax.ShapeDtypeStruct((rows, width), F32),
        compiler_params=params(),
        cost_estimate=cost(6 * rows * width * width, 6 * width * width + 16 * rows * width),
        name="input_grad",
    )(at, *g, w, rank_grad, down, x, gain, dx1)


def swap_order():
    bits = []
    n = 1
    while n < lax.axis_size("seq"):
        bits.append((0, n))
        n *= 2
    n = 2
    while n < lax.axis_size("dp"):
        bits.append((n, 0))
        n *= 2
    first = bits[:4]
    second = [first[1], first[0], first[3], first[2]]
    return (first, second), bits[4:]


def swap(values, step):
    size, ways = lax.axis_size("dp"), lax.axis_size("seq")
    perm = []
    for d in range(size):
        flip_d, flip_s = step[d & 1]
        for s in range(ways):
            perm.append((d * ways + s, (d ^ flip_d) * ways + (s ^ flip_s)))
    return lax.ppermute(values, ("dp", "seq"), perm)


def device_codes():
    orders, _rest = swap_order()
    d, s = lax.axis_index("dp"), lax.axis_index("seq")
    codes = []
    for order in orders:
        code = jnp.int32(0)
        for n, (bit_d, bit_s) in enumerate(order):
            on = ((d & bit_d) | (s & bit_s)) != 0
            code = code + jnp.where(on, 8 >> n, 0).astype(jnp.int32)
        codes.append(code)
    core = (d & 1).astype(jnp.int32)
    return core, jnp.where(core == 0, *codes), jnp.where(core == 0, codes[1], codes[0])


def slot_owners(index_all):
    orders, _rest = swap_order()
    masks = []
    for order in orders:
        slots = [0, 1]
        for bit_d, _s in order:
            slots = slots + [slot ^ bit_d for slot in slots]
        masks.append(np.array(slots, np.int32))
    d = lax.axis_index("dp")
    return index_all[d ^ jnp.where((d & 1) == 0, *masks)]


def scatter_steps():
    orders, _rest = swap_order()
    return [((1, 0), (1, 0))] + list(zip(*orders))


def scatter_stage(held, step):
    half = held.shape[1] // 2
    return jnp.concatenate([held[:, :half], swap(held[:, half:], step)], axis=0)


def owner_sum_kernel(owners, held, out, total):
    total[...] = jnp.zeros_like(total)
    for n in range(held.shape[0]):
        total[owners[n]] += held[n].astype(F32)
    for a in range(NADAPT):
        out[:, a] = total[a].astype(BF16)


def owner_sum(owners, held):
    slots, one, parts, rank, lanes = held.shape
    held = held.reshape(slots, parts, rank, lanes)
    out = pl.pallas_call(
        owner_sum_kernel,
        grid_spec=pltpu.PrefetchScalarGridSpec(
            num_scalar_prefetch=1,
            grid=(1,),
            in_specs=[whole(held.shape)],
            out_specs=whole((parts, NADAPT, rank, lanes)),
            scratch_shapes=[pltpu.VMEM((NADAPT, parts, rank, lanes), F32)],
        ),
        out_shape=jax.ShapeDtypeStruct((parts, NADAPT, rank, lanes), BF16),
        compiler_params=params(),
        cost_estimate=cost(held.size, 2 * held.size),
        name="owner_sum",
    )(owners, held)
    _orders, rest = swap_order()
    for bits in rest:
        out = (out.astype(F32) + swap(out, (bits, bits)).astype(F32)).astype(BF16)
    return out[None]


def gather_stage(total, step):
    return jnp.concatenate([total, swap(total, step)], axis=0)


def spread_kernel(at, mine, theirs, *outs, plan):
    for ref, part, first, count in zip(outs, *plan):
        for p in range(count):
            piece = jnp.int32(first + p)
            top = (piece >> 4) ^ at[1]
            low = (piece & 15) ^ jnp.where(top == 0, at[2], at[3])

            @pl.when(top == 0)
            def _():
                ref[:, :, p * LANES : (p + 1) * LANES] = mine[low, part].astype(F32)

            @pl.when(top != 0)
            def _():
                ref[:, :, p * LANES : (p + 1) * LANES] = theirs[low, part].astype(F32)


def spread(at, mine, theirs, plan):
    parts, firsts, counts = plan
    shapes = [(NADAPT, RANK, count * LANES) for count in counts]
    return pl.pallas_call(
        functools.partial(spread_kernel, plan=plan),
        grid_spec=pltpu.PrefetchScalarGridSpec(
            num_scalar_prefetch=1,
            grid=(1,),
            in_specs=[whole(mine.shape), whole(theirs.shape)],
            out_specs=[whole(shape) for shape in shapes],
        ),
        out_shape=[jax.ShapeDtypeStruct(shape, F32) for shape in shapes],
        compiler_params=params(),
        cost_estimate=cost(1, 12 * mine.size),
        name="spread",
    )(at, mine, theirs)


def tie(*values):
    flat, tree = jax.tree.flatten(values)
    return jax.tree.unflatten(tree, lax.optimization_barrier(flat))


def body(
    clip_tokens, adapter_index, ln1_gain, ln1_bias, qkv_weight, qkv_bias, qkv_down, qkv_up,
    out_weight, out_bias, out_down, out_up, ln2_gain, ln2_bias, fc1_weight, fc1_bias, fc1_down,
    fc1_up, fc2_weight, fc2_bias, fc2_down, fc2_up, cotangent,
):
    _one, rows, width = clip_tokens.shape
    devices = lax.axis_size("seq")
    here = lax.axis_index("seq")
    groups = 32
    row = lambda v: v.reshape(1, -1)
    x = clip_tokens[0]
    cot = cotangent[0]
    adapter = adapter_index[0]
    peers = range(1, devices)
    code = jnp.stack((adapter,) + device_codes())
    at = jnp.stack([adapter, here])
    at_peer = jnp.stack([adapter] + [(here + n) % devices for n in peers])
    tagged = jnp.broadcast_to(adapter_index.astype(BF16)[:, None], (256, LANES))
    tags = lax.all_gather(lax.optimization_barrier(tagged), "dp", axis=0, tiled=True)
    index_all = lax.optimization_barrier(tags)[::256, 0].astype(jnp.int32)
    owners = slot_owners(index_all)

    def from_peer(values, shift):
        return lax.ppermute(values, "seq", [((n + shift) % devices, n) for n in range(devices)])

    cos, sin = (jnp.asarray(t) for t in rotary_tables(rows * devices))
    x_peer = jnp.concatenate([from_peer(x, n) for n in peers], axis=0)
    first_set = (row(ln1_gain), row(ln1_bias), qkv_weight, row(qkv_bias), qkv_down, qkv_up)
    own, low_qkv = qkv_rows(at, x, *first_set, cos, sin, rows)
    back, grad2 = back_rows(at, cot, fc2_weight, fc2_down, fc2_up)
    state = attend(own, own)
    peer, _low = qkv_rows(at_peer, x_peer, *first_set, cos, sin, rows)
    mixed, lse = attend(own, peer, state)
    act, x1, low2, dx1, go, delta, pieces_a = block_rows(
        code, x, mixed, cot, lse, back, grad2,
        (out_weight, row(out_bias), out_down, out_up),
        (row(ln2_gain), row(ln2_bias)),
        (fc1_weight, row(fc1_bias), fc1_down, fc1_up),
        fc2_down, groups,
    )
    go_sent, sent, delta = tie(go, pieces_a[None], delta)
    go_peer = jnp.stack([from_peer(go_sent, n) for n in peers])
    steps = scatter_steps()

    def halves(held):
        half = held.shape[1] // 2
        return held[:, :half], held[:, half:]

    def join(*parts):
        return jnp.concatenate(parts, axis=0)

    grads = None
    for n, step in enumerate(steps[:4]):
        kept, sent = halves(sent)
        sent, delta = tie(sent, delta)
        arrived = swap(sent, step)
        grads = own_back(at, own, peer, go, lse, delta, cos, sin, (2 * n, 2), grads)
        arrived, grads, delta = tie(arrived, grads, delta)
        sent = join(kept, arrived)
    dq, dk, dv = grads
    kept, sent = halves(sent)
    sent, dk, go_peer = tie(sent, dk, go_peer)
    arrived = swap(sent, steps[4])
    back_kv = peer_back(at, own, peer, go_peer, cos, sin, dk, dv, (0, 4), None)
    arrived, back_kv, go_peer = tie(arrived, back_kv, go_peer)
    total_a = owner_sum(owners, join(kept, arrived))
    total_a, back_kv, go_peer = tie(total_a, back_kv, go_peer)
    arrived = swap(total_a, steps[4])
    back_kv = peer_back(at, own, peer, go_peer, cos, sin, dk, dv, (4, 4), back_kv)
    arrived, grads = tie(arrived, (dq,) + tuple(back_kv))
    total_a = join(total_a, arrived)
    total_a, grads = tie(total_a, grads)
    arrived_a = swap(total_a, steps[3])
    pieces_b, rank_grad = qkv_grad(
        code, grads, low_qkv[0], x, row(ln1_gain), row(ln1_bias), qkv_up, groups
    )
    held, arrived_a = tie(scatter_stage(pieces_b[None], steps[0]), arrived_a)
    total_a = join(total_a, arrived_a)

    kept, sent = halves(held)
    sent, total_a, rank_grad = tie(sent, total_a, rank_grad)
    arrived = swap(sent, steps[1])
    arrived_a = swap(total_a, steps[2])
    grad_in = input_grad(at, grads, qkv_weight, rank_grad, qkv_down, x, row(ln1_gain), dx1)
    arrived, arrived_a, grad_in = tie(arrived, arrived_a, grad_in)
    kept, sent = halves(join(kept, arrived))
    total_a = join(total_a, arrived_a)
    sent, total_a, low2 = tie(sent, total_a, low2)
    arrived = swap(sent, steps[2])
    arrived_a = swap(total_a, steps[1])
    block_output = output_rows(at, act, fc2_weight, x1, row(fc2_bias), low2, fc2_up)
    arrived, block_output = tie(arrived, block_output)
    held = scatter_stage(join(kept, arrived), steps[3])
    held = scatter_stage(held, steps[4])
    total_b = owner_sum(owners, held)
    total_b, total_a, arrived_a = tie(total_b, total_a, arrived_a)
    total_a = join(total_a, arrived_a)
    theirs_a = swap(total_a, steps[0])
    for step in steps[4:2:-1]:
        total_b = gather_stage(total_b, step)
    per = width // LANES
    total_b, total_a, theirs_a = tie(total_b, total_a, theirs_a)
    arrived = swap(total_b, steps[2])
    spread_a = spread(
        code, total_a, theirs_a,
        ((0, 1, 2, 2, 2, 2), (0, 0, 0, per, 2 * per, 3 * per), (32, 32, per, per, per, per)),
    )
    arrived, spread_a = tie(arrived, spread_a)
    up1, down2, up2, down1, up_o, down_o = spread_a
    total_b = gather_stage(join(total_b, arrived), steps[1])
    up_qkv, down_qkv = spread(
        code, total_b, swap(total_b, steps[0]), ((0, 0), (0, 3 * per), (3 * per, per))
    )
    return (
        block_output[None], grad_in[None], down_qkv, up_qkv, down_o, up_o, down1, up1, down2, up2,
    )


def solution(mesh):
    split = P("dp", "seq", None)
    return jax.shard_map(
        body,
        mesh=mesh,
        in_specs=(split, P("dp")) + (P(),) * 20 + (split,),
        out_specs=(split, split) + (P(),) * 8,
        check_vma=False,
    )
```

```python
import functools

import jax
import jax.numpy as jnp
import numpy as np
from jax import lax
from jax.experimental import pallas as pl
from jax.experimental.pallas import tpu as pltpu
from jax.sharding import PartitionSpec as P

HEADS = 16
HD = 64
GRID = 16
NADAPT = 8
RANK = 16
EPSILON = 1e-06
LANES = 128
EXTRA = 48

F32 = jnp.float32
BF16 = jnp.bfloat16
NN = (((1,), (0,)), ((), ()))
NT = (((1,), (1,)), ((), ()))

ERFC = (
    0.16918800211151383,
    0.1707152747822528,
    0.14833885959986734,
    0.21492717178376733,
    -0.09465313901935662,
    0.5477232747113128,
    -0.5122807406271995,
    0.48556441585520754,
    -0.1295231387829952,
)


def dot(a, b, dims=NN):
    return lax.dot_general(a, b, dims, preferred_element_type=F32)


def params(megabytes):
    return pltpu.CompilerParams(
        dimension_semantics=("arbitrary",), vmem_limit_bytes=megabytes << 20
    )


def cost(flops, moved, exps=0):
    return pl.CostEstimate(flops=int(flops), bytes_accessed=int(moved), transcendentals=int(exps))


def norm_rows(values):
    centre = values - jnp.mean(values, axis=-1, keepdims=True)
    spread = lax.rsqrt(jnp.mean(centre * centre, axis=-1, keepdims=True) + EPSILON)
    return centre * spread, spread


def norm_back(grad_rows, normed, spread, gain):
    scaled = grad_rows * gain
    first = jnp.mean(scaled, axis=-1, keepdims=True)
    second = jnp.mean(scaled * normed, axis=-1, keepdims=True)
    return spread * (scaled - first - normed * second)


def rotary_tables(length):
    half = HD // 2
    side = half // 3
    lead = half - 2 * side
    token = np.arange(length)
    pair = np.arange(half)
    kind = np.where(pair < lead, 0, np.where(pair < lead + side, 1, 2))
    local = np.where(kind == 0, pair, np.where(kind == 1, pair - lead, pair - lead - side))
    total = np.where(kind == 0, lead, side)
    frequency = np.power(
        np.float32(10000.0), -local.astype(np.float32) / total.astype(np.float32)
    ).astype(np.float32)
    place = np.where(
        kind[None] == 0,
        (token // (GRID * GRID))[:, None],
        np.where(kind[None] == 1, (token // GRID % GRID)[:, None], (token % GRID)[:, None]),
    ).astype(np.float32)
    angle = place * frequency[None]
    cosine, sine = np.cos(angle), np.sin(angle)
    cos_rows = np.concatenate([cosine] * 4, axis=1).astype(np.float32)
    sin_rows = np.concatenate([-sine, sine, -sine, sine], axis=1).astype(np.float32)
    return cos_rows, sin_rows


def swap_halves(values):
    lane = lax.broadcasted_iota(jnp.int32, (1, LANES), 1)
    low = (lane & (HD // 2)) == 0
    return jnp.where(
        low, pltpu.roll(values, LANES - HD // 2, 1), pltpu.roll(values, HD // 2, 1)
    )


def head_mask(values, head):
    lane = lax.broadcasted_iota(jnp.int32, (1, LANES), 1)
    keep = (lane < HD) if head == 0 else (lane >= HD)
    return jnp.where(keep, values, jnp.zeros_like(values))


def whole(shape):
    return pl.BlockSpec(shape, lambda *_: (0,) * len(shape))


def fixed(shape):
    return pl.BlockSpec(shape, lambda *_: (0,) * len(shape), pipeline_mode=pl.Buffered(1))


def chosen(shape):
    return pl.BlockSpec((1,) + shape, lambda *ids: (ids[-2][0], 0, 0))


def chosen_tile(tile, which):
    return pl.BlockSpec((1, RANK, tile), lambda j, adapter, at: (adapter[0], 0, which(j)))


def position(piece, at):
    top = (piece >> 4) ^ at[1]
    return 16 * top + ((piece & 15) ^ jnp.where(top == 0, at[2], at[3]))


CHUNK = 256


def qkv_tile(tile, h1, low, w, bias, up, cos, sin, out_ref, keep, first):
    scale = jnp.where(tile == 0, HD**-0.5, 1.0).astype(F32)
    turn = jnp.where(tile == 2, 0.0, 1.0).astype(F32)
    c = (cos[...] * turn + (1.0 - turn)) * scale
    s = sin[...] * (turn * scale)

    def chunk(n):
        cut = slice(n * CHUNK, (n + 1) * CHUNK)
        return dot(h1, w[:, cut]) + bias[:, cut] + dot(low, up[:, cut])

    count = w.shape[1] // CHUNK
    now = chunk(0)
    parts = []
    for n in range(count):
        later = chunk(n + 1) if n + 1 < count else None
        for g in range(CHUNK // LANES):
            part = now[:, g * LANES : (g + 1) * LANES]
            parts.append((part * c + swap_halves(part) * s).astype(BF16))
        now = later
    for n, part in enumerate(parts):
        out_ref[n] = part
        keep[first + n] = part


def attend_pairs(count, load, finish):
    loaded = [load(pair) for pair in range(count)]
    values_t = [v.T for _q, _k, v in loaded]

    def scores(item):
        pair, head = item
        q, k, _v = loaded[pair]
        return dot(k, head_mask(q, head), NT)

    items = [(pair, head) for pair in range(count) for head in range(2)]
    now = scores(items[0])
    for n, (pair, head) in enumerate(items):
        later = scores(items[n + 1]) if n + 1 < len(items) else None
        finish(pair, head, now, values_t[pair][head * HD : (head + 1) * HD])
        now = later


STEP_PAIRS = 2


def start_all(*groups):
    for group in groups:
        for copy in group:
            copy.start()


def wait_all(*groups):
    for group in groups:
        for copy in group:
            copy.wait()


def group(sems, pairs):
    return [pltpu.make_async_copy(a, b, sems.at[n]) for n, (a, b) in enumerate(pairs)]


def tiles(source, kept, size):
    return [(source.at[:, pl.ds(n * size, size)], kept.at[n]) for n in range(kept.shape[0])]


def front_kernel(
    adapter, at, x, w, w2,
    gain, shift, bias, down, up, cos, sin, cot, down2, up2,
    qkv, mixed_out, back, low, top_out, total_out, grad2,
    h1, keep, gain_k, shift_k, bias_k, down_k, up_k, cos_k, sin_k, cot_k, down2_k, up2_k,
    low_k, top_k, total_k, grad2_k, sem_a, sem_b, sem_c, sem_d,
    *, starts,
):
    j = pl.program_id(0)
    second, third = starts
    last = pl.num_programs(0) - 1
    mine = adapter[0]
    rows, width = x.shape
    place = pl.ds(pl.multiple_of(at[0] * rows, rows), rows)
    early = group(
        sem_a,
        [
            (gain, gain_k), (shift, shift_k), (down.at[mine], down_k),
            (cos.at[place], cos_k), (sin.at[place], sin_k),
        ]
        + tiles(bias, bias_k, width)
        + tiles(up.at[mine], up_k, width),
    )
    late = group(
        sem_b, [(cot, cot_k), (up2.at[mine], up2_k)] + tiles(down2.at[mine], down2_k, w2.shape[0])
    )
    stats = group(sem_c, [(low_k, low), (top_k, top_out), (total_k, total_out)])
    end = group(sem_d, [(grad2_k, grad2)])

    @pl.when(j == 0)
    def _():
        start_all(early, late)
        normed, _s = norm_rows(x[...].astype(F32))
        wait_all(early)
        held = (normed * gain_k[...] + shift_k[...]).astype(BF16)
        h1[...] = held
        low_k[...] = dot(held, down_k[...], NT).astype(BF16)

    @pl.when(j < second)
    def _():
        qkv_tile(j, h1[...], low_k[...], w, bias_k[j], up_k[j], cos_k, sin_k, qkv, keep, 8 * j)

    @pl.when((j >= second) & (j < third))
    def _():
        first = (j - second) * STEP_PAIRS

        def load(pair):
            return keep[first + pair], keep[8 + first + pair], keep[16 + first + pair]

        def finish(pair, head, scores, values_t):
            top = jnp.max(scores, axis=0, keepdims=True)
            weights = jnp.exp(scores - top)
            start = pair * LANES + head * HD
            mixed_out[start : start + HD, :] = dot(values_t, weights.astype(BF16))
            top_k[first + pair, head : head + 1, :] = top
            total_k[first + pair, head : head + 1, :] = jnp.sum(weights, axis=0, keepdims=True)

        attend_pairs(STEP_PAIRS, load, finish)

    @pl.when(j == third)
    def _():
        start_all(stats)
        wait_all(late)
        grad2_k[...] = dot(cot_k[...], up2_k[...], NT).astype(BF16)
        start_all(end)

    @pl.when(j >= third)
    def _():
        side = dot(grad2_k[...], down2_k[j - third])
        back[...] = (dot(cot_k[...], w2[...], NT) + side).astype(BF16)

    @pl.when(j == last)
    def _():
        wait_all(stats, end)


def clip(value, low, high):
    return jnp.minimum(jnp.maximum(value, low), high)


ANY = pl.BlockSpec(memory_space=pl.ANY)


def front_rows(at, x, cot, first_set, tables, w2, down2, up2):
    gain, shift, w, bias, down, up = first_set
    rows, width = x.shape
    ff = w2.shape[0]
    tile = 1024
    second = w.shape[1] // width
    third = second + HEADS // 2 // STEP_PAIRS
    steps = third + ff // tile
    one = lambda j: jnp.minimum(j, second - 1)
    two = lambda j: clip(j - second, 0, third - second - 1)
    three = lambda j: clip(j - third, 0, steps - third - 1)
    stat = (HEADS // 2, 2, rows)
    return pl.pallas_call(
        functools.partial(front_kernel, starts=(second, third)),
        grid_spec=pltpu.PrefetchScalarGridSpec(
            num_scalar_prefetch=2,
            grid=(steps,),
            in_specs=[
                fixed((rows, width)),
                pl.BlockSpec((width, width), lambda j, adapter, at: (0, one(j))),
                pl.BlockSpec((tile, width), lambda j, adapter, at: (three(j), 0)),
            ]
            + [ANY] * 10,
            out_specs=[
                pl.BlockSpec((8, rows, LANES), lambda j, adapter, at: (one(j), 0, 0)),
                pl.BlockSpec((STEP_PAIRS * LANES, rows), lambda j, adapter, at: (two(j), 0)),
                pl.BlockSpec((rows, tile), lambda j, adapter, at: (0, three(j))),
            ]
            + [ANY] * 4,
            scratch_shapes=[
                pltpu.VMEM((rows, width), BF16),
                pltpu.VMEM((24, rows, LANES), BF16),
                pltpu.VMEM((1, width), F32),
                pltpu.VMEM((1, width), F32),
                pltpu.VMEM((second, 1, width), F32),
                pltpu.VMEM((RANK, width), BF16),
                pltpu.VMEM((second, RANK, width), BF16),
                pltpu.VMEM((rows, LANES), F32),
                pltpu.VMEM((rows, LANES), F32),
                pltpu.VMEM((rows, width), BF16),
                pltpu.VMEM((ff // tile, RANK, tile), BF16),
                pltpu.VMEM((RANK, width), BF16),
                pltpu.VMEM((rows, RANK), BF16),
                pltpu.VMEM(stat, F32),
                pltpu.VMEM(stat, F32),
                pltpu.VMEM((rows, RANK), BF16),
                pltpu.SemaphoreType.DMA((5 + 2 * second,)),
                pltpu.SemaphoreType.DMA((2 + ff // tile,)),
                pltpu.SemaphoreType.DMA((3,)),
                pltpu.SemaphoreType.DMA((1,)),
            ],
        ),
        out_shape=[
            pltpu.HBM((24, rows, LANES), BF16),
            pltpu.HBM((width, rows), F32),
            pltpu.HBM((rows, ff), BF16),
            pltpu.HBM((rows, RANK), BF16),
            pltpu.HBM(stat, F32),
            pltpu.HBM(stat, F32),
            pltpu.HBM((rows, RANK), BF16),
        ],
        compiler_params=params(44),
        cost_estimate=cost(
            2 * rows * width * (3 * width + ff) + 16 * rows * rows * width, 20 << 20, 16 * rows * rows
        ),
        name="front_rows",
    )(*at, x, w, w2, gain, shift, bias, down, up, *tables, cot, down2, up2)


def gelu_both(f):
    z = jnp.abs(f) * (0.5**0.5)
    t = 1.0 / (1.0 + 0.3 * z)
    poly = ERFC[-1]
    for c in ERFC[-2::-1]:
        poly = poly * t + c
    bell = jnp.exp(f * f * -0.5)
    tail = (0.5 * poly) * t * bell
    phi = jnp.where(f < 0, tail, 1.0 - tail)
    return f * phi, phi + f * (bell * 0.3989422804014327)


def middle_kernel(
    adapter, at, xp, wq, w1, back,
    gain1, shift1, bq, downq, upq, cos, sin, own, mixed, top, total,
    x, cot, grad2, w_out, b_out, out_down, out_up, gain, shift, b1, down1, up1, down2,
    qkv, act_out, x1_out, low2_out, dx1_out, go_out, delta_out, lse_out, pieces_out,
    h1, lowq, keep, o, h2, dh2, low_o, low1, low1_t, grad2_t, low2, grad1,
    gain1_k, shift1_k, bq_k, downq_k, upq_k, cos_k, sin_k, q_own, mixed_in, top_in, total_in,
    x_k, cot_k, grad2_k, w_out_k, b_out_k, out_down_k, out_up_k, gain_k, shift_k, b1_k, down1_k, up1_k, down2_k,
    x1, low2_k, dx1_k, go, delta_k, lse, pieces,
    sem_a, sem_b, sem_c, sem_d, sem_e,
    *, starts, peers,
):
    j = pl.program_id(0)
    second, third = starts
    last = pl.num_programs(0) - 1
    rows, width = xp.shape
    tile = w1.shape[1]
    mine = adapter[0]
    places = [pl.ds(pl.multiple_of(at[6 + p] * rows, rows), rows) for p in range(peers)]
    early = group(
        sem_a,
        [(gain1, gain1_k), (shift1, shift1_k), (downq.at[mine], downq_k)]
        + [(cos.at[places[p]], cos_k.at[p]) for p in range(peers)]
        + [(sin.at[places[p]], sin_k.at[p]) for p in range(peers)]
        + tiles(bq, bq_k, width)
        + tiles(upq.at[mine], upq_k, width),
    )
    later = group(
        sem_b, [(own.at[pl.ds(0, 8)], q_own), (mixed, mixed_in), (top, top_in), (total, total_in)]
    )
    late = group(
        sem_c,
        [
            (x, x_k), (cot, cot_k), (grad2, grad2_k), (w_out, w_out_k), (b_out, b_out_k),
            (out_down.at[mine], out_down_k), (out_up.at[mine], out_up_k), (gain, gain_k),
            (shift, shift_k), (down1.at[mine], down1_k),
        ]
        + tiles(b1, b1_k, tile)
        + tiles(up1.at[mine], up1_k, tile)
        + tiles(down2.at[mine], down2_k, tile),
    )
    middle_out = group(sem_d, [(x1, x1_out), (lse, lse_out)])
    end = group(
        sem_e,
        [(low2_k, low2_out), (dx1_k, dx1_out), (go, go_out), (delta_k, delta_out), (pieces, pieces_out)],
    )

    @pl.when(j == 0)
    def _():
        start_all(early, later, late)

    @pl.when(j < second)
    def _():
        which, p = j // peers, lax.rem(j, peers)

        @pl.when(which == 0)
        def _():
            normed, _s = norm_rows(xp[...].astype(F32))

            @pl.when(j == 0)
            def _():
                wait_all(early)

            normed = (normed * gain1_k[...] + shift1_k[...]).astype(BF16)
            h1[p] = normed
            lowq[p] = dot(normed, downq_k[...], NT).astype(BF16)

        qkv_tile(
            which, h1[p], lowq[p], wq, bq_k[which], upq_k[which], cos_k.at[p], sin_k.at[p],
            qkv, keep, 24 * p + 8 * which,
        )

    @pl.when(j == second)
    def _():
        wait_all(later)

    @pl.when((j >= second) & (j < third))
    def _():
        first = (j - second) * STEP_PAIRS
        held = []

        def load(pair):
            n = first + pair
            k = [keep[24 * p + 8 + n] for p in range(peers)]
            v = [keep[24 * p + 16 + n] for p in range(peers)]
            if peers > 1:
                k, v = [jnp.concatenate(k, axis=0)], [jnp.concatenate(v, axis=0)]
            return q_own[n], k[0], v[0]

        def finish(pair, head, scores, values_t):
            n = first + pair
            before = top_in[n, head : head + 1, :]
            top = jnp.maximum(jnp.max(scores, axis=0, keepdims=True), before)
            scale = jnp.exp(before - top)
            weights = jnp.exp(scores - top)
            total = jnp.sum(weights, axis=0, keepdims=True)
            total = total + scale * total_in[n, head : head + 1, :]
            start = pl.ds(pl.multiple_of(n * LANES + head * HD, HD), HD)
            mixed = dot(values_t, weights.astype(BF16)) + scale * mixed_in[start, :]
            held.append(mixed * (1.0 / total))
            lse[n, head : head + 1, :] = top + jnp.log(total)
            if head == 1:
                o[n] = jnp.concatenate(held[-2:], axis=0).T.astype(BF16)

        attend_pairs(STEP_PAIRS, load, finish)

    def put(first, slot, grad):
        for p in range(grad.shape[1] // LANES):
            cut = slice(p * LANES, (p + 1) * LANES)
            pieces[position(first + p, at), slot] = grad[:, cut].astype(BF16)

    @pl.when(j == third)
    def _():
        wait_all(late)
        mixed = jnp.concatenate([o[n] for n in range(HEADS // 2)], axis=1)
        low = dot(mixed, out_down_k[...], NT).astype(BF16)
        low_o[...] = low
        branch = dot(mixed, w_out_k[...]) + b_out_k[...] + dot(low, out_up_k[...])
        mid = x_k[...].astype(F32) + branch
        x1[...] = mid
        normed, _s = norm_rows(mid)
        rows2 = (normed * gain_k[...] + shift_k[...]).astype(BF16)
        h2[...] = rows2
        low_1 = dot(rows2, down1_k[...], NT).astype(BF16)
        low1[...] = low_1
        low1_t[...] = low_1.T
        grad2_t[...] = grad2_k[...].T
        dh2[...] = jnp.zeros_like(dh2)
        low2[...] = jnp.zeros_like(low2)
        grad1[...] = jnp.zeros_like(grad1)
        start_all(middle_out)

    @pl.when(j >= third)
    def _():
        n_tile = j - third

        def hidden(n):
            cut = slice(n * CHUNK, (n + 1) * CHUNK)
            return dot(h2[...], w1[:, cut]) + b1_k[n_tile, :, cut] + dot(low1[...], up1_k[n_tile, :, cut])

        first = n_tile * (tile // LANES)
        count = tile // CHUNK
        now = hidden(0)
        acts, dfs = [], []
        for n in range(count):
            later = hidden(n + 1) if n + 1 < count else None
            cut = slice(n * CHUNK, (n + 1) * CHUNK)
            act, slope = gelu_both(now)
            acts.append(act.astype(BF16))
            dfs.append((back[:, cut].astype(F32) * slope).astype(BF16))
            now = later
        act, df = jnp.concatenate(acts, axis=1), jnp.concatenate(dfs, axis=1)
        dh2[...] += dot(df, w1[...], NT)
        low2[...] += dot(act, down2_k[n_tile], NT)
        grad1[...] += dot(df, up1_k[n_tile], NT)
        act_out[...] = act
        put(first, 0, dot(low1_t[...], df))
        put(first, 1, dot(grad2_t[...], act))

    @pl.when(j == last)
    def _():
        low_2 = low2[...].astype(BF16)
        low2_k[...] = low_2
        g1 = grad1[...].astype(BF16)
        back2 = dh2[...] + dot(g1, down1_k[...])
        normed, spread = norm_rows(x1[...])
        dx1 = cot_k[...].astype(F32) + norm_back(back2, normed, spread, gain_k[...])
        dx1_k[...] = dx1
        da = dx1.astype(BF16)
        g_o = dot(da, out_up_k[...], NT).astype(BF16)
        new_go = (dot(da, w_out_k[...], NT) + dot(g_o, out_down_k[...])).astype(BF16)
        go[EXTRA : EXTRA + rows, :] = new_go
        mixed = jnp.concatenate([o[n] for n in range(HEADS // 2)], axis=1)
        product = new_go.astype(F32) * mixed.astype(F32)
        high = product.astype(BF16)
        rest = (product - high.astype(F32)).astype(BF16)
        lane = lax.broadcasted_iota(jnp.int32, (HEADS, width), 1)
        head = lax.broadcasted_iota(jnp.int32, (HEADS, width), 0)
        pick = (lane // HD == head).astype(BF16)
        delta = dot(pick, high, NT) + dot(pick, rest, NT)
        delta_k[...] = delta
        if rows < width // 2:
            go[0:EXTRA, :] = jnp.zeros((EXTRA, width), BF16)
        logs = jnp.concatenate([lse[n] for n in range(HEADS // 2)], axis=0)
        for side, stat in enumerate((logs, delta)):
            left = stat
            for n in range(3):
                part = left.astype(BF16)
                go[16 * n : 16 * n + 16, side * (width // 2) : side * (width // 2) + rows] = part
                left = left - part.astype(F32)
        start_all(end[:4])
        per = width // LANES
        put(jnp.int32(0), 2, dot(low_2.T, cot_k[...]))
        put(jnp.int32(per), 2, dot(g1.T, h2[...]))
        put(jnp.int32(2 * per), 2, dot(low_o[...].T, da))
        put(jnp.int32(3 * per), 2, dot(g_o.T, mixed))
        start_all(end[4:])
        wait_all(middle_out, end)


def middle_rows(
    at, xp, first_set, tables, own, state, x, cot, back, grad2, out_set, norm_set, fc1_set, down2, groups
):
    rows, width = x.shape
    peers = xp.shape[0] // rows
    w1 = fc1_set[0]
    ff = w1.shape[1]
    tile = 1024
    second = 3 * peers
    third = second + HEADS // 2 // STEP_PAIRS
    steps = third + ff // tile
    one = lambda j: jnp.minimum(j, second - 1) // peers
    peer = lambda j: lax.rem(jnp.minimum(j, second - 1), peers)
    two = lambda j: clip(j - second, 0, third - second - 1)
    three = lambda j: clip(j - third, 0, steps - third - 1)
    stat = (HEADS // 2, 2, rows)
    count = ff // tile
    vmem = pltpu.VMEM
    return pl.pallas_call(
        functools.partial(middle_kernel, starts=(second, third), peers=peers),
        grid_spec=pltpu.PrefetchScalarGridSpec(
            num_scalar_prefetch=2,
            grid=(steps,),
            in_specs=[
                pl.BlockSpec((rows, width), lambda j, adapter, at: (jnp.minimum(j, peers - 1), 0)),
                pl.BlockSpec((width, width), lambda j, adapter, at: (0, one(j))),
                pl.BlockSpec((width, tile), lambda j, adapter, at: (0, three(j))),
                pl.BlockSpec((rows, tile), lambda j, adapter, at: (0, three(j))),
            ]
            + [ANY] * 24,
            out_specs=[
                pl.BlockSpec((8, rows, LANES), lambda j, adapter, at: (3 * peer(j) + one(j), 0, 0)),
                pl.BlockSpec((rows, tile), lambda j, adapter, at: (0, three(j))),
            ]
            + [ANY] * 7,
            scratch_shapes=[
                vmem((peers, rows, width), BF16),
                vmem((peers, rows, RANK), BF16),
                vmem((24 * peers, rows, LANES), BF16),
                vmem((HEADS // 2, rows, LANES), BF16),
                vmem((rows, width), BF16),
                vmem((rows, width), F32),
                vmem((rows, RANK), BF16),
                vmem((rows, RANK), BF16),
                vmem((RANK, rows), BF16),
                vmem((RANK, rows), BF16),
                vmem((rows, RANK), F32),
                vmem((rows, RANK), F32),
                vmem((1, width), F32),
                vmem((1, width), F32),
                vmem((3, 1, width), F32),
                vmem((RANK, width), BF16),
                vmem((3, RANK, width), BF16),
                vmem((peers, rows, LANES), F32),
                vmem((peers, rows, LANES), F32),
                vmem((8, rows, LANES), BF16),
                vmem((width, rows), F32),
                vmem(stat, F32),
                vmem(stat, F32),
                vmem((rows, width), BF16),
                vmem((rows, width), BF16),
                vmem((rows, RANK), BF16),
                vmem((width, width), BF16),
                vmem((1, width), F32),
                vmem((RANK, width), BF16),
                vmem((RANK, width), BF16),
                vmem((1, width), F32),
                vmem((1, width), F32),
                vmem((count, 1, tile), F32),
                vmem((RANK, width), BF16),
                vmem((count, RANK, tile), BF16),
                vmem((count, RANK, tile), BF16),
                vmem((rows, width), F32),
                vmem((rows, RANK), BF16),
                vmem((rows, width), F32),
                vmem((EXTRA + rows, width), BF16),
                vmem((HEADS, rows), F32),
                vmem(stat, F32),
                vmem((groups, 3, RANK, LANES), BF16),
                pltpu.SemaphoreType.DMA((9 + 2 * peers,)),
                pltpu.SemaphoreType.DMA((4,)),
                pltpu.SemaphoreType.DMA((10 + 3 * count,)),
                pltpu.SemaphoreType.DMA((2,)),
                pltpu.SemaphoreType.DMA((5,)),
            ],
        ),
        out_shape=[
            pltpu.HBM((24 * peers, rows, LANES), BF16),
            pltpu.HBM((rows, ff), BF16),
            pltpu.HBM((rows, width), F32),
            pltpu.HBM((rows, RANK), BF16),
            pltpu.HBM((rows, width), F32),
            pltpu.HBM((EXTRA + rows, width), BF16),
            pltpu.HBM((HEADS, rows), F32),
            pltpu.HBM(stat, F32),
            pltpu.HBM((groups, 3, RANK, LANES), BF16),
        ],
        compiler_params=params(60),
        cost_estimate=cost(
            4 * rows * width * ff + (4 + 6 * peers) * rows * width * width, 40 << 20, rows * ff
        ),
        name="middle_rows",
    )(
        *at, xp, first_set[2], w1, back,
        first_set[0], first_set[1], first_set[3], first_set[4], first_set[5], *tables, own, *state,
        x, cot, grad2, *out_set, *norm_set, *fc1_set[1:], down2,
    )


def output_kernel(_adapter, at, act, w2, x1, b2, low2, up2, out, y):
    j = pl.program_id(0)

    @pl.when(j == 0)
    def _():
        y[...] = x1[...] + (b2[...] + dot(low2[...], up2[0]))

    y[...] += dot(act[...], w2[...])

    @pl.when(j == pl.num_programs(0) - 1)
    def _():
        out[...] = y[...].astype(BF16)


def output_rows(at, act, w2, x1, b2, low2, up2):
    rows, ff = act.shape
    width = x1.shape[1]
    tile = 1024
    return pl.pallas_call(
        output_kernel,
        grid_spec=pltpu.PrefetchScalarGridSpec(
            num_scalar_prefetch=2,
            grid=(ff // tile,),
            in_specs=[
                pl.BlockSpec((rows, tile), lambda j, adapter, at: (0, j)),
                pl.BlockSpec((tile, width), lambda j, adapter, at: (j, 0)),
                whole((rows, width)),
                whole((1, width)),
                whole((rows, RANK)),
                chosen((RANK, width)),
            ],
            out_specs=whole((rows, width)),
            scratch_shapes=[pltpu.VMEM((rows, width), F32)],
        ),
        out_shape=jax.ShapeDtypeStruct((rows, width), BF16),
        compiler_params=params(24),
        cost_estimate=cost(2 * rows * width * ff, 2 * width * ff + 2 * rows * ff),
        name="output_rows",
    )(*at, act, w2, x1, b2, low2, up2)


def unrotate(values, cos, sin):
    return values * cos[...] - swap_halves(values) * sin[...]


def score_grads(s, dp, lse, delta):
    prob = jnp.exp(s - lse)
    return prob.astype(BF16), (prob * (dp - delta)).astype(BF16)


def own_back_kernel(_adapter, at, q0, k0, v0, go, lse0, delta0, cos, sin, *refs, first_pair, peers):
    k1, v1 = refs[:peers], refs[peers : 2 * peers]
    dq, dk, dv = refs[-3:]
    i = pl.program_id(0) + first_pair
    rows = q0.shape[1]
    keys = jnp.concatenate([k0[0]] + [k[0] for k in k1], axis=0)
    values = jnp.concatenate([v0[0]] + [v[0] for v in v1], axis=0)
    keys_t = keys.T

    def first(head):
        q = head_mask(q0[0], head)
        g = head_mask(go[EXTRA : EXTRA + rows, :], head)
        return dot(keys, q, NT), dot(values, g, NT), q, g

    grad_q = []
    now = first(0)
    for head in range(2):
        later = first(1) if head == 0 else None
        s, dp, q, g = now
        row = pl.ds(2 * i + head, 1)
        prob, ds = score_grads(s, dp, lse0[i, head : head + 1, :], delta0[row, :])
        grad_q.append(dot(keys_t[head * HD : (head + 1) * HD], ds))
        more_v = dot(prob[:rows], g)
        more_k = dot(ds[:rows], q)
        if head == 0:
            dv[...] = more_v
            dk[...] = more_k
        else:
            dv[...] += more_v
            dk[...] += more_k
        now = later
    dq[0] = unrotate(jnp.concatenate(grad_q, axis=0).T * (HD**-0.5), cos, sin).astype(BF16)


def peer_back_kernel(_adapter, at, k0, v0, gp, stats, cos, sin, dk_in, dv_in, *refs, first_pair, peers):
    q1 = refs[:peers]
    out, lse1, delta1 = refs[-3:]
    i = pl.program_id(0) + first_pair
    rows = k0.shape[1]
    half = stats.shape[2] // 2

    @pl.when(i == first_pair)
    def _():
        for n in range(peers):
            for side, ref in enumerate((lse1, delta1)):
                cut = slice(side * half, side * half + rows)
                ref[n] = (
                    stats[n, 0:16, cut].astype(F32)
                    + stats[n, 16:32, cut].astype(F32)
                    + stats[n, 32:48, cut].astype(F32)
                )

    def first(item):
        head, peer = item
        q = head_mask(q1[peer][0], head)
        g = head_mask(gp[peer, EXTRA : EXTRA + rows, :], head)
        return dot(k0[0], q, NT), dot(v0[0], g, NT), q, g

    items = [(head, peer) for peer in range(peers) for head in range(2)]
    grad_k, grad_v = dk_in[...], dv_in[...]
    now = first(items[0])
    for n, (head, peer) in enumerate(items):
        later = first(items[n + 1]) if n + 1 < len(items) else None
        s, dp, q, g = now
        row = pl.ds(2 * i + head, 1)
        prob, ds = score_grads(s, dp, lse1[peer, row, :], delta1[peer, row, :])
        grad_v = grad_v + dot(prob, g)
        grad_k = grad_k + dot(ds, q)
        now = later
    out[0] = unrotate(grad_k, cos, sin).astype(BF16)
    out[1] = grad_v.astype(BF16)


def attend_back(limit, kernel, at, args, specs, outs, blocks, before, pairs, peers, scratch, flops, name):
    first, count = pairs
    before = () if before is None else tuple(before)
    steps = HEADS // 2
    return pl.pallas_call(
        functools.partial(kernel, first_pair=first, peers=peers),
        grid_spec=pltpu.PrefetchScalarGridSpec(
            num_scalar_prefetch=2,
            grid=(count,),
            in_specs=specs + [pl.BlockSpec(memory_space=pl.ANY)] * len(before),
            out_specs=[pl.BlockSpec((blocks[0], outs[0].shape[1], LANES), lambda i, adapter, at: (blocks[1], 0, i + first))]
            + [pl.BlockSpec((o.shape[0], LANES), lambda i, adapter, at: (0, i + first)) for o in outs[1:]],
            scratch_shapes=scratch,
        ),
        out_shape=outs,
        input_output_aliases={2 + len(args) + n: n for n in range(len(before))},
        compiler_params=params(limit),
        cost_estimate=cost(
            flops * count // steps,
            4 * sum(a.size for a in args[:4]) * count // steps,
            flops * count // steps // 512,
        ),
        name=name,
    )(*at, *args, *before)


def own_back(at, own, peer, go, lse, delta, cos, sin, pairs, before):
    rows = own.shape[1]
    peers = peer.shape[0] // 24
    width = own.shape[0] // 3 * LANES
    first = pairs[0]

    def part(which):
        return pl.BlockSpec((1, rows, LANES), lambda i, adapter, at: (8 * which + first + i, 0, 0))

    table = pl.BlockSpec((rows, LANES), lambda i, adapter, at: (at[0], 0), pipeline_mode=pl.Buffered(1))
    return attend_back(
        24,
        own_back_kernel,
        at,
        (own, own, own, go, lse, delta, cos, sin) + (peer,) * (2 * peers),
        [part(0), part(1), part(2)]
        + [pl.BlockSpec((rows + EXTRA, LANES), lambda i, adapter, at: (0, i + first))]
        + [fixed((HEADS // 2, 2, rows)), fixed((HEADS, rows)), table, table]
        + [part(3 * p + 1) for p in range(peers)]
        + [part(3 * p + 2) for p in range(peers)],
        [jax.ShapeDtypeStruct((3, rows, width), BF16)] + [pltpu.HBM((rows, width), F32)] * 2,
        (1, 2),
        before,
        pairs,
        peers,
        [],
        2 * rows * width * 4 * rows * (5 + 3 * peers),
        "own_back",
    )


def peer_back(at, own, peer, gp, cos, sin, dk, dv, pairs, before):
    rows = own.shape[1]
    peers = gp.shape[0]
    width = own.shape[0] // 3 * LANES
    first = pairs[0]

    def part(which):
        return pl.BlockSpec((1, rows, LANES), lambda i, adapter, at: (8 * which + first + i, 0, 0))

    column = pl.BlockSpec((rows, LANES), lambda i, adapter, at: (0, i + first))
    table = pl.BlockSpec((rows, LANES), lambda i, adapter, at: (at[0], 0), pipeline_mode=pl.Buffered(1))
    return attend_back(
        24,
        peer_back_kernel,
        at,
        (own, own, gp, gp, cos, sin, dk, dv) + (peer,) * peers,
        [
            part(1), part(2),
            pl.BlockSpec((peers, rows + EXTRA, LANES), lambda i, adapter, at: (0, 0, i + first)),
            fixed((peers, EXTRA, width)),
            table, table, column, column,
        ]
        + [part(3 * p) for p in range(peers)],
        [jax.ShapeDtypeStruct((3, rows, width), BF16)],
        (2, 0),
        before,
        pairs,
        peers,
        [pltpu.VMEM((peers, HEADS, rows), F32), pltpu.VMEM((peers, HEADS, rows), F32)],
        2 * rows * width * 4 * 4 * rows * peers,
        "peer_back",
    )


def qkv_grad_kernel(_adapter, at, g, low, x, gain, shift, up, pieces, rank_grad):
    width = x.shape[1]
    low_t = low[...].T
    total = None
    def put(first, grad):
        for p in range(width // LANES):
            cut = slice(p * LANES, (p + 1) * LANES)
            pieces[(first + p) ^ (16 * at[1]), 0] = grad[:, cut].astype(BF16)

    for n in range(3):
        grad = g[(n + 2) % 3]
        put(n * (width // LANES), dot(low_t, grad))
        more = dot(grad, up[0, :, n * width : (n + 1) * width], NT)
        total = more if total is None else total + more
    rank = total.astype(BF16)
    rank_grad[...] = rank
    normed, _s = norm_rows(x[...].astype(F32))
    h1 = (normed * gain[...] + shift[...]).astype(BF16)
    put(3 * (width // LANES), dot(rank.T, h1))


def qkv_grad(at, g, low, x, gain, shift, up, groups):
    rows, width = x.shape
    return pl.pallas_call(
        qkv_grad_kernel,
        grid_spec=pltpu.PrefetchScalarGridSpec(
            num_scalar_prefetch=2,
            grid=(1,),
            in_specs=[
                whole((3, rows, width)),
                whole((rows, RANK)),
                whole((rows, width)),
                whole((1, width)),
                whole((1, width)),
                chosen((RANK, 3 * width)),
            ],
            out_specs=[whole((groups, 1, RANK, LANES)), whole((rows, RANK))],
        ),
        out_shape=[
            jax.ShapeDtypeStruct((groups, 1, RANK, LANES), BF16),
            jax.ShapeDtypeStruct((rows, RANK), BF16),
        ],
        compiler_params=params(16),
        cost_estimate=cost(2 * rows * 16 * 3 * width * 4, 8 * rows * width),
        name="qkv_grad",
    )(*at, g, low, x, gain, shift, up)


def input_grad_kernel(_adapter, at, g, w, rank_grad, down, x, gain, dx1, out, total):
    j = pl.program_id(0)
    rows = x.shape[0]

    @pl.when(j == 0)
    def _():
        total[...] = dot(rank_grad[...], down[0]) + dot(g[0], w[...], NT)

    @pl.when((j == 1) | (j == 2))
    def _():
        total[...] += dot(g[0], w[...], NT)

    @pl.when(j >= 3)
    def _():
        normed, spread = norm_rows(x[...].astype(F32))
        grad = total[pl.ds(pl.multiple_of((j - 3) * rows, rows), rows), :]
        out[...] = dx1[...] + norm_back(grad, normed, spread, gain[...])


def input_grad(at, g, w, rank_grad, down, x, gain, dx1):
    rows, width = x.shape
    cut = rows // 2
    part = pl.BlockSpec((cut, width), lambda j, adapter, at: (jnp.maximum(j - 3, 0), 0))
    order = lambda j: lax.rem(jnp.minimum(j, 2) + 1, 3)
    return pl.pallas_call(
        input_grad_kernel,
        grid_spec=pltpu.PrefetchScalarGridSpec(
            num_scalar_prefetch=2,
            grid=(3 + rows // cut,),
            in_specs=[
                pl.BlockSpec((1, rows, width), lambda j, adapter, at: (jnp.minimum(j, 2), 0, 0)),
                pl.BlockSpec((width, width), lambda j, adapter, at: (0, order(j))),
                fixed((rows, RANK)),
                chosen((RANK, width)),
                part,
                fixed((1, width)),
                part,
            ],
            out_specs=part,
            scratch_shapes=[pltpu.VMEM((rows, width), F32)],
        ),
        out_shape=jax.ShapeDtypeStruct((rows, width), F32),
        compiler_params=params(20),
        cost_estimate=cost(6 * rows * width * width, 6 * width * width + 16 * rows * width),
        name="input_grad",
    )(*at, g, w, rank_grad, down, x, gain, dx1)


def swap_order():
    bits = []
    n = 4
    while n < lax.axis_size("dp"):
        bits.append((n, 0))
        n *= 2
    n = 1
    while n < lax.axis_size("seq"):
        bits.append((0, n))
        n *= 2
    bits.append((2, 0))
    first = bits[:4]
    second = [first[1], first[0], first[3], first[2]]
    return (first, second), bits[4:]


def swap(values, step):
    size, ways = lax.axis_size("dp"), lax.axis_size("seq")
    perm = []
    for d in range(size):
        flip_d, flip_s = step[d & 1]
        for s in range(ways):
            perm.append((d * ways + s, (d ^ flip_d) * ways + (s ^ flip_s)))
    return lax.ppermute(values, ("dp", "seq"), perm)


def device_codes():
    orders, _rest = swap_order()
    size, ways = lax.axis_size("dp"), lax.axis_size("seq")
    table = np.zeros((size * ways, 6 + ways), np.int32)
    for d in range(size):
        for s in range(ways):
            codes = []
            for order in orders:
                on = [((d & bit_d) | (s & bit_s)) != 0 for bit_d, bit_s in order]
                codes.append(
                    (sum(8 >> n for n in range(4) if on[n]), sum(1 << n for n in range(4) if on[n]))
                )
            mine, theirs = codes[d & 1], codes[1 - (d & 1)]
            row = [s, d & 1, mine[0], theirs[0], mine[1], theirs[1]]
            table[d * ways + s] = row + [(s + n) % ways for n in range(1, ways)] + [0]
    place = lax.axis_index("dp") * ways + lax.axis_index("seq")
    return lax.dynamic_slice_in_dim(jnp.asarray(table), place, 1, 0)[0]


def slot_owners(index_all):
    orders, _rest = swap_order()
    masks = []
    for order in orders:
        slots = [0, 1]
        for bit_d, _s in order:
            slots = slots + [slot ^ bit_d for slot in slots]
        masks.append(np.array(slots, np.int32))
    d = lax.axis_index("dp")
    return index_all[d ^ jnp.where((d & 1) == 0, *masks)]


def scatter_steps():
    orders, _rest = swap_order()
    return [((1, 0), (1, 0))] + list(zip(*orders))


def scatter_stage(held, step):
    half = held.shape[1] // 2
    return jnp.concatenate([held[:, :half], swap(held[:, half:], step)], axis=0)


def owner_sum_kernel(owners, _at, held, out, total):
    total[...] = jnp.zeros_like(total)
    for n in range(held.shape[0]):
        total[owners[n]] += held[n].astype(F32)
    for a in range(NADAPT):
        out[:, a] = total[a].astype(BF16)


def owner_sum(owners, held):
    slots, groups, parts, rank, lanes = held.shape
    pieces = groups * parts
    held = held.reshape(slots, pieces, rank, lanes)
    step = min(pieces, 4)
    out = pl.pallas_call(
        owner_sum_kernel,
        grid_spec=pltpu.PrefetchScalarGridSpec(
            num_scalar_prefetch=2,
            grid=(pieces // step,),
            in_specs=[pl.BlockSpec((slots, step, rank, lanes), lambda i, *_: (0, i, 0, 0))],
            out_specs=pl.BlockSpec((step, NADAPT, rank, lanes), lambda i, *_: (i, 0, 0, 0)),
            scratch_shapes=[pltpu.VMEM((NADAPT, step, rank, lanes), F32)],
        ),
        out_shape=jax.ShapeDtypeStruct((pieces, NADAPT, rank, lanes), BF16),
        compiler_params=params(12),
        cost_estimate=cost(held.size, 2 * held.size),
        name="owner_sum",
    )(owners, owners, held)
    out = out.reshape(groups, parts, NADAPT, rank, lanes)
    _orders, rest = swap_order()
    for bits in rest:
        out = (out.astype(F32) + swap(out, (bits, bits)).astype(F32)).astype(BF16)
    return out


def spread_kernel(_adapter, at, mine, theirs, *outs, plan, straight):
    for core in range(2):

        @pl.when(at[1] == core)
        def _():
            for ref, part, first, count in zip(outs, *plan):
                for p in range(count):
                    piece = first + p
                    near = piece >> 4 == core
                    held = mine if near else theirs
                    if straight:
                        low = piece & 15
                    else:
                        low = int(f"{piece & 15:04b}"[::-1], 2) ^ (at[4] if near else at[5])
                    ref[:, :, p * LANES : (p + 1) * LANES] = held[low, part].astype(F32)


def spread(at, mine, theirs, plan, straight=False):
    parts, firsts, counts = plan
    shapes = [(NADAPT, RANK, count * LANES) for count in counts]
    return pl.pallas_call(
        functools.partial(spread_kernel, plan=plan, straight=straight),
        grid_spec=pltpu.PrefetchScalarGridSpec(
            num_scalar_prefetch=2,
            grid=(1,),
            in_specs=[whole(mine.shape), whole(theirs.shape)],
            out_specs=[whole(shape) for shape in shapes],
        ),
        out_shape=[jax.ShapeDtypeStruct(shape, F32) for shape in shapes],
        compiler_params=params(20),
        cost_estimate=cost(1, 12 * mine.size),
        name="spread",
    )(*at, mine, theirs)


def tie(*values):
    flat, tree = jax.tree.flatten(values)
    return jax.tree.unflatten(tree, lax.optimization_barrier(flat))


def body(
    clip_tokens, adapter_index, ln1_gain, ln1_bias, qkv_weight, qkv_bias, qkv_down, qkv_up,
    out_weight, out_bias, out_down, out_up, ln2_gain, ln2_bias, fc1_weight, fc1_bias, fc1_down,
    fc1_up, fc2_weight, fc2_bias, fc2_down, fc2_up, cotangent,
):
    _one, rows, width = clip_tokens.shape
    devices = lax.axis_size("seq")
    groups = 32
    pin = lambda v: pltpu.with_memory_space_constraint(v, pltpu.HBM)
    row = lambda v: pin(v.reshape(1, -1))
    x = pin(clip_tokens[0])
    cot = pin(cotangent[0])
    qkv_weight, qkv_down, qkv_up = pin(qkv_weight), pin(qkv_down), pin(qkv_up)
    out_weight, out_down, out_up = pin(out_weight), pin(out_down), pin(out_up)
    fc1_weight, fc1_down, fc1_up = pin(fc1_weight), pin(fc1_down), pin(fc1_up)
    fc2_weight, fc2_down, fc2_up = pin(fc2_weight), pin(fc2_down), pin(fc2_up)
    peers = range(1, devices)
    at = (adapter_index, device_codes())
    tagged = jnp.broadcast_to(adapter_index.astype(BF16)[:, None], (256, LANES))
    tags = lax.all_gather(lax.optimization_barrier(tagged), "dp", axis=0, tiled=True)
    index_all = lax.optimization_barrier(tags)[::256, 0].astype(jnp.int32)
    owners = slot_owners(index_all)

    def from_peer(values, shift):
        return lax.ppermute(values, "seq", [((n + shift) % devices, n) for n in range(devices)])

    tables = tuple(pin(jnp.asarray(t)) for t in rotary_tables(rows * devices))
    cos, sin = tables
    x_peer = jnp.concatenate([from_peer(clip_tokens[0], n) for n in peers], axis=0)
    first_set = (row(ln1_gain), row(ln1_bias), qkv_weight, row(qkv_bias), qkv_down, qkv_up)
    own, mixed, back, low_qkv, top, total, grad2 = front_rows(
        at, x, cot, first_set, tables, fc2_weight, fc2_down, fc2_up
    )
    peer, act, x1, low2, dx1, go, delta, lse, pieces_a = middle_rows(
        at, pin(x_peer), first_set, tables, own, (mixed, top, total), x, cot, back, grad2,
        (out_weight, row(out_bias), out_down, out_up),
        (row(ln2_gain), row(ln2_bias)),
        (fc1_weight, row(fc1_bias), fc1_down, fc1_up),
        fc2_down, groups,
    )
    own, peer = pin(own), pin(peer)
    go_sent, sent, delta = tie(go, pieces_a[None], delta)
    go_peer = jnp.stack([from_peer(go_sent, n) for n in peers])
    steps = scatter_steps()

    def halves(held):
        half = held.shape[1] // 2
        return held[:, :half], held[:, half:]

    def join(*parts):
        return jnp.concatenate(parts, axis=0)

    kept, sent = halves(sent)
    arrived = swap(sent, steps[0])
    kept, sent = halves(join(kept, arrived))
    sent, delta = tie(sent, delta)
    arrived = swap(sent, steps[1])
    grads = own_back(at, own, peer, go, lse, delta, cos, sin, (0, 4), None)
    arrived, grads, delta = tie(arrived, grads, delta)
    kept, sent = halves(join(kept, arrived))
    sent, delta = tie(sent, delta)
    arrived = swap(sent, steps[2])
    grads, dk, dv = own_back(at, own, peer, go, lse, delta, cos, sin, (4, 4), grads)
    arrived, dk, go_peer = tie(arrived, dk, go_peer)
    dk, dv = pin(dk), pin(dv)
    kept, sent = halves(join(kept, arrived))
    sent, go_peer = tie(sent, go_peer)
    arrived = swap(sent, steps[3])
    grads = peer_back(at, own, peer, go_peer, cos, sin, dk, dv, (0, 4), (grads,))[0]
    arrived, grads, go_peer = tie(arrived, grads, go_peer)
    kept, sent = halves(join(kept, arrived))
    sent, go_peer = tie(sent, go_peer)
    arrived = swap(sent, steps[4])
    grads = peer_back(at, own, peer, go_peer, cos, sin, dk, dv, (4, 4), (grads,))[0]
    arrived, grads = tie(arrived, grads)
    total_a = owner_sum(owners, join(kept, arrived))
    total_a, grads = tie(total_a, grads)
    arrived_a = swap(total_a, steps[1])
    pieces_b, rank_grad = qkv_grad(
        at, grads, low_qkv, x, row(ln1_gain), row(ln1_bias), qkv_up, groups
    )
    held, arrived_a = tie(scatter_stage(pieces_b[None], steps[0]), arrived_a)
    total_a = join(total_a, arrived_a)

    held, total_a, rank_grad = tie(held, total_a, rank_grad)
    arrived = swap(held, steps[1])
    arrived_a = swap(total_a, steps[2])
    grad_in = input_grad(at, grads, qkv_weight, rank_grad, qkv_down, x, row(ln1_gain), dx1)
    arrived, arrived_a, grad_in = tie(arrived, arrived_a, grad_in)
    held, total_a = join(held, arrived), join(total_a, arrived_a)
    held, total_a, low2 = tie(held, total_a, low2)
    arrived = swap(held, steps[2])
    arrived_a = swap(total_a, steps[3])
    block_output = output_rows(at, act, fc2_weight, x1, row(fc2_bias), low2, fc2_up)
    arrived, arrived_a, block_output = tie(arrived, arrived_a, block_output)
    held, total_a = join(held, arrived), join(total_a, arrived_a)
    held, total_a = tie(held, total_a)
    arrived = swap(held, steps[3])
    arrived_a = swap(total_a, steps[4])
    arrived, arrived_a = tie(arrived, arrived_a)
    held, total_a = join(held, arrived), join(total_a, arrived_a)
    held, total_a = tie(held, total_a)
    arrived = swap(held, steps[4])
    theirs_a = swap(total_a, steps[0])
    per = width // LANES
    spread_a = spread(
        at, total_a, theirs_a,
        ((0, 1, 2, 2, 2, 2), (0, 0, 0, per, 2 * per, 3 * per), (32, 32, per, per, per, per)),
    )
    arrived, spread_a = tie(arrived, spread_a)
    up1, down2, up2, down1, up_o, down_o = spread_a
    total_b = owner_sum(owners, join(held, arrived))
    up_qkv, down_qkv = spread(
        at, total_b, swap(total_b, steps[0]), ((0, 0), (0, 3 * per), (3 * per, per)), straight=True
    )
    return (
        block_output[None], grad_in[None], down_qkv, up_qkv, down_o, up_o, down1, up1, down2, up2,
    )


def solution(mesh):
    split = P("dp", "seq", None)
    return jax.shard_map(
        body,
        mesh=mesh,
        in_specs=(split, P("dp")) + (P(),) * 20 + (split,),
        out_specs=(split, split) + (P(),) * 8,
        check_vma=False,
    )
```

```python
import functools

import jax
import jax.numpy as jnp
import numpy as np
from jax import lax
from jax.experimental import pallas as pl
from jax.experimental.pallas import tpu as pltpu
from jax.sharding import PartitionSpec as P

HEADS = 16
HD = 64
GRID = 16
NADAPT = 8
RANK = 16
EPSILON = 1e-06
LANES = 128
EXTRA = 48

F32 = jnp.float32
BF16 = jnp.bfloat16
NN = (((1,), (0,)), ((), ()))
NT = (((1,), (1,)), ((), ()))

ERFC = (
    0.16918800211151383,
    0.1707152747822528,
    0.14833885959986734,
    0.21492717178376733,
    -0.09465313901935662,
    0.5477232747113128,
    -0.5122807406271995,
    0.48556441585520754,
    -0.1295231387829952,
)


def dot(a, b, dims=NN):
    return lax.dot_general(a, b, dims, preferred_element_type=F32)


def params(megabytes):
    return pltpu.CompilerParams(
        dimension_semantics=("arbitrary",), vmem_limit_bytes=megabytes << 20
    )


def cost(flops, moved, exps=0):
    return pl.CostEstimate(flops=int(flops), bytes_accessed=int(moved), transcendentals=int(exps))


def norm_rows(values):
    centre = values - jnp.mean(values, axis=-1, keepdims=True)
    spread = lax.rsqrt(jnp.mean(centre * centre, axis=-1, keepdims=True) + EPSILON)
    return centre * spread, spread


def norm_back(grad_rows, normed, spread, gain):
    scaled = grad_rows * gain
    first = jnp.mean(scaled, axis=-1, keepdims=True)
    second = jnp.mean(scaled * normed, axis=-1, keepdims=True)
    return spread * (scaled - first - normed * second)


def rotary_tables(length):
    half = HD // 2
    side = half // 3
    lead = half - 2 * side
    token = np.arange(length)
    pair = np.arange(half)
    kind = np.where(pair < lead, 0, np.where(pair < lead + side, 1, 2))
    local = np.where(kind == 0, pair, np.where(kind == 1, pair - lead, pair - lead - side))
    total = np.where(kind == 0, lead, side)
    frequency = np.power(
        np.float32(10000.0), -local.astype(np.float32) / total.astype(np.float32)
    ).astype(np.float32)
    place = np.where(
        kind[None] == 0,
        (token // (GRID * GRID))[:, None],
        np.where(kind[None] == 1, (token // GRID % GRID)[:, None], (token % GRID)[:, None]),
    ).astype(np.float32)
    angle = place * frequency[None]
    cosine, sine = np.cos(angle), np.sin(angle)
    cos_rows = np.concatenate([cosine] * 4, axis=1).astype(np.float32)
    sin_rows = np.concatenate([-sine, sine, -sine, sine], axis=1).astype(np.float32)
    return cos_rows, sin_rows


def swap_halves(values):
    lane = lax.broadcasted_iota(jnp.int32, (1, LANES), 1)
    low = (lane & (HD // 2)) == 0
    return jnp.where(
        low, pltpu.roll(values, LANES - HD // 2, 1), pltpu.roll(values, HD // 2, 1)
    )


def head_mask(values, head):
    lane = lax.broadcasted_iota(jnp.int32, (1, LANES), 1)
    keep = (lane < HD) if head == 0 else (lane >= HD)
    return jnp.where(keep, values, jnp.zeros_like(values))


def whole(shape):
    return pl.BlockSpec(shape, lambda *_: (0,) * len(shape))


def fixed(shape):
    return pl.BlockSpec(shape, lambda *_: (0,) * len(shape), pipeline_mode=pl.Buffered(1))


def chosen(shape):
    return pl.BlockSpec((1,) + shape, lambda *ids: (ids[-2][0], 0, 0))


def chosen_tile(tile, which):
    return pl.BlockSpec((1, RANK, tile), lambda j, adapter, at: (adapter[0], 0, which(j)))


def position(piece, at, first=2):
    top = (piece >> 4) ^ at[1]
    return 16 * top + ((piece & 15) ^ jnp.where(top == 0, at[first], at[first + 1]))


CHUNK = 256


def qkv_tile(tile, h1, low, w, bias, up, cos, sin, out_ref, keep, first):
    scale = jnp.where(tile == 0, HD**-0.5, 1.0).astype(F32)
    turn = jnp.where(tile == 2, 0.0, 1.0).astype(F32)
    c = (cos[...] * turn + (1.0 - turn)) * scale
    s = sin[...] * (turn * scale)

    def chunk(n):
        cut = slice(n * CHUNK, (n + 1) * CHUNK)
        return dot(h1, w[:, cut]) + bias[:, cut] + dot(low, up[:, cut])

    count = w.shape[1] // CHUNK
    now = chunk(0)
    parts = []
    for n in range(count):
        later = chunk(n + 1) if n + 1 < count else None
        for g in range(CHUNK // LANES):
            part = now[:, g * LANES : (g + 1) * LANES]
            parts.append((part * c + swap_halves(part) * s).astype(BF16))
        now = later
    for n, part in enumerate(parts):
        out_ref[n] = part
        keep[first + n] = part


def attend_pairs(count, load, finish):
    loaded = [load(pair) for pair in range(count)]
    values_t = [v.T for _q, _k, v in loaded]

    def scores(item):
        pair, head = item
        q, k, _v = loaded[pair]
        return dot(k, head_mask(q, head), NT)

    items = [(pair, head) for pair in range(count) for head in range(2)]
    now = scores(items[0])
    for n, (pair, head) in enumerate(items):
        later = scores(items[n + 1]) if n + 1 < len(items) else None
        finish(pair, head, now, values_t[pair][head * HD : (head + 1) * HD])
        now = later


STEP_PAIRS = 2


def start_all(*groups):
    for group in groups:
        for copy in group:
            copy.start()


def wait_all(*groups):
    for group in groups:
        for copy in group:
            copy.wait()


def group(sems, pairs):
    return [pltpu.make_async_copy(a, b, sems.at[n]) for n, (a, b) in enumerate(pairs)]


def tiles(source, kept, size):
    return [(source.at[:, pl.ds(n * size, size)], kept.at[n]) for n in range(kept.shape[0])]


def front_kernel(
    adapter, at, x, w, w2,
    gain, shift, bias, down, up, cos, sin, cot, down2, up2,
    qkv, mixed_out, back, low, top_out, total_out, grad2,
    h1, keep, gain_k, shift_k, bias_k, down_k, up_k, cos_k, sin_k, cot_k, down2_k, up2_k,
    low_k, top_k, total_k, grad2_k, sem_a, sem_b, sem_c, sem_d,
    *, starts,
):
    j = pl.program_id(0)
    second, third = starts
    last = pl.num_programs(0) - 1
    mine = adapter[0]
    rows, width = x.shape
    place = pl.ds(pl.multiple_of(at[0] * rows, rows), rows)
    early = group(
        sem_a,
        [
            (gain, gain_k), (shift, shift_k), (down.at[mine], down_k),
            (cos.at[place], cos_k), (sin.at[place], sin_k),
        ]
        + tiles(bias, bias_k, width)
        + tiles(up.at[mine], up_k, width),
    )
    late = group(
        sem_b, [(cot, cot_k), (up2.at[mine], up2_k)] + tiles(down2.at[mine], down2_k, w2.shape[0])
    )
    stats = group(sem_c, [(low_k, low), (top_k, top_out), (total_k, total_out)])
    end = group(sem_d, [(grad2_k, grad2)])

    @pl.when(j == 0)
    def _():
        start_all(early, late)
        normed, _s = norm_rows(x[...].astype(F32))
        wait_all(early)
        held = (normed * gain_k[...] + shift_k[...]).astype(BF16)
        h1[...] = held
        low_k[...] = dot(held, down_k[...], NT).astype(BF16)

    @pl.when(j < second)
    def _():
        qkv_tile(j, h1[...], low_k[...], w, bias_k[j], up_k[j], cos_k, sin_k, qkv, keep, 8 * j)

    @pl.when((j >= second) & (j < third))
    def _():
        first = (j - second) * STEP_PAIRS

        def load(pair):
            return keep[first + pair], keep[8 + first + pair], keep[16 + first + pair]

        def finish(pair, head, scores, values_t):
            top = jnp.max(scores, axis=0, keepdims=True)
            weights = jnp.exp(scores - top)
            start = pair * LANES + head * HD
            mixed_out[start : start + HD, :] = dot(values_t, weights.astype(BF16))
            top_k[first + pair, head : head + 1, :] = top
            total_k[first + pair, head : head + 1, :] = jnp.sum(weights, axis=0, keepdims=True)

        attend_pairs(STEP_PAIRS, load, finish)

    @pl.when(j == third)
    def _():
        start_all(stats)
        wait_all(late)
        grad2_k[...] = dot(cot_k[...], up2_k[...], NT).astype(BF16)
        start_all(end)

    @pl.when(j >= third)
    def _():
        side = dot(grad2_k[...], down2_k[j - third])
        back[...] = (dot(cot_k[...], w2[...], NT) + side).astype(BF16)

    @pl.when(j == last)
    def _():
        wait_all(stats, end)


def clip(value, low, high):
    return jnp.minimum(jnp.maximum(value, low), high)


ANY = pl.BlockSpec(memory_space=pl.ANY)


def front_rows(at, x, cot, first_set, tables, w2, down2, up2):
    gain, shift, w, bias, down, up = first_set
    rows, width = x.shape
    ff = w2.shape[0]
    tile = 1024
    second = w.shape[1] // width
    third = second + HEADS // 2 // STEP_PAIRS
    steps = third + ff // tile
    one = lambda j: jnp.minimum(j, second - 1)
    two = lambda j: clip(j - second, 0, third - second - 1)
    three = lambda j: clip(j - third, 0, steps - third - 1)
    stat = (HEADS // 2, 2, rows)
    return pl.pallas_call(
        functools.partial(front_kernel, starts=(second, third)),
        grid_spec=pltpu.PrefetchScalarGridSpec(
            num_scalar_prefetch=2,
            grid=(steps,),
            in_specs=[
                fixed((rows, width)),
                pl.BlockSpec((width, width), lambda j, adapter, at: (0, one(j))),
                pl.BlockSpec((tile, width), lambda j, adapter, at: (three(j), 0)),
            ]
            + [ANY] * 10,
            out_specs=[
                pl.BlockSpec((8, rows, LANES), lambda j, adapter, at: (one(j), 0, 0)),
                pl.BlockSpec((STEP_PAIRS * LANES, rows), lambda j, adapter, at: (two(j), 0)),
                pl.BlockSpec((rows, tile), lambda j, adapter, at: (0, three(j))),
            ]
            + [ANY] * 4,
            scratch_shapes=[
                pltpu.VMEM((rows, width), BF16),
                pltpu.VMEM((24, rows, LANES), BF16),
                pltpu.VMEM((1, width), F32),
                pltpu.VMEM((1, width), F32),
                pltpu.VMEM((second, 1, width), F32),
                pltpu.VMEM((RANK, width), BF16),
                pltpu.VMEM((second, RANK, width), BF16),
                pltpu.VMEM((rows, LANES), F32),
                pltpu.VMEM((rows, LANES), F32),
                pltpu.VMEM((rows, width), BF16),
                pltpu.VMEM((ff // tile, RANK, tile), BF16),
                pltpu.VMEM((RANK, width), BF16),
                pltpu.VMEM((rows, RANK), BF16),
                pltpu.VMEM(stat, F32),
                pltpu.VMEM(stat, F32),
                pltpu.VMEM((rows, RANK), BF16),
                pltpu.SemaphoreType.DMA((5 + 2 * second,)),
                pltpu.SemaphoreType.DMA((2 + ff // tile,)),
                pltpu.SemaphoreType.DMA((3,)),
                pltpu.SemaphoreType.DMA((1,)),
            ],
        ),
        out_shape=[
            pltpu.HBM((24, rows, LANES), BF16),
            pltpu.HBM((width, rows), F32),
            pltpu.HBM((rows, ff), BF16),
            pltpu.HBM((rows, RANK), BF16),
            pltpu.HBM(stat, F32),
            pltpu.HBM(stat, F32),
            pltpu.HBM((rows, RANK), BF16),
        ],
        compiler_params=params(44),
        cost_estimate=cost(
            2 * rows * width * (3 * width + ff) + 16 * rows * rows * width, 20 << 20, 16 * rows * rows
        ),
        name="front_rows",
    )(*at, x, w, w2, gain, shift, bias, down, up, *tables, cot, down2, up2)


def gelu_both(f):
    z = jnp.abs(f) * (0.5**0.5)
    t = 1.0 / (1.0 + 0.3 * z)
    poly = ERFC[-1]
    for c in ERFC[-2::-1]:
        poly = poly * t + c
    bell = jnp.exp(f * f * -0.5)
    tail = (0.5 * poly) * t * bell
    phi = jnp.where(f < 0, tail, 1.0 - tail)
    return f * phi, phi + f * (bell * 0.3989422804014327)


def middle_kernel(
    adapter, at, xp, wq, w1, back,
    gain1, shift1, bq, downq, upq, cos, sin, own, mixed, top, total,
    x, cot, grad2, w_out, b_out, out_down, out_up, gain, shift, b1, down1, up1, down2,
    qkv, act_out, x1_out, low2_out, dx1_out, go_out, delta_out, lse_out, pieces_out,
    h1, lowq, keep, o, h2, dh2, low_o, low1, low1_t, grad2_t, low2, grad1,
    gain1_k, shift1_k, bq_k, downq_k, upq_k, cos_k, sin_k, q_own, mixed_in, top_in, total_in,
    x_k, cot_k, grad2_k, w_out_k, b_out_k, out_down_k, out_up_k, gain_k, shift_k, b1_k, down1_k, up1_k, down2_k,
    x1, low2_k, dx1_k, go, delta_k, lse, pieces,
    sem_a, sem_b, sem_c, sem_d, sem_e,
    *, starts, peers,
):
    j = pl.program_id(0)
    second, third = starts
    last = pl.num_programs(0) - 1
    rows, width = xp.shape
    tile = w1.shape[1]
    mine = adapter[0]
    places = [pl.ds(pl.multiple_of(at[9 + p] * rows, rows), rows) for p in range(peers)]
    early = group(
        sem_a,
        [(gain1, gain1_k), (shift1, shift1_k), (downq.at[mine], downq_k)]
        + [(cos.at[places[p]], cos_k.at[p]) for p in range(peers)]
        + [(sin.at[places[p]], sin_k.at[p]) for p in range(peers)]
        + tiles(bq, bq_k, width)
        + tiles(upq.at[mine], upq_k, width),
    )
    later = group(
        sem_b, [(own.at[pl.ds(0, 8)], q_own), (mixed, mixed_in), (top, top_in), (total, total_in)]
    )
    late = group(
        sem_c,
        [
            (x, x_k), (cot, cot_k), (grad2, grad2_k), (w_out, w_out_k), (b_out, b_out_k),
            (out_down.at[mine], out_down_k), (out_up.at[mine], out_up_k), (gain, gain_k),
            (shift, shift_k), (down1.at[mine], down1_k),
        ]
        + tiles(b1, b1_k, tile)
        + tiles(up1.at[mine], up1_k, tile)
        + tiles(down2.at[mine], down2_k, tile),
    )
    middle_out = group(sem_d, [(x1, x1_out), (lse, lse_out)])
    end = group(
        sem_e,
        [(low2_k, low2_out), (dx1_k, dx1_out), (go, go_out), (delta_k, delta_out), (pieces, pieces_out)],
    )

    @pl.when(j == 0)
    def _():
        start_all(early, later, late)

    @pl.when(j < second)
    def _():
        which, p = j // peers, lax.rem(j, peers)

        @pl.when(which == 0)
        def _():
            normed, _s = norm_rows(xp[...].astype(F32))

            @pl.when(j == 0)
            def _():
                wait_all(early)

            normed = (normed * gain1_k[...] + shift1_k[...]).astype(BF16)
            h1[p] = normed
            lowq[p] = dot(normed, downq_k[...], NT).astype(BF16)

        qkv_tile(
            which, h1[p], lowq[p], wq, bq_k[which], upq_k[which], cos_k.at[p], sin_k.at[p],
            qkv, keep, 24 * p + 8 * which,
        )

    @pl.when(j == second)
    def _():
        wait_all(later)

    @pl.when((j >= second) & (j < third))
    def _():
        first = (j - second) * STEP_PAIRS
        held = []

        def load(pair):
            n = first + pair
            k = [keep[24 * p + 8 + n] for p in range(peers)]
            v = [keep[24 * p + 16 + n] for p in range(peers)]
            if peers > 1:
                k, v = [jnp.concatenate(k, axis=0)], [jnp.concatenate(v, axis=0)]
            return q_own[n], k[0], v[0]

        def finish(pair, head, scores, values_t):
            n = first + pair
            before = top_in[n, head : head + 1, :]
            top = jnp.maximum(jnp.max(scores, axis=0, keepdims=True), before)
            scale = jnp.exp(before - top)
            weights = jnp.exp(scores - top)
            total = jnp.sum(weights, axis=0, keepdims=True)
            total = total + scale * total_in[n, head : head + 1, :]
            start = pl.ds(pl.multiple_of(n * LANES + head * HD, HD), HD)
            mixed = dot(values_t, weights.astype(BF16)) + scale * mixed_in[start, :]
            held.append(mixed * (1.0 / total))
            lse[n, head : head + 1, :] = top + jnp.log(total)
            if head == 1:
                o[n] = jnp.concatenate(held[-2:], axis=0).T.astype(BF16)

        attend_pairs(STEP_PAIRS, load, finish)

    def put(first, slot, grad):
        for p in range(grad.shape[1] // LANES):
            cut = slice(p * LANES, (p + 1) * LANES)
            pieces[position(first + p, at), slot] = grad[:, cut].astype(BF16)

    @pl.when(j == third)
    def _():
        wait_all(late)
        mixed = jnp.concatenate([o[n] for n in range(HEADS // 2)], axis=1)
        low = dot(mixed, out_down_k[...], NT).astype(BF16)
        low_o[...] = low
        branch = dot(mixed, w_out_k[...]) + b_out_k[...] + dot(low, out_up_k[...])
        mid = x_k[...].astype(F32) + branch
        x1[...] = mid
        normed, _s = norm_rows(mid)
        rows2 = (normed * gain_k[...] + shift_k[...]).astype(BF16)
        h2[...] = rows2
        low_1 = dot(rows2, down1_k[...], NT).astype(BF16)
        low1[...] = low_1
        low1_t[...] = low_1.T
        grad2_t[...] = grad2_k[...].T
        dh2[...] = jnp.zeros_like(dh2)
        low2[...] = jnp.zeros_like(low2)
        grad1[...] = jnp.zeros_like(grad1)
        start_all(middle_out)

    @pl.when(j >= third)
    def _():
        n_tile = j - third

        def hidden(n):
            cut = slice(n * CHUNK, (n + 1) * CHUNK)
            return dot(h2[...], w1[:, cut]) + b1_k[n_tile, :, cut] + dot(low1[...], up1_k[n_tile, :, cut])

        first = n_tile * (tile // LANES)
        count = tile // CHUNK
        now = hidden(0)
        acts, dfs = [], []
        for n in range(count):
            later = hidden(n + 1) if n + 1 < count else None
            cut = slice(n * CHUNK, (n + 1) * CHUNK)
            act, slope = gelu_both(now)
            acts.append(act.astype(BF16))
            dfs.append((back[:, cut].astype(F32) * slope).astype(BF16))
            now = later
        act, df = jnp.concatenate(acts, axis=1), jnp.concatenate(dfs, axis=1)
        dh2[...] += dot(df, w1[...], NT)
        low2[...] += dot(act, down2_k[n_tile], NT)
        grad1[...] += dot(df, up1_k[n_tile], NT)
        act_out[...] = act
        put(first, 0, dot(low1_t[...], df))
        put(first, 1, dot(grad2_t[...], act))

    @pl.when(j == last)
    def _():
        low_2 = low2[...].astype(BF16)
        low2_k[...] = low_2
        g1 = grad1[...].astype(BF16)
        back2 = dh2[...] + dot(g1, down1_k[...])
        normed, spread = norm_rows(x1[...])
        dx1 = cot_k[...].astype(F32) + norm_back(back2, normed, spread, gain_k[...])
        dx1_k[...] = dx1
        da = dx1.astype(BF16)
        g_o = dot(da, out_up_k[...], NT).astype(BF16)
        new_go = (dot(da, w_out_k[...], NT) + dot(g_o, out_down_k[...])).astype(BF16)
        go[EXTRA : EXTRA + rows, :] = new_go
        mixed = jnp.concatenate([o[n] for n in range(HEADS // 2)], axis=1)
        product = new_go.astype(F32) * mixed.astype(F32)
        high = product.astype(BF16)
        rest = (product - high.astype(F32)).astype(BF16)
        lane = lax.broadcasted_iota(jnp.int32, (HEADS, width), 1)
        head = lax.broadcasted_iota(jnp.int32, (HEADS, width), 0)
        pick = (lane // HD == head).astype(BF16)
        delta = dot(pick, high, NT) + dot(pick, rest, NT)
        delta_k[...] = delta
        if rows < width // 2:
            go[0:EXTRA, :] = jnp.zeros((EXTRA, width), BF16)
        logs = jnp.concatenate([lse[n] for n in range(HEADS // 2)], axis=0)
        for side, stat in enumerate((logs, delta)):
            left = stat
            for n in range(3):
                part = left.astype(BF16)
                go[16 * n : 16 * n + 16, side * (width // 2) : side * (width // 2) + rows] = part
                left = left - part.astype(F32)
        start_all(end[:4])
        per = width // LANES
        put(jnp.int32(0), 2, dot(low_2.T, cot_k[...]))
        put(jnp.int32(per), 2, dot(g1.T, h2[...]))
        put(jnp.int32(2 * per), 2, dot(low_o[...].T, da))
        put(jnp.int32(3 * per), 2, dot(g_o.T, mixed))
        start_all(end[4:])
        wait_all(middle_out, end)


def middle_rows(
    at, xp, first_set, tables, own, state, x, cot, back, grad2, out_set, norm_set, fc1_set, down2, groups
):
    rows, width = x.shape
    peers = xp.shape[0] // rows
    w1 = fc1_set[0]
    ff = w1.shape[1]
    tile = 1024
    second = 3 * peers
    third = second + HEADS // 2 // STEP_PAIRS
    steps = third + ff // tile
    one = lambda j: jnp.minimum(j, second - 1) // peers
    peer = lambda j: lax.rem(jnp.minimum(j, second - 1), peers)
    two = lambda j: clip(j - second, 0, third - second - 1)
    three = lambda j: clip(j - third, 0, steps - third - 1)
    stat = (HEADS // 2, 2, rows)
    count = ff // tile
    vmem = pltpu.VMEM
    return pl.pallas_call(
        functools.partial(middle_kernel, starts=(second, third), peers=peers),
        grid_spec=pltpu.PrefetchScalarGridSpec(
            num_scalar_prefetch=2,
            grid=(steps,),
            in_specs=[
                pl.BlockSpec((rows, width), lambda j, adapter, at: (jnp.minimum(j, peers - 1), 0)),
                pl.BlockSpec((width, width), lambda j, adapter, at: (0, one(j))),
                pl.BlockSpec((width, tile), lambda j, adapter, at: (0, three(j))),
                pl.BlockSpec((rows, tile), lambda j, adapter, at: (0, three(j))),
            ]
            + [ANY] * 24,
            out_specs=[
                pl.BlockSpec((8, rows, LANES), lambda j, adapter, at: (3 * peer(j) + one(j), 0, 0)),
                pl.BlockSpec((rows, tile), lambda j, adapter, at: (0, three(j))),
            ]
            + [ANY] * 7,
            scratch_shapes=[
                vmem((peers, rows, width), BF16),
                vmem((peers, rows, RANK), BF16),
                vmem((24 * peers, rows, LANES), BF16),
                vmem((HEADS // 2, rows, LANES), BF16),
                vmem((rows, width), BF16),
                vmem((rows, width), F32),
                vmem((rows, RANK), BF16),
                vmem((rows, RANK), BF16),
                vmem((RANK, rows), BF16),
                vmem((RANK, rows), BF16),
                vmem((rows, RANK), F32),
                vmem((rows, RANK), F32),
                vmem((1, width), F32),
                vmem((1, width), F32),
                vmem((3, 1, width), F32),
                vmem((RANK, width), BF16),
                vmem((3, RANK, width), BF16),
                vmem((peers, rows, LANES), F32),
                vmem((peers, rows, LANES), F32),
                vmem((8, rows, LANES), BF16),
                vmem((width, rows), F32),
                vmem(stat, F32),
                vmem(stat, F32),
                vmem((rows, width), BF16),
                vmem((rows, width), BF16),
                vmem((rows, RANK), BF16),
                vmem((width, width), BF16),
                vmem((1, width), F32),
                vmem((RANK, width), BF16),
                vmem((RANK, width), BF16),
                vmem((1, width), F32),
                vmem((1, width), F32),
                vmem((count, 1, tile), F32),
                vmem((RANK, width), BF16),
                vmem((count, RANK, tile), BF16),
                vmem((count, RANK, tile), BF16),
                vmem((rows, width), F32),
                vmem((rows, RANK), BF16),
                vmem((rows, width), F32),
                vmem((EXTRA + rows, width), BF16),
                vmem((HEADS, rows), F32),
                vmem(stat, F32),
                vmem((groups, 3, RANK, LANES), BF16),
                pltpu.SemaphoreType.DMA((9 + 2 * peers,)),
                pltpu.SemaphoreType.DMA((4,)),
                pltpu.SemaphoreType.DMA((10 + 3 * count,)),
                pltpu.SemaphoreType.DMA((2,)),
                pltpu.SemaphoreType.DMA((5,)),
            ],
        ),
        out_shape=[
            pltpu.HBM((24 * peers, rows, LANES), BF16),
            pltpu.HBM((rows, ff), BF16),
            pltpu.HBM((rows, width), F32),
            pltpu.HBM((rows, RANK), BF16),
            pltpu.HBM((rows, width), F32),
            pltpu.HBM((EXTRA + rows, width), BF16),
            pltpu.HBM((HEADS, rows), F32),
            pltpu.HBM(stat, F32),
            pltpu.HBM((groups, 3, RANK, LANES), BF16),
        ],
        compiler_params=params(60),
        cost_estimate=cost(
            4 * rows * width * ff + (4 + 6 * peers) * rows * width * width, 40 << 20, rows * ff
        ),
        name="middle_rows",
    )(
        *at, xp, first_set[2], w1, back,
        first_set[0], first_set[1], first_set[3], first_set[4], first_set[5], *tables, own, *state,
        x, cot, grad2, *out_set, *norm_set, *fc1_set[1:], down2,
    )


def output_kernel(_adapter, at, act, w2, x1, b2, low2, up2, *refs):
    out, y = refs[-2:]
    j = pl.program_id(0)
    last = pl.num_programs(0) - 1

    @pl.when(j == 0)
    def _():
        y[...] = dot(act[...], w2[...])

    @pl.when((j > 0) & (j < last))
    def _():
        y[...] += dot(act[...], w2[...])

    @pl.when(j == last)
    def _():
        side = b2[...] + dot(low2[...], up2[0])
        out[...] = (x1[...] + (y[...] + dot(act[...], w2[...]) + side)).astype(BF16)


def output_rows(at, act, w2, x1, b2, low2, up2, half, before=()):
    rows, ff = act.shape
    width = x1.shape[1]
    wide = width // 2
    tile = 1024
    part = pl.BlockSpec((rows, wide), lambda j, adapter, at: (0, half))
    return pl.pallas_call(
        output_kernel,
        grid_spec=pltpu.PrefetchScalarGridSpec(
            num_scalar_prefetch=2,
            grid=(ff // tile,),
            in_specs=[
                pl.BlockSpec((rows, tile), lambda j, adapter, at: (0, j)),
                pl.BlockSpec((tile, wide), lambda j, adapter, at: (j, half)),
                part,
                pl.BlockSpec((1, wide), lambda j, adapter, at: (0, half)),
                fixed((rows, RANK)),
                pl.BlockSpec((1, RANK, wide), lambda j, adapter, at: (adapter[0], 0, half)),
            ]
            + [ANY] * len(before),
            out_specs=part,
            scratch_shapes=[pltpu.VMEM((rows, wide), F32)],
        ),
        out_shape=jax.ShapeDtypeStruct((rows, width), BF16),
        input_output_aliases={8 + n: n for n in range(len(before))},
        compiler_params=params(24),
        cost_estimate=cost(rows * width * ff, width * ff + 2 * rows * ff),
        name="output_rows",
    )(*at, act, w2, x1, b2, low2, up2, *before)


def unrotate(values, cos, sin):
    return values * cos[...] - swap_halves(values) * sin[...]


def score_grads(s, dp, lse, delta):
    prob = jnp.exp(s - lse)
    return prob.astype(BF16), (prob * (dp - delta)).astype(BF16)


def own_back_kernel(_adapter, at, q0, k0, v0, go, lse0, delta0, cos, sin, *refs, first_pair, peers):
    k1, v1 = refs[:peers], refs[peers : 2 * peers]
    dq, dk, dv = refs[-3:]
    i = pl.program_id(0) + first_pair
    rows = q0.shape[1]
    keys = jnp.concatenate([k0[0]] + [k[0] for k in k1], axis=0)
    values = jnp.concatenate([v0[0]] + [v[0] for v in v1], axis=0)
    keys_t = keys.T

    def first(head):
        q = head_mask(q0[0], head)
        g = head_mask(go[EXTRA : EXTRA + rows, :], head)
        return dot(keys, q, NT), dot(values, g, NT), q, g

    grad_q = []
    now = first(0)
    for head in range(2):
        later = first(1) if head == 0 else None
        s, dp, q, g = now
        row = pl.ds(2 * i + head, 1)
        prob, ds = score_grads(s, dp, lse0[i, head : head + 1, :], delta0[row, :])
        grad_q.append(dot(keys_t[head * HD : (head + 1) * HD], ds))
        more_v = dot(prob[:rows], g)
        more_k = dot(ds[:rows], q)
        if head == 0:
            dv[...] = more_v
            dk[...] = more_k
        else:
            dv[...] += more_v
            dk[...] += more_k
        now = later
    dq[0] = unrotate(jnp.concatenate(grad_q, axis=0).T * (HD**-0.5), cos, sin).astype(BF16)


def peer_back_kernel(_adapter, at, k0, v0, gp, stats, cos, sin, dk_in, dv_in, *refs, first_pair, peers):
    q1 = refs[:peers]
    out, lse1, delta1 = refs[-3:]
    i = pl.program_id(0) + first_pair
    rows = k0.shape[1]
    half = stats.shape[2] // 2

    @pl.when(i == first_pair)
    def _():
        for n in range(peers):
            for side, ref in enumerate((lse1, delta1)):
                cut = slice(side * half, side * half + rows)
                ref[n] = (
                    stats[n, 0:16, cut].astype(F32)
                    + stats[n, 16:32, cut].astype(F32)
                    + stats[n, 32:48, cut].astype(F32)
                )

    def first(item):
        head, peer = item
        q = head_mask(q1[peer][0], head)
        g = head_mask(gp[peer, EXTRA : EXTRA + rows, :], head)
        return dot(k0[0], q, NT), dot(v0[0], g, NT), q, g

    items = [(head, peer) for peer in range(peers) for head in range(2)]
    grad_k, grad_v = dk_in[...], dv_in[...]
    now = first(items[0])
    for n, (head, peer) in enumerate(items):
        later = first(items[n + 1]) if n + 1 < len(items) else None
        s, dp, q, g = now
        row = pl.ds(2 * i + head, 1)
        prob, ds = score_grads(s, dp, lse1[peer, row, :], delta1[peer, row, :])
        grad_v = grad_v + dot(prob, g)
        grad_k = grad_k + dot(ds, q)
        now = later
    out[0] = unrotate(grad_k, cos, sin).astype(BF16)
    out[1] = grad_v.astype(BF16)


def attend_back(limit, kernel, at, args, specs, outs, blocks, before, pairs, peers, scratch, flops, name):
    first, count = pairs
    before = () if before is None else tuple(before)
    steps = HEADS // 2
    return pl.pallas_call(
        functools.partial(kernel, first_pair=first, peers=peers),
        grid_spec=pltpu.PrefetchScalarGridSpec(
            num_scalar_prefetch=2,
            grid=(count,),
            in_specs=specs + [pl.BlockSpec(memory_space=pl.ANY)] * len(before),
            out_specs=[pl.BlockSpec((blocks[0], outs[0].shape[1], LANES), lambda i, adapter, at: (blocks[1], 0, i + first))]
            + [pl.BlockSpec((o.shape[0], LANES), lambda i, adapter, at: (0, i + first)) for o in outs[1:]],
            scratch_shapes=scratch,
        ),
        out_shape=outs,
        input_output_aliases={2 + len(args) + n: n for n in range(len(before))},
        compiler_params=params(limit),
        cost_estimate=cost(
            flops * count // steps,
            4 * sum(a.size for a in args[:4]) * count // steps,
            flops * count // steps // 512,
        ),
        name=name,
    )(*at, *args, *before)


def own_back(at, own, peer, go, lse, delta, cos, sin, pairs, before):
    rows = own.shape[1]
    peers = peer.shape[0] // 24
    width = own.shape[0] // 3 * LANES
    first = pairs[0]

    def part(which):
        return pl.BlockSpec((1, rows, LANES), lambda i, adapter, at: (8 * which + first + i, 0, 0))

    table = pl.BlockSpec((rows, LANES), lambda i, adapter, at: (at[0], 0), pipeline_mode=pl.Buffered(1))
    return attend_back(
        24,
        own_back_kernel,
        at,
        (own, own, own, go, lse, delta, cos, sin) + (peer,) * (2 * peers),
        [part(0), part(1), part(2)]
        + [pl.BlockSpec((rows + EXTRA, LANES), lambda i, adapter, at: (0, i + first))]
        + [fixed((HEADS // 2, 2, rows)), fixed((HEADS, rows)), table, table]
        + [part(3 * p + 1) for p in range(peers)]
        + [part(3 * p + 2) for p in range(peers)],
        [jax.ShapeDtypeStruct((3, rows, width), BF16)] + [pltpu.HBM((rows, width), F32)] * 2,
        (1, 2),
        before,
        pairs,
        peers,
        [],
        2 * rows * width * 4 * rows * (5 + 3 * peers),
        "own_back",
    )


def peer_back(at, own, peer, gp, cos, sin, dk, dv, pairs, before):
    rows = own.shape[1]
    peers = gp.shape[0]
    width = own.shape[0] // 3 * LANES
    first = pairs[0]

    def part(which):
        return pl.BlockSpec((1, rows, LANES), lambda i, adapter, at: (8 * which + first + i, 0, 0))

    column = pl.BlockSpec((rows, LANES), lambda i, adapter, at: (0, i + first))
    table = pl.BlockSpec((rows, LANES), lambda i, adapter, at: (at[0], 0), pipeline_mode=pl.Buffered(1))
    return attend_back(
        24,
        peer_back_kernel,
        at,
        (own, own, gp, gp, cos, sin, dk, dv) + (peer,) * peers,
        [
            part(1), part(2),
            pl.BlockSpec((peers, rows + EXTRA, LANES), lambda i, adapter, at: (0, 0, i + first)),
            fixed((peers, EXTRA, width)),
            table, table, column, column,
        ]
        + [part(3 * p) for p in range(peers)],
        [jax.ShapeDtypeStruct((3, rows, width), BF16)],
        (2, 0),
        before,
        pairs,
        peers,
        [pltpu.VMEM((peers, HEADS, rows), F32), pltpu.VMEM((peers, HEADS, rows), F32)],
        2 * rows * width * 4 * 4 * rows * peers,
        "peer_back",
    )


def qkv_grad_kernel(_adapter, at, g, low, x, gain, shift, up, pieces, rank_grad):
    width = x.shape[1]
    low_t = low[...].T
    total = None
    def put(first, grad):
        for p in range(width // LANES):
            cut = slice(p * LANES, (p + 1) * LANES)
            pieces[position(jnp.int32(first + p), at, 6), 0] = grad[:, cut].astype(BF16)

    for n in range(3):
        grad = g[(n + 2) % 3]
        put(n * (width // LANES), dot(low_t, grad))
        more = dot(grad, up[0, :, n * width : (n + 1) * width], NT)
        total = more if total is None else total + more
    rank = total.astype(BF16)
    rank_grad[...] = rank
    normed, _s = norm_rows(x[...].astype(F32))
    h1 = (normed * gain[...] + shift[...]).astype(BF16)
    put(3 * (width // LANES), dot(rank.T, h1))


def qkv_grad(at, g, low, x, gain, shift, up, groups):
    rows, width = x.shape
    return pl.pallas_call(
        qkv_grad_kernel,
        grid_spec=pltpu.PrefetchScalarGridSpec(
            num_scalar_prefetch=2,
            grid=(1,),
            in_specs=[
                whole((3, rows, width)),
                whole((rows, RANK)),
                whole((rows, width)),
                whole((1, width)),
                whole((1, width)),
                chosen((RANK, 3 * width)),
            ],
            out_specs=[whole((groups, 1, RANK, LANES)), whole((rows, RANK))],
        ),
        out_shape=[
            jax.ShapeDtypeStruct((groups, 1, RANK, LANES), BF16),
            jax.ShapeDtypeStruct((rows, RANK), BF16),
        ],
        compiler_params=params(16),
        cost_estimate=cost(2 * rows * 16 * 3 * width * 4, 8 * rows * width),
        name="qkv_grad",
    )(*at, g, low, x, gain, shift, up)


def input_grad_kernel(_adapter, at, g, w, rank_grad, down, x, gain, dx1, *refs):
    out, total = refs[-2:]
    j = pl.program_id(0)

    @pl.when(j == 0)
    def _():
        total[...] = dot(rank_grad[...], down[0]) + dot(g[0], w[...], NT)

    @pl.when(j == 1)
    def _():
        total[...] += dot(g[0], w[...], NT)

    @pl.when(j == 2)
    def _():
        grad = total[...] + dot(g[0], w[...], NT)
        normed, spread = norm_rows(x[...].astype(F32))
        out[...] = dx1[...] + norm_back(grad, normed, spread, gain[...])


def input_grad(at, g, w, rank_grad, down, x, gain, dx1, half, before=()):
    rows, width = x.shape
    cut = rows // 2
    part = pl.BlockSpec((cut, width), lambda j, adapter, at: (half, 0))
    order = lambda j: lax.rem(j + 1, 3)
    return pl.pallas_call(
        input_grad_kernel,
        grid_spec=pltpu.PrefetchScalarGridSpec(
            num_scalar_prefetch=2,
            grid=(3,),
            in_specs=[
                pl.BlockSpec((1, cut, width), lambda j, adapter, at: (j, half, 0)),
                pl.BlockSpec((width, width), lambda j, adapter, at: (0, order(j))),
                pl.BlockSpec((cut, RANK), lambda j, adapter, at: (half, 0)),
                chosen((RANK, width)),
                part,
                fixed((1, width)),
                part,
            ]
            + [ANY] * len(before),
            out_specs=part,
            scratch_shapes=[pltpu.VMEM((cut, width), F32)],
        ),
        out_shape=jax.ShapeDtypeStruct((rows, width), F32),
        input_output_aliases={9 + n: n for n in range(len(before))},
        compiler_params=params(20),
        cost_estimate=cost(3 * rows * width * width, 6 * width * width + 8 * rows * width),
        name="input_grad",
    )(*at, g, w, rank_grad, down, x, gain, dx1, *before)


def swap_order():
    bits = []
    n = 4
    while n < lax.axis_size("dp"):
        bits.append((n, 0))
        n *= 2
    n = 1
    while n < lax.axis_size("seq"):
        bits.append((0, n))
        n *= 2
    bits.append((2, 0))
    first = bits[:4]
    second = [first[1], first[0], first[3], first[2]]
    return (first, second), bits[4:]


def swap(values, step):
    size, ways = lax.axis_size("dp"), lax.axis_size("seq")
    perm = []
    for d in range(size):
        flip_d, flip_s = step[d & 1]
        for s in range(ways):
            perm.append((d * ways + s, (d ^ flip_d) * ways + (s ^ flip_s)))
    return lax.ppermute(values, ("dp", "seq"), perm)


def device_codes():
    orders, _rest = swap_order()
    size, ways = lax.axis_size("dp"), lax.axis_size("seq")
    table = np.zeros((size * ways, 9 + ways), np.int32)
    for d in range(size):
        for s in range(ways):
            codes = []
            for order in orders:
                on = [((d & bit_d) | (s & bit_s)) != 0 for bit_d, bit_s in order]
                codes.append(
                    (
                        sum(8 >> n for n in range(4) if on[n]),
                        sum(1 << n for n in range(4) if on[n]),
                        8 * on[2] + 4 * on[3],
                    )
                )
            mine, theirs = codes[d & 1], codes[1 - (d & 1)]
            row = [s, d & 1, mine[0], theirs[0], mine[1], theirs[1], mine[2], theirs[2], d]
            table[d * ways + s] = row + [(s + n) % ways for n in range(1, ways)] + [0]
    place = lax.axis_index("dp") * ways + lax.axis_index("seq")
    return lax.dynamic_slice_in_dim(jnp.asarray(table), place, 1, 0)[0]


def slot_masks(sequence):
    orders, _rest = swap_order()
    masks = []
    for order in orders:
        slots = [0, 1]
        for n in sequence:
            slots = slots + [slot ^ order[n][0] for slot in slots]
        masks.append(slots)
    return masks


def scatter_steps():
    orders, _rest = swap_order()
    return [((1, 0), (1, 0))] + list(zip(*orders))


def scatter_stage(held, step):
    half = held.shape[1] // 2
    return jnp.concatenate([held[:, :half], swap(held[:, half:], step)], axis=0)


def owner_sum_kernel(owners, at, held, out, total, *, masks):
    total[...] = jnp.zeros_like(total)
    for n, (even, odd) in enumerate(zip(*masks)):
        mask = even if even == odd else jnp.where(at[1] == 0, even, odd)
        total[owners[at[8] ^ mask]] += held[n].astype(F32)
    for a in range(NADAPT):
        out[:, a] = total[a].astype(BF16)


def owner_sum(at, owners, held, masks):
    slots, groups, parts, rank, lanes = held.shape
    pieces = groups * parts
    held = held.reshape(slots, pieces, rank, lanes)
    step = min(pieces, 4)
    out = pl.pallas_call(
        functools.partial(owner_sum_kernel, masks=masks),
        grid_spec=pltpu.PrefetchScalarGridSpec(
            num_scalar_prefetch=2,
            grid=(pieces // step,),
            in_specs=[pl.BlockSpec((slots, step, rank, lanes), lambda i, *_: (0, i, 0, 0))],
            out_specs=pl.BlockSpec((step, NADAPT, rank, lanes), lambda i, *_: (i, 0, 0, 0)),
            scratch_shapes=[pltpu.VMEM((NADAPT, step, rank, lanes), F32)],
        ),
        out_shape=jax.ShapeDtypeStruct((pieces, NADAPT, rank, lanes), BF16),
        compiler_params=params(12),
        cost_estimate=cost(held.size, 2 * held.size),
        name="owner_sum",
    )(owners, at[1], held)
    out = out.reshape(groups, parts, NADAPT, rank, lanes)
    _orders, rest = swap_order()
    for bits in rest:
        out = (out.astype(F32) + swap(out, (bits, bits)).astype(F32)).astype(BF16)
    return out


def spread_kernel(_adapter, at, mine, theirs, *outs, plan, straight):
    for core in range(2):

        @pl.when(at[1] == core)
        def _():
            for ref, part, first, count in zip(outs, *plan):
                for p in range(count):
                    piece = first + p
                    near = piece >> 4 == core
                    held = mine if near else theirs
                    if straight:
                        low = (piece & 15) ^ (at[6] if near else at[7])
                    else:
                        low = int(f"{piece & 15:04b}"[::-1], 2) ^ (at[4] if near else at[5])
                    ref[:, :, p * LANES : (p + 1) * LANES] = held[low, part].astype(F32)


def spread(at, mine, theirs, plan, straight=False):
    parts, firsts, counts = plan
    shapes = [(NADAPT, RANK, count * LANES) for count in counts]
    return pl.pallas_call(
        functools.partial(spread_kernel, plan=plan, straight=straight),
        grid_spec=pltpu.PrefetchScalarGridSpec(
            num_scalar_prefetch=2,
            grid=(1,),
            in_specs=[whole(mine.shape), whole(theirs.shape)],
            out_specs=[whole(shape) for shape in shapes],
        ),
        out_shape=[jax.ShapeDtypeStruct(shape, F32) for shape in shapes],
        compiler_params=params(20),
        cost_estimate=cost(1, 12 * mine.size),
        name="spread",
    )(*at, mine, theirs)


def tie(*values):
    flat, tree = jax.tree.flatten(values)
    return jax.tree.unflatten(tree, lax.optimization_barrier(flat))


def body(
    clip_tokens, adapter_index, ln1_gain, ln1_bias, qkv_weight, qkv_bias, qkv_down, qkv_up,
    out_weight, out_bias, out_down, out_up, ln2_gain, ln2_bias, fc1_weight, fc1_bias, fc1_down,
    fc1_up, fc2_weight, fc2_bias, fc2_down, fc2_up, cotangent,
):
    _one, rows, width = clip_tokens.shape
    devices = lax.axis_size("seq")
    groups = 32
    pin = lambda v: pltpu.with_memory_space_constraint(v, pltpu.HBM)
    row = lambda v: pin(v.reshape(1, -1))
    x = pin(clip_tokens[0])
    cot = cotangent[0]
    free_qkv = qkv_weight
    qkv_weight, qkv_down, qkv_up = pin(qkv_weight), pin(qkv_down), pin(qkv_up)
    out_weight, out_down, out_up = pin(out_weight), pin(out_down), pin(out_up)
    fc1_weight, fc1_down, fc1_up = pin(fc1_weight), pin(fc1_down), pin(fc1_up)
    fc2_weight, fc2_down, fc2_up = pin(fc2_weight), pin(fc2_down), pin(fc2_up)
    peers = range(1, devices)
    at = (adapter_index, device_codes())
    tagged = jnp.broadcast_to(adapter_index.astype(BF16)[:, None], (256, LANES))
    tagged, cot = tie(tagged, cot)
    tags = lax.all_gather(tagged, "dp", axis=0, tiled=True)
    masks_a, masks_b = slot_masks((0, 1, 2, 3)), slot_masks((2, 3, 0, 1))

    def from_peer(values, shift):
        return lax.ppermute(values, "seq", [((n + shift) % devices, n) for n in range(devices)])

    tables = tuple(pin(jnp.asarray(t)) for t in rotary_tables(rows * devices))
    cos, sin = tables
    x_peer = jnp.concatenate([from_peer(clip_tokens[0], n) for n in peers], axis=0)
    first_set = (row(ln1_gain), row(ln1_bias), qkv_weight, row(qkv_bias), qkv_down, qkv_up)
    own, mixed, back, low_qkv, top, total, grad2 = front_rows(
        at, x, pin(cot), first_set, tables, fc2_weight, fc2_down, fc2_up
    )
    peer, act, x1, low2, dx1, go, delta, lse, pieces_a = middle_rows(
        at, x_peer, first_set, tables, own, (mixed, top, total), x, pin(cot), back, grad2,
        (out_weight, row(out_bias), out_down, out_up),
        (row(ln2_gain), row(ln2_bias)),
        (fc1_weight, row(fc1_bias), fc1_down, fc1_up),
        fc2_down, groups,
    )
    own, peer, lse = pin(own), pin(peer), pin(lse)
    go_sent, sent, delta, tags = tie(go, pieces_a[None], delta, tags)
    index_all = tags[::256, 0].astype(jnp.int32)
    go_peer = jnp.stack([from_peer(go_sent, n) for n in peers])
    steps = scatter_steps()

    def halves(held):
        half = held.shape[1] // 2
        return held[:, :half], held[:, half:]

    def join(*parts):
        return jnp.concatenate(parts, axis=0)

    kept, sent = halves(sent)
    arrived = swap(sent, steps[0])
    kept, sent = halves(join(kept, arrived))
    sent, delta = tie(sent, delta)
    arrived = swap(sent, steps[1])
    back = functools.partial(own_back, at, own, peer, pin(go), lse, pin(delta), cos, sin)
    grads = back((0, 4), None)
    arrived, grads = tie(arrived, grads)
    kept, sent = halves(join(kept, arrived))
    sent, grads = tie(sent, grads)
    arrived = swap(sent, steps[2])
    grads, dk, dv = back((4, 4), grads)
    arrived, dk, go_peer = tie(arrived, dk, go_peer)
    dk, dv = pin(dk), pin(dv)
    kept, sent = halves(join(kept, arrived))
    sent, go_peer = tie(sent, go_peer)
    arrived = swap(sent, steps[3])
    grads = peer_back(at, own, peer, go_peer, cos, sin, dk, dv, (0, 4), (grads,))[0]
    arrived, grads, go_peer = tie(arrived, grads, go_peer)
    kept, sent = halves(join(kept, arrived))
    sent, go_peer = tie(sent, go_peer)
    arrived = swap(sent, steps[4])
    grads = peer_back(at, own, peer, go_peer, cos, sin, dk, dv, (4, 4), (grads,))[0]
    arrived, grads = tie(arrived, grads)
    total_a = owner_sum(at, index_all, join(kept, arrived), masks_a)
    total_a, grads = tie(total_a, grads)
    arrived_a = swap(total_a, steps[1])
    pieces_b, rank_grad = qkv_grad(
        at, grads, low_qkv, x, row(ln1_gain), row(ln1_bias), qkv_up, groups
    )
    held = scatter_stage(pieces_b[None], steps[0])

    def grad_half(half, rank_grad, before=()):
        return input_grad(
            at, grads, free_qkv, rank_grad, qkv_down, x, row(ln1_gain), pin(dx1), half, before
        )

    def output_half(half, low2, before=()):
        return output_rows(at, pin(act), fc2_weight, pin(x1), row(fc2_bias), low2, fc2_up, half, before)

    kept, sent = halves(held)
    sent, rank_grad = tie(sent, rank_grad)
    arrived = swap(sent, steps[3])
    grad_in = grad_half(0, rank_grad)
    arrived, arrived_a, rank_grad, grad_in = tie(arrived, arrived_a, rank_grad, grad_in)
    kept, sent = halves(join(kept, arrived))
    total_a = join(total_a, arrived_a)
    sent, total_a, rank_grad = tie(sent, total_a, rank_grad)
    arrived = swap(sent, steps[4])
    arrived_a = swap(total_a, steps[2])
    grad_in = grad_half(1, rank_grad, (grad_in,))
    arrived, arrived_a, grad_in = tie(arrived, arrived_a, grad_in)
    held, total_a = join(kept, arrived), join(total_a, arrived_a)
    held, total_a, low2 = tie(held, total_a, low2)
    arrived = swap(held, steps[1])
    arrived_a = swap(total_a, steps[3])
    block_output = output_half(0, low2)
    arrived, arrived_a, low2, block_output = tie(arrived, arrived_a, low2, block_output)
    held, total_a = join(held, arrived), join(total_a, arrived_a)
    held, total_a, low2 = tie(held, total_a, low2)
    arrived = swap(held, steps[2])
    arrived_a = swap(total_a, steps[4])
    block_output = output_half(1, low2, (block_output,))
    arrived, block_output = tie(arrived, block_output)
    total_b = owner_sum(at, index_all, join(held, arrived), masks_b)
    total_b, arrived_a = tie(total_b, arrived_a)
    total_a = join(total_a, arrived_a)
    arrived = swap(total_b, steps[4])
    theirs_a = swap(total_a, steps[0])
    total_b = join(total_b, arrived)
    total_b, total_a, theirs_a = tie(total_b, total_a, theirs_a)
    arrived = swap(total_b, steps[3])
    per = width // LANES
    spread_a = spread(
        at, total_a, theirs_a,
        ((0, 1, 2, 2, 2, 2), (0, 0, 0, per, 2 * per, 3 * per), (32, 32, per, per, per, per)),
    )
    arrived, spread_a = tie(arrived, spread_a)
    up1, down2, up2, down1, up_o, down_o = spread_a
    total_b = join(total_b, arrived)
    up_qkv, down_qkv = spread(
        at, total_b, swap(total_b, steps[0]), ((0, 0), (0, 3 * per), (3 * per, per)), straight=True
    )
    return (
        block_output[None], grad_in[None], down_qkv, up_qkv, down_o, up_o, down1, up1, down2, up2,
    )


def solution(mesh):
    split = P("dp", "seq", None)
    return jax.shard_map(
        body,
        mesh=mesh,
        in_specs=(split, P("dp")) + (P(),) * 20 + (split,),
        out_specs=(split, split) + (P(),) * 8,
        check_vma=False,
    )
```

```python
import functools

import jax
import jax.numpy as jnp
import numpy as np
from jax import lax
from jax.experimental import pallas as pl
from jax.experimental.pallas import tpu as pltpu
from jax.sharding import PartitionSpec as P

HEADS = 16
HD = 64
GRID = 16
NADAPT = 8
RANK = 16
EPSILON = 1e-06
LANES = 128
EXTRA = 48

F32 = jnp.float32
BF16 = jnp.bfloat16
NN = (((1,), (0,)), ((), ()))
NT = (((1,), (1,)), ((), ()))

ERFC = (
    0.16918800211151383,
    0.1707152747822528,
    0.14833885959986734,
    0.21492717178376733,
    -0.09465313901935662,
    0.5477232747113128,
    -0.5122807406271995,
    0.48556441585520754,
    -0.1295231387829952,
)


def dot(a, b, dims=NN):
    return lax.dot_general(a, b, dims, preferred_element_type=F32)


def params(megabytes):
    return pltpu.CompilerParams(
        dimension_semantics=("arbitrary",), vmem_limit_bytes=megabytes << 20
    )


def cost(flops, moved, exps=0):
    return pl.CostEstimate(flops=int(flops), bytes_accessed=int(moved), transcendentals=int(exps))


def norm_rows(values):
    centre = values - jnp.mean(values, axis=-1, keepdims=True)
    spread = lax.rsqrt(jnp.mean(centre * centre, axis=-1, keepdims=True) + EPSILON)
    return centre * spread, spread


def norm_back(grad_rows, normed, spread, gain):
    scaled = grad_rows * gain
    first = jnp.mean(scaled, axis=-1, keepdims=True)
    second = jnp.mean(scaled * normed, axis=-1, keepdims=True)
    return spread * (scaled - first - normed * second)


def rotary_tables(length):
    half = HD // 2
    side = half // 3
    lead = half - 2 * side
    token = np.arange(length)
    pair = np.arange(half)
    kind = np.where(pair < lead, 0, np.where(pair < lead + side, 1, 2))
    local = np.where(kind == 0, pair, np.where(kind == 1, pair - lead, pair - lead - side))
    total = np.where(kind == 0, lead, side)
    frequency = np.power(
        np.float32(10000.0), -local.astype(np.float32) / total.astype(np.float32)
    ).astype(np.float32)
    place = np.where(
        kind[None] == 0,
        (token // (GRID * GRID))[:, None],
        np.where(kind[None] == 1, (token // GRID % GRID)[:, None], (token % GRID)[:, None]),
    ).astype(np.float32)
    angle = place * frequency[None]
    cosine, sine = np.cos(angle), np.sin(angle)
    cos_rows = np.concatenate([cosine] * 4, axis=1).astype(np.float32)
    sin_rows = np.concatenate([-sine, sine, -sine, sine], axis=1).astype(np.float32)
    return cos_rows, sin_rows


def swap_halves(values):
    lane = lax.broadcasted_iota(jnp.int32, (1, LANES), 1)
    low = (lane & (HD // 2)) == 0
    return jnp.where(
        low, pltpu.roll(values, LANES - HD // 2, 1), pltpu.roll(values, HD // 2, 1)
    )


def head_mask(values, head):
    lane = lax.broadcasted_iota(jnp.int32, (1, LANES), 1)
    keep = (lane < HD) if head == 0 else (lane >= HD)
    return jnp.where(keep, values, jnp.zeros_like(values))


def whole(shape):
    return pl.BlockSpec(shape, lambda *_: (0,) * len(shape))


def fixed(shape):
    return pl.BlockSpec(shape, lambda *_: (0,) * len(shape), pipeline_mode=pl.Buffered(1))


def chosen(shape):
    return pl.BlockSpec((1,) + shape, lambda *ids: (ids[-2][0], 0, 0))


def chosen_tile(tile, which):
    return pl.BlockSpec((1, RANK, tile), lambda j, adapter, at: (adapter[0], 0, which(j)))


def position(piece, at, first=2):
    top = (piece >> 4) ^ at[1]
    return 16 * top + ((piece & 15) ^ jnp.where(top == 0, at[first], at[first + 1]))


CHUNK = 256


def qkv_tile(tile, h1, low, w, bias, up, cos, sin, out_ref, keep, first):
    scale = jnp.where(tile == 0, HD**-0.5, 1.0).astype(F32)
    turn = jnp.where(tile == 2, 0.0, 1.0).astype(F32)
    c = (cos[...] * turn + (1.0 - turn)) * scale
    s = sin[...] * (turn * scale)

    def chunk(n):
        cut = slice(n * CHUNK, (n + 1) * CHUNK)
        return dot(h1, w[:, cut]) + bias[:, cut] + dot(low, up[:, cut])

    count = w.shape[1] // CHUNK
    now = chunk(0)
    parts = []
    for n in range(count):
        later = chunk(n + 1) if n + 1 < count else None
        for g in range(CHUNK // LANES):
            part = now[:, g * LANES : (g + 1) * LANES]
            parts.append((part * c + swap_halves(part) * s).astype(BF16))
        now = later
    for n, part in enumerate(parts):
        out_ref[n] = part
        keep[first + n] = part


def attend_pairs(count, load, finish):
    loaded = [load(pair) for pair in range(count)]
    values_t = [v.T for _q, _k, v in loaded]

    def scores(item):
        pair, head = item
        q, k, _v = loaded[pair]
        return dot(k, head_mask(q, head), NT)

    items = [(pair, head) for pair in range(count) for head in range(2)]
    now = scores(items[0])
    for n, (pair, head) in enumerate(items):
        later = scores(items[n + 1]) if n + 1 < len(items) else None
        finish(pair, head, now, values_t[pair][head * HD : (head + 1) * HD])
        now = later


STEP_PAIRS = 2


def start_all(*groups):
    for group in groups:
        for copy in group:
            copy.start()


def wait_all(*groups):
    for group in groups:
        for copy in group:
            copy.wait()


def group(sems, pairs):
    return [pltpu.make_async_copy(a, b, sems.at[n]) for n, (a, b) in enumerate(pairs)]


def tiles(source, kept, size):
    return [(source.at[:, pl.ds(n * size, size)], kept.at[n]) for n in range(kept.shape[0])]


def front_kernel(
    adapter, at, x, w, w2,
    gain, shift, bias, down, up, cos, sin, cot, down2, up2,
    qkv, mixed_out, back, low, top_out, total_out, grad2,
    h1, keep, gain_k, shift_k, bias_k, down_k, up_k, cos_k, sin_k, cot_k, down2_k, up2_k,
    low_k, top_k, total_k, grad2_k, sem_a, sem_b, sem_c, sem_d,
    *, starts,
):
    j = pl.program_id(0)
    second, third = starts
    last = pl.num_programs(0) - 1
    mine = adapter[0]
    rows, width = x.shape
    place = pl.ds(pl.multiple_of(at[0] * rows, rows), rows)
    early = group(
        sem_a,
        [
            (gain, gain_k), (shift, shift_k), (down.at[mine], down_k),
            (cos.at[place], cos_k), (sin.at[place], sin_k),
        ]
        + tiles(bias, bias_k, width)
        + tiles(up.at[mine], up_k, width),
    )
    late = group(
        sem_b, [(cot, cot_k), (up2.at[mine], up2_k)] + tiles(down2.at[mine], down2_k, w2.shape[0])
    )
    stats = group(sem_c, [(low_k, low), (top_k, top_out), (total_k, total_out)])
    end = group(sem_d, [(grad2_k, grad2)])

    @pl.when(j == 0)
    def _():
        start_all(early, late)
        normed, _s = norm_rows(x[...].astype(F32))
        wait_all(early)
        held = (normed * gain_k[...] + shift_k[...]).astype(BF16)
        h1[...] = held
        low_k[...] = dot(held, down_k[...], NT).astype(BF16)

    @pl.when(j < second)
    def _():
        qkv_tile(j, h1[...], low_k[...], w, bias_k[j], up_k[j], cos_k, sin_k, qkv, keep, 8 * j)

    @pl.when((j >= second) & (j < third))
    def _():
        first = (j - second) * STEP_PAIRS

        def load(pair):
            return keep[first + pair], keep[8 + first + pair], keep[16 + first + pair]

        def finish(pair, head, scores, values_t):
            top = jnp.max(scores, axis=0, keepdims=True)
            weights = jnp.exp(scores - top)
            start = pair * LANES + head * HD
            mixed_out[start : start + HD, :] = dot(values_t, weights.astype(BF16))
            top_k[first + pair, head : head + 1, :] = top
            total_k[first + pair, head : head + 1, :] = jnp.sum(weights, axis=0, keepdims=True)

        attend_pairs(STEP_PAIRS, load, finish)

    @pl.when(j == third)
    def _():
        start_all(stats)
        wait_all(late)
        grad2_k[...] = dot(cot_k[...], up2_k[...], NT).astype(BF16)
        start_all(end)

    @pl.when(j >= third)
    def _():
        side = dot(grad2_k[...], down2_k[j - third])
        back[...] = (dot(cot_k[...], w2[...], NT) + side).astype(BF16)

    @pl.when(j == last)
    def _():
        wait_all(stats, end)


def clip(value, low, high):
    return jnp.minimum(jnp.maximum(value, low), high)


ANY = pl.BlockSpec(memory_space=pl.ANY)


def front_rows(at, x, cot, first_set, tables, w2, down2, up2):
    gain, shift, w, bias, down, up = first_set
    rows, width = x.shape
    ff = w2.shape[0]
    tile = 1024
    second = w.shape[1] // width
    third = second + HEADS // 2 // STEP_PAIRS
    steps = third + ff // tile
    one = lambda j: jnp.minimum(j, second - 1)
    two = lambda j: clip(j - second, 0, third - second - 1)
    three = lambda j: clip(j - third, 0, steps - third - 1)
    stat = (HEADS // 2, 2, rows)
    return pl.pallas_call(
        functools.partial(front_kernel, starts=(second, third)),
        grid_spec=pltpu.PrefetchScalarGridSpec(
            num_scalar_prefetch=2,
            grid=(steps,),
            in_specs=[
                fixed((rows, width)),
                pl.BlockSpec((width, width), lambda j, adapter, at: (0, one(j))),
                pl.BlockSpec((tile, width), lambda j, adapter, at: (three(j), 0)),
            ]
            + [ANY] * 10,
            out_specs=[
                pl.BlockSpec((8, rows, LANES), lambda j, adapter, at: (one(j), 0, 0)),
                pl.BlockSpec((STEP_PAIRS * LANES, rows), lambda j, adapter, at: (two(j), 0)),
                pl.BlockSpec((rows, tile), lambda j, adapter, at: (0, three(j))),
            ]
            + [ANY] * 4,
            scratch_shapes=[
                pltpu.VMEM((rows, width), BF16),
                pltpu.VMEM((24, rows, LANES), BF16),
                pltpu.VMEM((1, width), F32),
                pltpu.VMEM((1, width), F32),
                pltpu.VMEM((second, 1, width), F32),
                pltpu.VMEM((RANK, width), BF16),
                pltpu.VMEM((second, RANK, width), BF16),
                pltpu.VMEM((rows, LANES), F32),
                pltpu.VMEM((rows, LANES), F32),
                pltpu.VMEM((rows, width), BF16),
                pltpu.VMEM((ff // tile, RANK, tile), BF16),
                pltpu.VMEM((RANK, width), BF16),
                pltpu.VMEM((rows, RANK), BF16),
                pltpu.VMEM(stat, F32),
                pltpu.VMEM(stat, F32),
                pltpu.VMEM((rows, RANK), BF16),
                pltpu.SemaphoreType.DMA((5 + 2 * second,)),
                pltpu.SemaphoreType.DMA((2 + ff // tile,)),
                pltpu.SemaphoreType.DMA((3,)),
                pltpu.SemaphoreType.DMA((1,)),
            ],
        ),
        out_shape=[
            pltpu.HBM((24, rows, LANES), BF16),
            pltpu.HBM((width, rows), F32),
            pltpu.HBM((rows, ff), BF16),
            pltpu.HBM((rows, RANK), BF16),
            pltpu.HBM(stat, F32),
            pltpu.HBM(stat, F32),
            pltpu.HBM((rows, RANK), BF16),
        ],
        compiler_params=params(44),
        cost_estimate=cost(
            2 * rows * width * (3 * width + ff) + 16 * rows * rows * width, 20 << 20, 16 * rows * rows
        ),
        name="front_rows",
    )(*at, x, w, w2, gain, shift, bias, down, up, *tables, cot, down2, up2)


def gelu_both(f):
    z = jnp.abs(f) * (0.5**0.5)
    t = 1.0 / (1.0 + 0.3 * z)
    poly = ERFC[-1]
    for c in ERFC[-2::-1]:
        poly = poly * t + c
    bell = jnp.exp(f * f * -0.5)
    tail = (0.5 * poly) * t * bell
    phi = jnp.where(f < 0, tail, 1.0 - tail)
    return f * phi, phi + f * (bell * 0.3989422804014327)


def middle_kernel(
    adapter, at, xp, wq, w1, back,
    gain1, shift1, bq, downq, upq, cos, sin, own, mixed, top, total,
    x, cot, grad2, w_out, b_out, out_down, out_up, gain, shift, b1, down1, up1, down2,
    qkv, act_out, x1_out, low2_out, dx1_out, go_out, delta_out, lse_out, stay_out, leave_out,
    h1, lowq, keep, o, h2, dh2, low_o, low1, low1_t, grad2_t, low2, grad1,
    gain1_k, shift1_k, bq_k, downq_k, upq_k, cos_k, sin_k, q_own, mixed_in, top_in, total_in,
    x_k, cot_k, grad2_k, w_out_k, b_out_k, out_down_k, out_up_k, gain_k, shift_k, b1_k, down1_k, up1_k, down2_k,
    x1, low2_k, dx1_k, go, delta_k, lse, pieces,
    sem_a, sem_b, sem_c, sem_d, sem_e,
    *, starts, peers,
):
    j = pl.program_id(0)
    second, third = starts
    last = pl.num_programs(0) - 1
    rows, width = xp.shape
    tile = w1.shape[1]
    mine = adapter[0]
    places = [pl.ds(pl.multiple_of(at[9 + p] * rows, rows), rows) for p in range(peers)]
    early = group(
        sem_a,
        [(gain1, gain1_k), (shift1, shift1_k), (downq.at[mine], downq_k)]
        + [(cos.at[places[p]], cos_k.at[p]) for p in range(peers)]
        + [(sin.at[places[p]], sin_k.at[p]) for p in range(peers)]
        + tiles(bq, bq_k, width)
        + tiles(upq.at[mine], upq_k, width),
    )
    later = group(
        sem_b, [(own.at[pl.ds(0, 8)], q_own), (mixed, mixed_in), (top, top_in), (total, total_in)]
    )
    late = group(
        sem_c,
        [
            (x, x_k), (cot, cot_k), (grad2, grad2_k), (w_out, w_out_k), (b_out, b_out_k),
            (out_down.at[mine], out_down_k), (out_up.at[mine], out_up_k), (gain, gain_k),
            (shift, shift_k), (down1.at[mine], down1_k),
        ]
        + tiles(b1, b1_k, tile)
        + tiles(up1.at[mine], up1_k, tile)
        + tiles(down2.at[mine], down2_k, tile),
    )
    middle_out = group(sem_d, [(x1, x1_out), (lse, lse_out)])
    end = group(
        sem_e,
        [(low2_k, low2_out), (dx1_k, dx1_out), (go, go_out), (delta_k, delta_out)]
        + [(pieces.at[pl.ds(0, 16)], stay_out), (pieces.at[pl.ds(16, 16)], leave_out)],
    )

    @pl.when(j == 0)
    def _():
        start_all(early, later, late)

    @pl.when(j < second)
    def _():
        which, p = j // peers, lax.rem(j, peers)

        @pl.when(which == 0)
        def _():
            normed, _s = norm_rows(xp[...].astype(F32))

            @pl.when(j == 0)
            def _():
                wait_all(early)

            normed = (normed * gain1_k[...] + shift1_k[...]).astype(BF16)
            h1[p] = normed
            lowq[p] = dot(normed, downq_k[...], NT).astype(BF16)

        qkv_tile(
            which, h1[p], lowq[p], wq, bq_k[which], upq_k[which], cos_k.at[p], sin_k.at[p],
            qkv, keep, 24 * p + 8 * which,
        )

    @pl.when(j == second)
    def _():
        wait_all(later)

    @pl.when((j >= second) & (j < third))
    def _():
        first = (j - second) * STEP_PAIRS
        held = []

        def load(pair):
            n = first + pair
            k = [keep[24 * p + 8 + n] for p in range(peers)]
            v = [keep[24 * p + 16 + n] for p in range(peers)]
            if peers > 1:
                k, v = [jnp.concatenate(k, axis=0)], [jnp.concatenate(v, axis=0)]
            return q_own[n], k[0], v[0]

        def finish(pair, head, scores, values_t):
            n = first + pair
            before = top_in[n, head : head + 1, :]
            top = jnp.maximum(jnp.max(scores, axis=0, keepdims=True), before)
            scale = jnp.exp(before - top)
            weights = jnp.exp(scores - top)
            total = jnp.sum(weights, axis=0, keepdims=True)
            total = total + scale * total_in[n, head : head + 1, :]
            start = pl.ds(pl.multiple_of(n * LANES + head * HD, HD), HD)
            mixed = dot(values_t, weights.astype(BF16)) + scale * mixed_in[start, :]
            held.append(mixed * (1.0 / total))
            lse[n, head : head + 1, :] = top + jnp.log(total)
            if head == 1:
                o[n] = jnp.concatenate(held[-2:], axis=0).T.astype(BF16)

        attend_pairs(STEP_PAIRS, load, finish)

    def put(first, slot, grad):
        for p in range(grad.shape[1] // LANES):
            cut = slice(p * LANES, (p + 1) * LANES)
            pieces[position(first + p, at), slot] = grad[:, cut].astype(BF16)

    @pl.when(j == third)
    def _():
        wait_all(late)
        mixed = jnp.concatenate([o[n] for n in range(HEADS // 2)], axis=1)
        low = dot(mixed, out_down_k[...], NT).astype(BF16)
        low_o[...] = low
        branch = dot(mixed, w_out_k[...]) + b_out_k[...] + dot(low, out_up_k[...])
        mid = x_k[...].astype(F32) + branch
        x1[...] = mid
        normed, _s = norm_rows(mid)
        rows2 = (normed * gain_k[...] + shift_k[...]).astype(BF16)
        h2[...] = rows2
        low_1 = dot(rows2, down1_k[...], NT).astype(BF16)
        low1[...] = low_1
        low1_t[...] = low_1.T
        grad2_t[...] = grad2_k[...].T
        dh2[...] = jnp.zeros_like(dh2)
        low2[...] = jnp.zeros_like(low2)
        grad1[...] = jnp.zeros_like(grad1)
        start_all(middle_out)

    @pl.when(j >= third)
    def _():
        n_tile = j - third

        def hidden(n):
            cut = slice(n * CHUNK, (n + 1) * CHUNK)
            return dot(h2[...], w1[:, cut]) + b1_k[n_tile, :, cut] + dot(low1[...], up1_k[n_tile, :, cut])

        first = n_tile * (tile // LANES)
        count = tile // CHUNK
        now = hidden(0)
        acts, dfs = [], []
        for n in range(count):
            later = hidden(n + 1) if n + 1 < count else None
            cut = slice(n * CHUNK, (n + 1) * CHUNK)
            act, slope = gelu_both(now)
            acts.append(act.astype(BF16))
            dfs.append((back[:, cut].astype(F32) * slope).astype(BF16))
            now = later
        act, df = jnp.concatenate(acts, axis=1), jnp.concatenate(dfs, axis=1)
        dh2[...] += dot(df, w1[...], NT)
        low2[...] += dot(act, down2_k[n_tile], NT)
        grad1[...] += dot(df, up1_k[n_tile], NT)
        act_out[...] = act
        put(first, 0, dot(low1_t[...], df))
        put(first, 1, dot(grad2_t[...], act))

    @pl.when(j == last)
    def _():
        low_2 = low2[...].astype(BF16)
        low2_k[...] = low_2
        g1 = grad1[...].astype(BF16)
        back2 = dh2[...] + dot(g1, down1_k[...])
        normed, spread = norm_rows(x1[...])
        dx1 = cot_k[...].astype(F32) + norm_back(back2, normed, spread, gain_k[...])
        dx1_k[...] = dx1
        da = dx1.astype(BF16)
        g_o = dot(da, out_up_k[...], NT).astype(BF16)
        new_go = (dot(da, w_out_k[...], NT) + dot(g_o, out_down_k[...])).astype(BF16)
        go[EXTRA : EXTRA + rows, :] = new_go
        mixed = jnp.concatenate([o[n] for n in range(HEADS // 2)], axis=1)
        product = new_go.astype(F32) * mixed.astype(F32)
        high = product.astype(BF16)
        rest = (product - high.astype(F32)).astype(BF16)
        lane = lax.broadcasted_iota(jnp.int32, (HEADS, width), 1)
        head = lax.broadcasted_iota(jnp.int32, (HEADS, width), 0)
        pick = (lane // HD == head).astype(BF16)
        delta = dot(pick, high, NT) + dot(pick, rest, NT)
        delta_k[...] = delta
        if rows < width // 2:
            go[0:EXTRA, :] = jnp.zeros((EXTRA, width), BF16)
        logs = jnp.concatenate([lse[n] for n in range(HEADS // 2)], axis=0)
        for side, stat in enumerate((logs, delta)):
            left = stat
            for n in range(3):
                part = left.astype(BF16)
                go[16 * n : 16 * n + 16, side * (width // 2) : side * (width // 2) + rows] = part
                left = left - part.astype(F32)
        start_all(end[:4])
        per = width // LANES
        put(jnp.int32(0), 2, dot(low_2.T, cot_k[...]))
        put(jnp.int32(per), 2, dot(g1.T, h2[...]))
        put(jnp.int32(2 * per), 2, dot(low_o[...].T, da))
        put(jnp.int32(3 * per), 2, dot(g_o.T, mixed))
        start_all(end[4:])
        wait_all(middle_out, end)


def middle_rows(
    at, xp, first_set, tables, own, state, x, cot, back, grad2, out_set, norm_set, fc1_set, down2, groups
):
    rows, width = x.shape
    peers = xp.shape[0] // rows
    w1 = fc1_set[0]
    ff = w1.shape[1]
    tile = 1024
    second = 3 * peers
    third = second + HEADS // 2 // STEP_PAIRS
    steps = third + ff // tile
    one = lambda j: jnp.minimum(j, second - 1) // peers
    peer = lambda j: lax.rem(jnp.minimum(j, second - 1), peers)
    two = lambda j: clip(j - second, 0, third - second - 1)
    three = lambda j: clip(j - third, 0, steps - third - 1)
    stat = (HEADS // 2, 2, rows)
    count = ff // tile
    vmem = pltpu.VMEM
    return pl.pallas_call(
        functools.partial(middle_kernel, starts=(second, third), peers=peers),
        grid_spec=pltpu.PrefetchScalarGridSpec(
            num_scalar_prefetch=2,
            grid=(steps,),
            in_specs=[
                pl.BlockSpec((rows, width), lambda j, adapter, at: (jnp.minimum(j, peers - 1), 0)),
                pl.BlockSpec((width, width), lambda j, adapter, at: (0, one(j))),
                pl.BlockSpec((width, tile), lambda j, adapter, at: (0, three(j))),
                pl.BlockSpec((rows, tile), lambda j, adapter, at: (0, three(j))),
            ]
            + [ANY] * 24,
            out_specs=[
                pl.BlockSpec((8, rows, LANES), lambda j, adapter, at: (3 * peer(j) + one(j), 0, 0)),
                pl.BlockSpec((rows, tile), lambda j, adapter, at: (0, three(j))),
            ]
            + [ANY] * 8,
            scratch_shapes=[
                vmem((peers, rows, width), BF16),
                vmem((peers, rows, RANK), BF16),
                vmem((24 * peers, rows, LANES), BF16),
                vmem((HEADS // 2, rows, LANES), BF16),
                vmem((rows, width), BF16),
                vmem((rows, width), F32),
                vmem((rows, RANK), BF16),
                vmem((rows, RANK), BF16),
                vmem((RANK, rows), BF16),
                vmem((RANK, rows), BF16),
                vmem((rows, RANK), F32),
                vmem((rows, RANK), F32),
                vmem((1, width), F32),
                vmem((1, width), F32),
                vmem((3, 1, width), F32),
                vmem((RANK, width), BF16),
                vmem((3, RANK, width), BF16),
                vmem((peers, rows, LANES), F32),
                vmem((peers, rows, LANES), F32),
                vmem((8, rows, LANES), BF16),
                vmem((width, rows), F32),
                vmem(stat, F32),
                vmem(stat, F32),
                vmem((rows, width), BF16),
                vmem((rows, width), BF16),
                vmem((rows, RANK), BF16),
                vmem((width, width), BF16),
                vmem((1, width), F32),
                vmem((RANK, width), BF16),
                vmem((RANK, width), BF16),
                vmem((1, width), F32),
                vmem((1, width), F32),
                vmem((count, 1, tile), F32),
                vmem((RANK, width), BF16),
                vmem((count, RANK, tile), BF16),
                vmem((count, RANK, tile), BF16),
                vmem((rows, width), F32),
                vmem((rows, RANK), BF16),
                vmem((rows, width), F32),
                vmem((EXTRA + rows, width), BF16),
                vmem((HEADS, rows), F32),
                vmem(stat, F32),
                vmem((groups, 3, RANK, LANES), BF16),
                pltpu.SemaphoreType.DMA((9 + 2 * peers,)),
                pltpu.SemaphoreType.DMA((4,)),
                pltpu.SemaphoreType.DMA((10 + 3 * count,)),
                pltpu.SemaphoreType.DMA((2,)),
                pltpu.SemaphoreType.DMA((6,)),
            ],
        ),
        out_shape=[
            pltpu.HBM((24 * peers, rows, LANES), BF16),
            pltpu.HBM((rows, ff), BF16),
            pltpu.HBM((rows, width), F32),
            pltpu.HBM((rows, RANK), BF16),
            pltpu.HBM((rows, width), F32),
            pltpu.HBM((EXTRA + rows, width), BF16),
            pltpu.HBM((HEADS, rows), F32),
            pltpu.HBM(stat, F32),
            pltpu.HBM((groups // 2, 3, RANK, LANES), BF16),
            pltpu.HBM((groups // 2, 3, RANK, LANES), BF16),
        ],
        compiler_params=params(56),
        cost_estimate=cost(
            4 * rows * width * ff + (4 + 6 * peers) * rows * width * width, 40 << 20, rows * ff
        ),
        name="middle_rows",
    )(
        *at, xp, first_set[2], w1, back,
        first_set[0], first_set[1], first_set[3], first_set[4], first_set[5], *tables, own, *state,
        x, cot, grad2, *out_set, *norm_set, *fc1_set[1:], down2,
    )


def output_kernel(_adapter, at, act, w2, x1, b2, low2, up2, *refs):
    out, y = refs[-2:]
    j = pl.program_id(0)
    last = pl.num_programs(0) - 1

    @pl.when(j == 0)
    def _():
        y[...] = dot(act[...], w2[...])

    @pl.when((j > 0) & (j < last))
    def _():
        y[...] += dot(act[...], w2[...])

    @pl.when(j == last)
    def _():
        side = b2[...] + dot(low2[...], up2[0])
        out[...] = (x1[...] + (y[...] + dot(act[...], w2[...]) + side)).astype(BF16)


def output_rows(at, act, w2, x1, b2, low2, up2, half, before=()):
    rows, ff = act.shape
    width = x1.shape[1]
    wide = width // 2
    tile = 1024
    part = pl.BlockSpec((rows, wide), lambda j, adapter, at: (0, half))
    return pl.pallas_call(
        output_kernel,
        grid_spec=pltpu.PrefetchScalarGridSpec(
            num_scalar_prefetch=2,
            grid=(ff // tile,),
            in_specs=[
                pl.BlockSpec((rows, tile), lambda j, adapter, at: (0, j)),
                pl.BlockSpec((tile, wide), lambda j, adapter, at: (j, half)),
                part,
                pl.BlockSpec((1, wide), lambda j, adapter, at: (0, half)),
                fixed((rows, RANK)),
                pl.BlockSpec((1, RANK, wide), lambda j, adapter, at: (adapter[0], 0, half)),
            ]
            + [ANY] * len(before),
            out_specs=part,
            scratch_shapes=[pltpu.VMEM((rows, wide), F32)],
        ),
        out_shape=jax.ShapeDtypeStruct((rows, width), BF16),
        input_output_aliases={8 + n: n for n in range(len(before))},
        compiler_params=params(24),
        cost_estimate=cost(rows * width * ff, width * ff + 2 * rows * ff),
        name="output_rows",
    )(*at, act, w2, x1, b2, low2, up2, *before)


def unrotate(values, cos, sin):
    return values * cos[...] - swap_halves(values) * sin[...]


def score_grads(s, dp, lse, delta):
    prob = jnp.exp(s - lse)
    return prob.astype(BF16), (prob * (dp - delta)).astype(BF16)


def own_back_kernel(_adapter, at, q0, k0, v0, go, lse0, delta0, cos, sin, *refs, first_pair, peers):
    k1, v1 = refs[:peers], refs[peers : 2 * peers]
    dq, dk, dv = refs[-3:]
    i = pl.program_id(0) + first_pair
    rows = q0.shape[1]
    keys = jnp.concatenate([k0[0]] + [k[0] for k in k1], axis=0)
    values = jnp.concatenate([v0[0]] + [v[0] for v in v1], axis=0)
    keys_t = keys.T

    def first(head):
        q = head_mask(q0[0], head)
        g = head_mask(go[EXTRA : EXTRA + rows, :], head)
        return dot(keys, q, NT), dot(values, g, NT), q, g

    grad_q = []
    now = first(0)
    for head in range(2):
        later = first(1) if head == 0 else None
        s, dp, q, g = now
        row = pl.ds(2 * i + head, 1)
        prob, ds = score_grads(s, dp, lse0[i, head : head + 1, :], delta0[row, :])
        grad_q.append(dot(keys_t[head * HD : (head + 1) * HD], ds))
        more_v = dot(prob[:rows], g)
        more_k = dot(ds[:rows], q)
        if head == 0:
            dv[...] = more_v
            dk[...] = more_k
        else:
            dv[...] += more_v
            dk[...] += more_k
        now = later
    dq[0] = unrotate(jnp.concatenate(grad_q, axis=0).T * (HD**-0.5), cos, sin).astype(BF16)


def peer_back_kernel(_adapter, at, k0, v0, gp, stats, cos, sin, dk_in, dv_in, *refs, first_pair, peers):
    q1 = refs[:peers]
    out, lse1, delta1 = refs[-3:]
    i = pl.program_id(0) + first_pair
    rows = k0.shape[1]
    half = stats.shape[2] // 2

    @pl.when(i == first_pair)
    def _():
        for n in range(peers):
            for side, ref in enumerate((lse1, delta1)):
                cut = slice(side * half, side * half + rows)
                ref[n] = (
                    stats[n, 0:16, cut].astype(F32)
                    + stats[n, 16:32, cut].astype(F32)
                    + stats[n, 32:48, cut].astype(F32)
                )

    def first(item):
        head, peer = item
        q = head_mask(q1[peer][0], head)
        g = head_mask(gp[peer, EXTRA : EXTRA + rows, :], head)
        return dot(k0[0], q, NT), dot(v0[0], g, NT), q, g

    items = [(head, peer) for peer in range(peers) for head in range(2)]
    grad_k, grad_v = dk_in[...], dv_in[...]
    now = first(items[0])
    for n, (head, peer) in enumerate(items):
        later = first(items[n + 1]) if n + 1 < len(items) else None
        s, dp, q, g = now
        row = pl.ds(2 * i + head, 1)
        prob, ds = score_grads(s, dp, lse1[peer, row, :], delta1[peer, row, :])
        grad_v = grad_v + dot(prob, g)
        grad_k = grad_k + dot(ds, q)
        now = later
    out[0] = unrotate(grad_k, cos, sin).astype(BF16)
    out[1] = grad_v.astype(BF16)


def attend_back(limit, kernel, at, args, specs, outs, blocks, before, pairs, peers, scratch, flops, name):
    first, count = pairs
    before = () if before is None else tuple(before)
    steps = HEADS // 2
    return pl.pallas_call(
        functools.partial(kernel, first_pair=first, peers=peers),
        grid_spec=pltpu.PrefetchScalarGridSpec(
            num_scalar_prefetch=2,
            grid=(count,),
            in_specs=specs + [pl.BlockSpec(memory_space=pl.ANY)] * len(before),
            out_specs=[pl.BlockSpec((blocks[0], outs[0].shape[1], LANES), lambda i, adapter, at: (blocks[1], 0, i + first))]
            + [pl.BlockSpec((o.shape[0], LANES), lambda i, adapter, at: (0, i + first)) for o in outs[1:]],
            scratch_shapes=scratch,
        ),
        out_shape=outs,
        input_output_aliases={2 + len(args) + n: n for n in range(len(before))},
        compiler_params=params(limit),
        cost_estimate=cost(
            flops * count // steps,
            4 * sum(a.size for a in args[:4]) * count // steps,
            flops * count // steps // 512,
        ),
        name=name,
    )(*at, *args, *before)


def own_back(at, own, peer, go, lse, delta, cos, sin, pairs, before):
    rows = own.shape[1]
    peers = peer.shape[0] // 24
    width = own.shape[0] // 3 * LANES
    first = pairs[0]

    def part(which):
        return pl.BlockSpec((1, rows, LANES), lambda i, adapter, at: (8 * which + first + i, 0, 0))

    table = pl.BlockSpec((rows, LANES), lambda i, adapter, at: (at[0], 0), pipeline_mode=pl.Buffered(1))
    return attend_back(
        24,
        own_back_kernel,
        at,
        (own, own, own, go, lse, delta, cos, sin) + (peer,) * (2 * peers),
        [part(0), part(1), part(2)]
        + [pl.BlockSpec((rows + EXTRA, LANES), lambda i, adapter, at: (0, i + first))]
        + [fixed((HEADS // 2, 2, rows)), fixed((HEADS, rows)), table, table]
        + [part(3 * p + 1) for p in range(peers)]
        + [part(3 * p + 2) for p in range(peers)],
        [jax.ShapeDtypeStruct((3, rows, width), BF16)] + [pltpu.HBM((rows, width), F32)] * 2,
        (1, 2),
        before,
        pairs,
        peers,
        [],
        2 * rows * width * 4 * rows * (5 + 3 * peers),
        "own_back",
    )


def peer_back(at, own, peer, gp, cos, sin, dk, dv, pairs, before):
    rows = own.shape[1]
    peers = gp.shape[0]
    width = own.shape[0] // 3 * LANES
    first = pairs[0]

    def part(which):
        return pl.BlockSpec((1, rows, LANES), lambda i, adapter, at: (8 * which + first + i, 0, 0))

    column = pl.BlockSpec((rows, LANES), lambda i, adapter, at: (0, i + first))
    table = pl.BlockSpec((rows, LANES), lambda i, adapter, at: (at[0], 0), pipeline_mode=pl.Buffered(1))
    return attend_back(
        24,
        peer_back_kernel,
        at,
        (own, own, gp, gp, cos, sin, dk, dv) + (peer,) * peers,
        [
            part(1), part(2),
            pl.BlockSpec((peers, rows + EXTRA, LANES), lambda i, adapter, at: (0, 0, i + first)),
            fixed((peers, EXTRA, width)),
            table, table, column, column,
        ]
        + [part(3 * p) for p in range(peers)],
        [jax.ShapeDtypeStruct((3, rows, width), BF16)],
        (2, 0),
        before,
        pairs,
        peers,
        [pltpu.VMEM((peers, HEADS, rows), F32), pltpu.VMEM((peers, HEADS, rows), F32)],
        2 * rows * width * 4 * 4 * rows * peers,
        "peer_back",
    )


def qkv_grad_kernel(
    _adapter, at, g, low, x, gain, shift, up, stay_out, leave_out, rank_grad, pieces, sems
):
    width = x.shape[1]
    low_t = low[...].T
    total = None
    def put(first, grad):
        for p in range(width // LANES):
            cut = slice(p * LANES, (p + 1) * LANES)
            pieces[position(jnp.int32(first + p), at, 6), 0] = grad[:, cut].astype(BF16)

    for n in range(3):
        grad = g[(n + 2) % 3]
        put(n * (width // LANES), dot(low_t, grad))
        more = dot(grad, up[0, :, n * width : (n + 1) * width], NT)
        total = more if total is None else total + more
    rank = total.astype(BF16)
    rank_grad[...] = rank
    normed, _s = norm_rows(x[...].astype(F32))
    h1 = (normed * gain[...] + shift[...]).astype(BF16)
    put(3 * (width // LANES), dot(rank.T, h1))
    leave = group(
        sems, [(pieces.at[pl.ds(0, 16)], stay_out), (pieces.at[pl.ds(16, 16)], leave_out)]
    )
    start_all(leave)
    wait_all(leave)


def qkv_grad(at, g, low, x, gain, shift, up, groups):
    rows, width = x.shape
    return pl.pallas_call(
        qkv_grad_kernel,
        grid_spec=pltpu.PrefetchScalarGridSpec(
            num_scalar_prefetch=2,
            grid=(1,),
            in_specs=[
                whole((3, rows, width)),
                whole((rows, RANK)),
                whole((rows, width)),
                whole((1, width)),
                whole((1, width)),
                chosen((RANK, 3 * width)),
            ],
            out_specs=[ANY, ANY, whole((rows, RANK))],
            scratch_shapes=[
                pltpu.VMEM((groups, 1, RANK, LANES), BF16),
                pltpu.SemaphoreType.DMA((2,)),
            ],
        ),
        out_shape=[
            jax.ShapeDtypeStruct((groups // 2, 1, RANK, LANES), BF16),
            jax.ShapeDtypeStruct((groups // 2, 1, RANK, LANES), BF16),
            jax.ShapeDtypeStruct((rows, RANK), BF16),
        ],
        compiler_params=params(16),
        cost_estimate=cost(2 * rows * 16 * 3 * width * 4, 8 * rows * width),
        name="qkv_grad",
    )(*at, g, low, x, gain, shift, up)


def input_grad_kernel(_adapter, at, g, w, rank_grad, down, x, gain, dx1, *refs):
    out, total = refs[-2:]
    j = pl.program_id(0)

    @pl.when(j == 0)
    def _():
        total[...] = dot(rank_grad[...], down[0]) + dot(g[0], w[...], NT)

    @pl.when(j == 1)
    def _():
        total[...] += dot(g[0], w[...], NT)

    @pl.when(j == 2)
    def _():
        grad = total[...] + dot(g[0], w[...], NT)
        normed, spread = norm_rows(x[...].astype(F32))
        out[...] = dx1[...] + norm_back(grad, normed, spread, gain[...])


def input_grad(at, g, w, rank_grad, down, x, gain, dx1, half, before=()):
    rows, width = x.shape
    cut = rows // 2
    part = pl.BlockSpec((cut, width), lambda j, adapter, at: (half, 0))
    order = lambda j: lax.rem(j + 1, 3)
    return pl.pallas_call(
        input_grad_kernel,
        grid_spec=pltpu.PrefetchScalarGridSpec(
            num_scalar_prefetch=2,
            grid=(3,),
            in_specs=[
                pl.BlockSpec((1, cut, width), lambda j, adapter, at: (j, half, 0)),
                pl.BlockSpec((width, width), lambda j, adapter, at: (0, order(j))),
                pl.BlockSpec((cut, RANK), lambda j, adapter, at: (half, 0)),
                chosen((RANK, width)),
                part,
                fixed((1, width)),
                part,
            ]
            + [ANY] * len(before),
            out_specs=part,
            scratch_shapes=[pltpu.VMEM((cut, width), F32)],
        ),
        out_shape=jax.ShapeDtypeStruct((rows, width), F32),
        input_output_aliases={9 + n: n for n in range(len(before))},
        compiler_params=params(20),
        cost_estimate=cost(3 * rows * width * width, 6 * width * width + 8 * rows * width),
        name="input_grad",
    )(*at, g, w, rank_grad, down, x, gain, dx1, *before)


def swap_order():
    bits = []
    n = 4
    while n < lax.axis_size("dp"):
        bits.append((n, 0))
        n *= 2
    n = 1
    while n < lax.axis_size("seq"):
        bits.append((0, n))
        n *= 2
    bits.append((2, 0))
    first = bits[:4]
    second = [first[1], first[0], first[3], first[2]]
    return (first, second), bits[4:]


def swap(values, step):
    size, ways = lax.axis_size("dp"), lax.axis_size("seq")
    perm = []
    for d in range(size):
        flip_d, flip_s = step[d & 1]
        for s in range(ways):
            perm.append((d * ways + s, (d ^ flip_d) * ways + (s ^ flip_s)))
    return lax.ppermute(values, ("dp", "seq"), perm)


def device_codes():
    orders, _rest = swap_order()
    size, ways = lax.axis_size("dp"), lax.axis_size("seq")
    table = np.zeros((size * ways, 9 + ways), np.int32)
    for d in range(size):
        for s in range(ways):
            codes = []
            for order in orders:
                on = [((d & bit_d) | (s & bit_s)) != 0 for bit_d, bit_s in order]
                codes.append(
                    (
                        sum(8 >> n for n in range(4) if on[n]),
                        sum(1 << n for n in range(4) if on[n]),
                        8 * on[2] + 4 * on[3],
                    )
                )
            mine, theirs = codes[d & 1], codes[1 - (d & 1)]
            row = [s, d & 1, mine[0], theirs[0], mine[1], theirs[1], mine[2], theirs[2], d]
            table[d * ways + s] = row + [(s + n) % ways for n in range(1, ways)] + [0]
    place = lax.axis_index("dp") * ways + lax.axis_index("seq")
    return lax.dynamic_slice_in_dim(jnp.asarray(table), place, 1, 0)[0]


def slot_masks(sequence):
    orders, _rest = swap_order()
    masks = []
    for order in orders:
        slots = [0, 1]
        for n in sequence:
            slots = slots + [slot ^ order[n][0] for slot in slots]
        masks.append(slots)
    return masks


def scatter_steps():
    orders, _rest = swap_order()
    return [((1, 0), (1, 0))] + list(zip(*orders))


def scatter_stage(held, step):
    half = held.shape[1] // 2
    return jnp.concatenate([held[:, :half], swap(held[:, half:], step)], axis=0)


def owner_sum_kernel(owners, at, held, out, total, *, masks):
    total[...] = jnp.zeros_like(total)
    for n, (even, odd) in enumerate(zip(*masks)):
        mask = even if even == odd else jnp.where(at[1] == 0, even, odd)
        total[owners[at[8] ^ mask]] += held[n].astype(F32)
    for a in range(NADAPT):
        out[:, a] = total[a].astype(BF16)


def owner_sum(at, owners, held, masks):
    slots, groups, parts, rank, lanes = held.shape
    pieces = groups * parts
    held = held.reshape(slots, pieces, rank, lanes)
    step = min(pieces, 4)
    out = pl.pallas_call(
        functools.partial(owner_sum_kernel, masks=masks),
        grid_spec=pltpu.PrefetchScalarGridSpec(
            num_scalar_prefetch=2,
            grid=(pieces // step,),
            in_specs=[pl.BlockSpec((slots, step, rank, lanes), lambda i, *_: (0, i, 0, 0))],
            out_specs=pl.BlockSpec((step, NADAPT, rank, lanes), lambda i, *_: (i, 0, 0, 0)),
            scratch_shapes=[pltpu.VMEM((NADAPT, step, rank, lanes), F32)],
        ),
        out_shape=jax.ShapeDtypeStruct((pieces, NADAPT, rank, lanes), BF16),
        compiler_params=params(12),
        cost_estimate=cost(held.size, 2 * held.size),
        name="owner_sum",
    )(owners, at[1], held)
    out = out.reshape(groups, parts, NADAPT, rank, lanes)
    _orders, rest = swap_order()
    for bits in rest:
        out = (out.astype(F32) + swap(out, (bits, bits)).astype(F32)).astype(BF16)
    return out


def spread_kernel(_adapter, at, mine, theirs, *outs, plan, straight):
    for core in range(2):

        @pl.when(at[1] == core)
        def _():
            for ref, part, first, count in zip(outs, *plan):
                for p in range(count):
                    piece = first + p
                    near = piece >> 4 == core
                    held = mine if near else theirs
                    if straight:
                        low = (piece & 15) ^ (at[6] if near else at[7])
                    else:
                        low = int(f"{piece & 15:04b}"[::-1], 2) ^ (at[4] if near else at[5])
                    ref[:, :, p * LANES : (p + 1) * LANES] = held[low, part].astype(F32)


def spread(at, mine, theirs, plan, straight=False):
    parts, firsts, counts = plan
    shapes = [(NADAPT, RANK, count * LANES) for count in counts]
    return pl.pallas_call(
        functools.partial(spread_kernel, plan=plan, straight=straight),
        grid_spec=pltpu.PrefetchScalarGridSpec(
            num_scalar_prefetch=2,
            grid=(1,),
            in_specs=[whole(mine.shape), whole(theirs.shape)],
            out_specs=[whole(shape) for shape in shapes],
        ),
        out_shape=[jax.ShapeDtypeStruct(shape, F32) for shape in shapes],
        compiler_params=params(20),
        cost_estimate=cost(1, 12 * mine.size),
        name="spread",
    )(*at, mine, theirs)


def tie(*values):
    flat, tree = jax.tree.flatten(values)
    return jax.tree.unflatten(tree, lax.optimization_barrier(flat))


def body(
    clip_tokens, adapter_index, ln1_gain, ln1_bias, qkv_weight, qkv_bias, qkv_down, qkv_up,
    out_weight, out_bias, out_down, out_up, ln2_gain, ln2_bias, fc1_weight, fc1_bias, fc1_down,
    fc1_up, fc2_weight, fc2_bias, fc2_down, fc2_up, cotangent,
):
    _one, rows, width = clip_tokens.shape
    devices = lax.axis_size("seq")
    groups = 32
    pin = lambda v: pltpu.with_memory_space_constraint(v, pltpu.HBM)
    row = lambda v: pin(v.reshape(1, -1))
    x = pin(clip_tokens[0])
    cot = cotangent[0]
    free_qkv, free_fc2 = qkv_weight, fc2_weight
    qkv_weight, qkv_down, qkv_up = pin(qkv_weight), pin(qkv_down), pin(qkv_up)
    out_weight, out_down, out_up = pin(out_weight), pin(out_down), pin(out_up)
    fc1_weight, fc1_down, fc1_up = pin(fc1_weight), pin(fc1_down), pin(fc1_up)
    fc2_weight, fc2_down, fc2_up = pin(fc2_weight), pin(fc2_down), pin(fc2_up)
    peers = range(1, devices)
    at = (adapter_index, device_codes())
    tagged = jnp.broadcast_to(adapter_index.astype(BF16)[:, None], (256, LANES))
    tagged, cot = tie(tagged, cot)
    tags = lax.all_gather(tagged, "dp", axis=0, tiled=True)
    masks_a, masks_b = slot_masks((0, 1, 2, 3)), slot_masks((2, 3, 0, 1))

    def from_peer(values, shift):
        return lax.ppermute(values, "seq", [((n + shift) % devices, n) for n in range(devices)])

    tables = tuple(pin(jnp.asarray(t)) for t in rotary_tables(rows * devices))
    cos, sin = tables
    x_peer = jnp.concatenate([from_peer(clip_tokens[0], n) for n in peers], axis=0)
    first_set = (row(ln1_gain), row(ln1_bias), qkv_weight, row(qkv_bias), qkv_down, qkv_up)
    own, mixed, back, low_qkv, top, total, grad2 = front_rows(
        at, x, pin(cot), first_set, tables, fc2_weight, fc2_down, fc2_up
    )
    peer, act, x1, low2, dx1, go, delta, lse, *pieces_a = middle_rows(
        at, x_peer, first_set, tables, own, (mixed, top, total), x, pin(cot), back, grad2,
        (out_weight, row(out_bias), out_down, out_up),
        (row(ln2_gain), row(ln2_bias)),
        (fc1_weight, row(fc1_bias), fc1_down, fc1_up),
        fc2_down, groups,
    )
    own, peer, lse = pin(own), pin(peer), pin(lse)
    go_sent, kept, sent, delta, tags = tie(go, pieces_a[0][None], pieces_a[1][None], delta, tags)
    index_all = tags[::256, 0].astype(jnp.int32)
    go_peer = jnp.stack([from_peer(go_sent, n) for n in peers])
    steps = scatter_steps()

    def halves(held):
        half = held.shape[1] // 2
        return held[:, :half], held[:, half:]

    def join(*parts):
        return jnp.concatenate(parts, axis=0)

    arrived = swap(sent, steps[0])
    kept, sent = halves(join(kept, arrived))
    sent, delta = tie(sent, delta)
    arrived = swap(sent, steps[1])
    back = functools.partial(own_back, at, own, peer, pin(go), lse, pin(delta), cos, sin)
    grads = back((0, 4), None)
    arrived, grads = tie(arrived, grads)
    kept, sent = halves(join(kept, arrived))
    sent, grads = tie(sent, grads)
    arrived = swap(sent, steps[2])
    grads, dk, dv = back((4, 4), grads)
    arrived, dk, go_peer = tie(arrived, dk, go_peer)
    dk, dv = pin(dk), pin(dv)
    kept, sent = halves(join(kept, arrived))
    sent, go_peer = tie(sent, go_peer)
    arrived = swap(sent, steps[3])
    grads = peer_back(at, own, peer, go_peer, cos, sin, dk, dv, (0, 8), (grads,))[0]
    arrived, grads = tie(arrived, grads)
    kept_a, sent = halves(join(kept, arrived))
    sent, grads = tie(sent, grads)
    arrived_a = swap(sent, steps[4])
    kept, sent, rank_grad = qkv_grad(
        at, grads, low_qkv, x, row(ln1_gain), row(ln1_bias), qkv_up, groups
    )
    arrived_a, sent, rank_grad = tie(arrived_a, sent, rank_grad)
    held = join(kept[None], swap(sent[None], steps[0]))
    total_a = owner_sum(at, index_all, join(kept_a, arrived_a), masks_a)

    def grad_half(half, rank_grad, before=()):
        return input_grad(
            at, grads, free_qkv, rank_grad, qkv_down, x, row(ln1_gain), pin(dx1), half, before
        )

    def output_half(half, low2, before=()):
        return output_rows(at, pin(act), free_fc2, pin(x1), row(fc2_bias), low2, fc2_up, half, before)

    kept, sent = halves(held)
    arrived = swap(sent, steps[3])
    sent, total_a, rank_grad = tie(sent, total_a, rank_grad)
    arrived_a = swap(total_a, steps[1])
    grad_in = grad_half(0, rank_grad)
    arrived, arrived_a, rank_grad, grad_in = tie(arrived, arrived_a, rank_grad, grad_in)
    kept, sent = halves(join(kept, arrived))
    total_a = join(total_a, arrived_a)
    sent, total_a, rank_grad = tie(sent, total_a, rank_grad)
    arrived = swap(sent, steps[4])
    arrived_a = swap(total_a, steps[2])
    grad_in = grad_half(1, rank_grad, (grad_in,))
    arrived, arrived_a, grad_in = tie(arrived, arrived_a, grad_in)
    held, total_a = join(kept, arrived), join(total_a, arrived_a)
    held, total_a, low2 = tie(held, total_a, low2)
    arrived = swap(held, steps[1])
    arrived_a = swap(total_a, steps[3])
    block_output = output_half(0, low2)
    arrived, arrived_a, low2, block_output = tie(arrived, arrived_a, low2, block_output)
    held, total_a = join(held, arrived), join(total_a, arrived_a)
    held, total_a, low2 = tie(held, total_a, low2)
    arrived = swap(held, steps[2])
    arrived_a = swap(total_a, steps[4])
    block_output = output_half(1, low2, (block_output,))
    arrived, block_output = tie(arrived, block_output)
    total_b = owner_sum(at, index_all, join(held, arrived), masks_b)
    total_b, arrived_a = tie(total_b, arrived_a)
    total_a = join(total_a, arrived_a)
    arrived = swap(total_b, steps[4])
    theirs_a = swap(total_a, steps[0])
    total_b = join(total_b, arrived)
    total_b, total_a, theirs_a = tie(total_b, total_a, theirs_a)
    arrived = swap(total_b, steps[3])
    per = width // LANES
    spread_a = spread(
        at, total_a, theirs_a,
        ((0, 1, 2, 2, 2, 2), (0, 0, 0, per, 2 * per, 3 * per), (32, 32, per, per, per, per)),
    )
    arrived, spread_a = tie(arrived, spread_a)
    up1, down2, up2, down1, up_o, down_o = spread_a
    total_b = join(total_b, arrived)
    up_qkv, down_qkv = spread(
        at, total_b, swap(total_b, steps[0]), ((0, 0), (0, 3 * per), (3 * per, per)), straight=True
    )
    return (
        block_output[None], grad_in[None], down_qkv, up_qkv, down_o, up_o, down1, up1, down2, up2,
    )


def solution(mesh):
    split = P("dp", "seq", None)
    return jax.shard_map(
        body,
        mesh=mesh,
        in_specs=(split, P("dp")) + (P(),) * 20 + (split,),
        out_specs=(split, split) + (P(),) * 8,
        check_vma=False,
    )
```

```python
import functools

import jax
import jax.numpy as jnp
import numpy as np
from jax import lax
from jax.experimental import pallas as pl
from jax.experimental.pallas import tpu as pltpu
from jax.sharding import PartitionSpec as P

HEADS = 16
HD = 64
GRID = 16
NADAPT = 8
RANK = 16
EPSILON = 1e-06
LANES = 128
EXTRA = 48

F32 = jnp.float32
BF16 = jnp.bfloat16
NN = (((1,), (0,)), ((), ()))
NT = (((1,), (1,)), ((), ()))

ERFC = (
    0.16918800211151383,
    0.1707152747822528,
    0.14833885959986734,
    0.21492717178376733,
    -0.09465313901935662,
    0.5477232747113128,
    -0.5122807406271995,
    0.48556441585520754,
    -0.1295231387829952,
)


def dot(a, b, dims=NN):
    return lax.dot_general(a, b, dims, preferred_element_type=F32)


def params(megabytes):
    return pltpu.CompilerParams(
        dimension_semantics=("arbitrary",), vmem_limit_bytes=megabytes << 20
    )


def cost(flops, moved, exps=0):
    return pl.CostEstimate(flops=int(flops), bytes_accessed=int(moved), transcendentals=int(exps))


def norm_rows(values):
    centre = values - jnp.mean(values, axis=-1, keepdims=True)
    spread = lax.rsqrt(jnp.mean(centre * centre, axis=-1, keepdims=True) + EPSILON)
    return centre * spread, spread


def norm_back(grad_rows, normed, spread, gain):
    scaled = grad_rows * gain
    first = jnp.mean(scaled, axis=-1, keepdims=True)
    second = jnp.mean(scaled * normed, axis=-1, keepdims=True)
    return spread * (scaled - first - normed * second)


def rotary_tables(length):
    half = HD // 2
    side = half // 3
    lead = half - 2 * side
    token = np.arange(length)
    pair = np.arange(half)
    kind = np.where(pair < lead, 0, np.where(pair < lead + side, 1, 2))
    local = np.where(kind == 0, pair, np.where(kind == 1, pair - lead, pair - lead - side))
    total = np.where(kind == 0, lead, side)
    frequency = np.power(
        np.float32(10000.0), -local.astype(np.float32) / total.astype(np.float32)
    ).astype(np.float32)
    place = np.where(
        kind[None] == 0,
        (token // (GRID * GRID))[:, None],
        np.where(kind[None] == 1, (token // GRID % GRID)[:, None], (token % GRID)[:, None]),
    ).astype(np.float32)
    angle = place * frequency[None]
    cosine, sine = np.cos(angle), np.sin(angle)
    cos_rows = np.concatenate([cosine] * 4, axis=1).astype(np.float32)
    sin_rows = np.concatenate([-sine, sine, -sine, sine], axis=1).astype(np.float32)
    return cos_rows, sin_rows


def swap_halves(values):
    lane = lax.broadcasted_iota(jnp.int32, (1, LANES), 1)
    low = (lane & (HD // 2)) == 0
    return jnp.where(
        low, pltpu.roll(values, LANES - HD // 2, 1), pltpu.roll(values, HD // 2, 1)
    )


def head_mask(values, head):
    lane = lax.broadcasted_iota(jnp.int32, (1, LANES), 1)
    keep = (lane < HD) if head == 0 else (lane >= HD)
    return jnp.where(keep, values, jnp.zeros_like(values))


def whole(shape):
    return pl.BlockSpec(shape, lambda *_: (0,) * len(shape))


def fixed(shape):
    return pl.BlockSpec(shape, lambda *_: (0,) * len(shape), pipeline_mode=pl.Buffered(1))


def chosen(shape):
    return pl.BlockSpec((1,) + shape, lambda *ids: (ids[-2][0], 0, 0))


def chosen_tile(tile, which):
    return pl.BlockSpec((1, RANK, tile), lambda j, adapter, at: (adapter[0], 0, which(j)))


def position(piece, at, first=2):
    top = (piece >> 4) ^ at[1]
    return 16 * top + ((piece & 15) ^ jnp.where(top == 0, at[first], at[first + 1]))


CHUNK = 256


def qkv_tile(tile, h1, low, w, bias, up, cos, sin, out_ref, keep, first):
    scale = jnp.where(tile == 0, HD**-0.5, 1.0).astype(F32)
    turn = jnp.where(tile == 2, 0.0, 1.0).astype(F32)
    c = (cos[...] * turn + (1.0 - turn)) * scale
    s = sin[...] * (turn * scale)

    def chunk(n):
        cut = slice(n * CHUNK, (n + 1) * CHUNK)
        return dot(h1, w[:, cut]) + bias[:, cut] + dot(low, up[:, cut])

    count = w.shape[1] // CHUNK
    now = chunk(0)
    parts = []
    for n in range(count):
        later = chunk(n + 1) if n + 1 < count else None
        for g in range(CHUNK // LANES):
            part = now[:, g * LANES : (g + 1) * LANES]
            parts.append((part * c + swap_halves(part) * s).astype(BF16))
        now = later
    for n, part in enumerate(parts):
        out_ref[n] = part
        keep[first + n] = part


def attend_pairs(count, load, finish):
    loaded = [load(pair) for pair in range(count)]
    values_t = [v.T for _q, _k, v in loaded]

    def scores(item):
        pair, head = item
        q, k, _v = loaded[pair]
        return dot(k, head_mask(q, head), NT)

    items = [(pair, head) for pair in range(count) for head in range(2)]
    now = scores(items[0])
    for n, (pair, head) in enumerate(items):
        later = scores(items[n + 1]) if n + 1 < len(items) else None
        finish(pair, head, now, values_t[pair][head * HD : (head + 1) * HD])
        now = later


STEP_PAIRS = 4


def start_all(*groups):
    for group in groups:
        for copy in group:
            copy.start()


def wait_all(*groups):
    for group in groups:
        for copy in group:
            copy.wait()


def group(sems, pairs):
    return [pltpu.make_async_copy(a, b, sems.at[n]) for n, (a, b) in enumerate(pairs)]


def tiles(source, kept, size):
    return [(source.at[:, pl.ds(n * size, size)], kept.at[n]) for n in range(kept.shape[0])]


def front_kernel(
    adapter, at, x, w, w2,
    gain, shift, bias, down, up, cos, sin, cot, down2, up2,
    qkv, mixed_out, back, low, top_out, total_out, grad2,
    h1, keep, gain_k, shift_k, bias_k, down_k, up_k, cos_k, sin_k, cot_k, down2_k, up2_k,
    low_k, top_k, total_k, grad2_k, sem_a, sem_b, sem_c, sem_d,
    *, starts,
):
    j = pl.program_id(0)
    second, third = starts
    last = pl.num_programs(0) - 1
    mine = adapter[0]
    rows, width = x.shape
    place = pl.ds(pl.multiple_of(at[0] * rows, rows), rows)
    early = group(
        sem_a,
        [
            (gain, gain_k), (shift, shift_k), (down.at[mine], down_k),
            (cos.at[place], cos_k), (sin.at[place], sin_k),
        ]
        + tiles(bias, bias_k, width)
        + tiles(up.at[mine], up_k, width),
    )
    late = group(
        sem_b, [(cot, cot_k), (up2.at[mine], up2_k)] + tiles(down2.at[mine], down2_k, w2.shape[0])
    )
    stats = group(sem_c, [(low_k, low), (top_k, top_out), (total_k, total_out)])
    end = group(sem_d, [(grad2_k, grad2)])

    @pl.when(j == 0)
    def _():
        start_all(early, late)
        normed, _s = norm_rows(x[...].astype(F32))
        wait_all(early)
        held = (normed * gain_k[...] + shift_k[...]).astype(BF16)
        h1[...] = held
        low_k[...] = dot(held, down_k[...], NT).astype(BF16)

    @pl.when(j < second)
    def _():
        qkv_tile(j, h1[...], low_k[...], w, bias_k[j], up_k[j], cos_k, sin_k, qkv, keep, 8 * j)

    @pl.when((j >= second) & (j < third))
    def _():
        first = (j - second) * STEP_PAIRS

        def load(pair):
            return keep[first + pair], keep[8 + first + pair], keep[16 + first + pair]

        def finish(pair, head, scores, values_t):
            top = jnp.max(scores, axis=0, keepdims=True)
            weights = jnp.exp(scores - top)
            start = pair * LANES + head * HD
            mixed_out[start : start + HD, :] = dot(values_t, weights.astype(BF16))
            top_k[first + pair, head : head + 1, :] = top
            total_k[first + pair, head : head + 1, :] = jnp.sum(weights, axis=0, keepdims=True)

        attend_pairs(STEP_PAIRS, load, finish)

    @pl.when(j == third)
    def _():
        start_all(stats)
        wait_all(late)
        grad2_k[...] = dot(cot_k[...], up2_k[...], NT).astype(BF16)
        start_all(end)

    @pl.when(j >= third)
    def _():
        side = dot(grad2_k[...], down2_k[j - third])
        back[...] = (dot(cot_k[...], w2[...], NT) + side).astype(BF16)

    @pl.when(j == last)
    def _():
        wait_all(stats, end)


def clip(value, low, high):
    return jnp.minimum(jnp.maximum(value, low), high)


ANY = pl.BlockSpec(memory_space=pl.ANY)


def front_rows(at, x, cot, first_set, tables, w2, down2, up2):
    gain, shift, w, bias, down, up = first_set
    rows, width = x.shape
    ff = w2.shape[0]
    tile = 1024
    second = w.shape[1] // width
    third = second + HEADS // 2 // STEP_PAIRS
    steps = third + ff // tile
    one = lambda j: jnp.minimum(j, second - 1)
    two = lambda j: clip(j - second, 0, third - second - 1)
    three = lambda j: clip(j - third, 0, steps - third - 1)
    stat = (HEADS // 2, 2, rows)
    return pl.pallas_call(
        functools.partial(front_kernel, starts=(second, third)),
        grid_spec=pltpu.PrefetchScalarGridSpec(
            num_scalar_prefetch=2,
            grid=(steps,),
            in_specs=[
                fixed((rows, width)),
                pl.BlockSpec((width, width), lambda j, adapter, at: (0, one(j))),
                pl.BlockSpec((tile, width), lambda j, adapter, at: (three(j), 0)),
            ]
            + [ANY] * 10,
            out_specs=[
                pl.BlockSpec((8, rows, LANES), lambda j, adapter, at: (one(j), 0, 0)),
                pl.BlockSpec((STEP_PAIRS * LANES, rows), lambda j, adapter, at: (two(j), 0)),
                pl.BlockSpec((rows, tile), lambda j, adapter, at: (0, three(j))),
            ]
            + [ANY] * 4,
            scratch_shapes=[
                pltpu.VMEM((rows, width), BF16),
                pltpu.VMEM((24, rows, LANES), BF16),
                pltpu.VMEM((1, width), F32),
                pltpu.VMEM((1, width), F32),
                pltpu.VMEM((second, 1, width), F32),
                pltpu.VMEM((RANK, width), BF16),
                pltpu.VMEM((second, RANK, width), BF16),
                pltpu.VMEM((rows, LANES), F32),
                pltpu.VMEM((rows, LANES), F32),
                pltpu.VMEM((rows, width), BF16),
                pltpu.VMEM((ff // tile, RANK, tile), BF16),
                pltpu.VMEM((RANK, width), BF16),
                pltpu.VMEM((rows, RANK), BF16),
                pltpu.VMEM(stat, F32),
                pltpu.VMEM(stat, F32),
                pltpu.VMEM((rows, RANK), BF16),
                pltpu.SemaphoreType.DMA((5 + 2 * second,)),
                pltpu.SemaphoreType.DMA((2 + ff // tile,)),
                pltpu.SemaphoreType.DMA((3,)),
                pltpu.SemaphoreType.DMA((1,)),
            ],
        ),
        out_shape=[
            pltpu.HBM((24, rows, LANES), BF16),
            pltpu.HBM((width, rows), F32),
            pltpu.HBM((rows, ff), BF16),
            pltpu.HBM((rows, RANK), BF16),
            pltpu.HBM(stat, F32),
            pltpu.HBM(stat, F32),
            pltpu.HBM((rows, RANK), BF16),
        ],
        compiler_params=params(44),
        cost_estimate=cost(
            2 * rows * width * (3 * width + ff) + 16 * rows * rows * width, 20 << 20, 16 * rows * rows
        ),
        name="front_rows",
    )(*at, x, w, w2, gain, shift, bias, down, up, *tables, cot, down2, up2)


def gelu_both(f):
    z = jnp.abs(f) * (0.5**0.5)
    t = 1.0 / (1.0 + 0.3 * z)
    poly = ERFC[-1]
    for c in ERFC[-2::-1]:
        poly = poly * t + c
    bell = jnp.exp(f * f * -0.5)
    tail = (0.5 * poly) * t * bell
    phi = jnp.where(f < 0, tail, 1.0 - tail)
    return f * phi, phi + f * (bell * 0.3989422804014327)


def middle_kernel(
    adapter, at, xp, wq, w1, back,
    gain1, shift1, bq, downq, upq, cos, sin, own, mixed, top, total,
    x, cot, grad2, w_out, b_out, out_down, out_up, gain, shift, b1, down1, up1, down2,
    qkv, act_out, x1_out, low2_out, dx1_out, go_out, delta_out, lse_out, stay_out, leave_out,
    h1, lowq, keep, o, h2, dh2, low_o, low1, low1_t, grad2_t, low2, grad1,
    gain1_k, shift1_k, bq_k, downq_k, upq_k, cos_k, sin_k, q_own, mixed_in, top_in, total_in,
    x_k, cot_k, grad2_k, w_out_k, b_out_k, out_down_k, out_up_k, gain_k, shift_k, b1_k, down1_k, up1_k, down2_k,
    x1, low2_k, dx1_k, go, delta_k, lse, pieces,
    sem_a, sem_b, sem_c, sem_d, sem_e,
    *, starts, peers,
):
    j = pl.program_id(0)
    second, third = starts
    last = pl.num_programs(0) - 1
    rows, width = xp.shape
    tile = w1.shape[1]
    mine = adapter[0]
    places = [pl.ds(pl.multiple_of(at[9 + p] * rows, rows), rows) for p in range(peers)]
    early = group(
        sem_a,
        [(gain1, gain1_k), (shift1, shift1_k), (downq.at[mine], downq_k)]
        + [(cos.at[places[p]], cos_k.at[p]) for p in range(peers)]
        + [(sin.at[places[p]], sin_k.at[p]) for p in range(peers)]
        + tiles(bq, bq_k, width)
        + tiles(upq.at[mine], upq_k, width),
    )
    later = group(
        sem_b, [(own.at[pl.ds(0, 8)], q_own), (mixed, mixed_in), (top, top_in), (total, total_in)]
    )
    late = group(
        sem_c,
        [
            (x, x_k), (cot, cot_k), (grad2, grad2_k), (w_out, w_out_k), (b_out, b_out_k),
            (out_down.at[mine], out_down_k), (out_up.at[mine], out_up_k), (gain, gain_k),
            (shift, shift_k), (down1.at[mine], down1_k),
        ]
        + tiles(b1, b1_k, tile)
        + tiles(up1.at[mine], up1_k, tile)
        + tiles(down2.at[mine], down2_k, tile),
    )
    middle_out = group(sem_d, [(x1, x1_out), (lse, lse_out)])
    end = group(
        sem_e,
        [(low2_k, low2_out), (dx1_k, dx1_out), (go, go_out), (delta_k, delta_out)]
        + [(pieces.at[pl.ds(0, 16)], stay_out), (pieces.at[pl.ds(16, 16)], leave_out)],
    )

    @pl.when(j == 0)
    def _():
        start_all(early, later, late)

    @pl.when(j < second)
    def _():
        which, p = j // peers, lax.rem(j, peers)

        @pl.when(which == 0)
        def _():
            normed, _s = norm_rows(xp[...].astype(F32))

            @pl.when(j == 0)
            def _():
                wait_all(early)

            normed = (normed * gain1_k[...] + shift1_k[...]).astype(BF16)
            h1[p] = normed
            lowq[p] = dot(normed, downq_k[...], NT).astype(BF16)

        qkv_tile(
            which, h1[p], lowq[p], wq, bq_k[which], upq_k[which], cos_k.at[p], sin_k.at[p],
            qkv, keep, 24 * p + 8 * which,
        )

    @pl.when(j == second)
    def _():
        wait_all(later)

    @pl.when((j >= second) & (j < third))
    def _():
        first = (j - second) * STEP_PAIRS
        held = []

        def load(pair):
            n = first + pair
            k = [keep[24 * p + 8 + n] for p in range(peers)]
            v = [keep[24 * p + 16 + n] for p in range(peers)]
            if peers > 1:
                k, v = [jnp.concatenate(k, axis=0)], [jnp.concatenate(v, axis=0)]
            return q_own[n], k[0], v[0]

        def finish(pair, head, scores, values_t):
            n = first + pair
            before = top_in[n, head : head + 1, :]
            top = jnp.maximum(jnp.max(scores, axis=0, keepdims=True), before)
            scale = jnp.exp(before - top)
            weights = jnp.exp(scores - top)
            total = jnp.sum(weights, axis=0, keepdims=True)
            total = total + scale * total_in[n, head : head + 1, :]
            start = pl.ds(pl.multiple_of(n * LANES + head * HD, HD), HD)
            mixed = dot(values_t, weights.astype(BF16)) + scale * mixed_in[start, :]
            held.append(mixed * (1.0 / total))
            lse[n, head : head + 1, :] = top + jnp.log(total)
            if head == 1:
                o[n] = jnp.concatenate(held[-2:], axis=0).T.astype(BF16)

        attend_pairs(STEP_PAIRS, load, finish)

    def put(first, slot, grad):
        for p in range(grad.shape[1] // LANES):
            cut = slice(p * LANES, (p + 1) * LANES)
            pieces[position(first + p, at), slot] = grad[:, cut].astype(BF16)

    @pl.when(j == third)
    def _():
        wait_all(late)
        mixed = jnp.concatenate([o[n] for n in range(HEADS // 2)], axis=1)
        low = dot(mixed, out_down_k[...], NT).astype(BF16)
        low_o[...] = low
        branch = dot(mixed, w_out_k[...]) + b_out_k[...] + dot(low, out_up_k[...])
        mid = x_k[...].astype(F32) + branch
        x1[...] = mid
        normed, _s = norm_rows(mid)
        rows2 = (normed * gain_k[...] + shift_k[...]).astype(BF16)
        h2[...] = rows2
        low_1 = dot(rows2, down1_k[...], NT).astype(BF16)
        low1[...] = low_1
        low1_t[...] = low_1.T
        grad2_t[...] = grad2_k[...].T
        dh2[...] = jnp.zeros_like(dh2)
        low2[...] = jnp.zeros_like(low2)
        grad1[...] = jnp.zeros_like(grad1)
        start_all(middle_out)

    @pl.when(j >= third)
    def _():
        n_tile = j - third

        def hidden(n):
            cut = slice(n * CHUNK, (n + 1) * CHUNK)
            return dot(h2[...], w1[:, cut]) + b1_k[n_tile, :, cut] + dot(low1[...], up1_k[n_tile, :, cut])

        first = n_tile * (tile // LANES)
        count = tile // CHUNK
        now = hidden(0)
        acts, dfs = [], []
        for n in range(count):
            later = hidden(n + 1) if n + 1 < count else None
            cut = slice(n * CHUNK, (n + 1) * CHUNK)
            act, slope = gelu_both(now)
            acts.append(act.astype(BF16))
            dfs.append((back[:, cut].astype(F32) * slope).astype(BF16))
            now = later
        act, df = jnp.concatenate(acts, axis=1), jnp.concatenate(dfs, axis=1)
        dh2[...] += dot(df, w1[...], NT)
        low2[...] += dot(act, down2_k[n_tile], NT)
        grad1[...] += dot(df, up1_k[n_tile], NT)
        act_out[...] = act
        put(first, 0, dot(low1_t[...], df))
        put(first, 1, dot(grad2_t[...], act))

    @pl.when(j == last)
    def _():
        low_2 = low2[...].astype(BF16)
        low2_k[...] = low_2
        g1 = grad1[...].astype(BF16)
        back2 = dh2[...] + dot(g1, down1_k[...])
        normed, spread = norm_rows(x1[...])
        dx1 = cot_k[...].astype(F32) + norm_back(back2, normed, spread, gain_k[...])
        dx1_k[...] = dx1
        da = dx1.astype(BF16)
        g_o = dot(da, out_up_k[...], NT).astype(BF16)
        new_go = (dot(da, w_out_k[...], NT) + dot(g_o, out_down_k[...])).astype(BF16)
        go[EXTRA : EXTRA + rows, :] = new_go
        mixed = jnp.concatenate([o[n] for n in range(HEADS // 2)], axis=1)
        product = new_go.astype(F32) * mixed.astype(F32)
        high = product.astype(BF16)
        rest = (product - high.astype(F32)).astype(BF16)
        lane = lax.broadcasted_iota(jnp.int32, (HEADS, width), 1)
        head = lax.broadcasted_iota(jnp.int32, (HEADS, width), 0)
        pick = (lane // HD == head).astype(BF16)
        delta = dot(pick, high, NT) + dot(pick, rest, NT)
        delta_k[...] = delta
        if rows < width // 2:
            go[0:EXTRA, :] = jnp.zeros((EXTRA, width), BF16)
        logs = jnp.concatenate([lse[n] for n in range(HEADS // 2)], axis=0)
        for side, stat in enumerate((logs, delta)):
            left = stat
            for n in range(3):
                part = left.astype(BF16)
                go[16 * n : 16 * n + 16, side * (width // 2) : side * (width // 2) + rows] = part
                left = left - part.astype(F32)
        start_all(end[:4])
        per = width // LANES
        put(jnp.int32(0), 2, dot(low_2.T, cot_k[...]))
        put(jnp.int32(per), 2, dot(g1.T, h2[...]))
        put(jnp.int32(2 * per), 2, dot(low_o[...].T, da))
        put(jnp.int32(3 * per), 2, dot(g_o.T, mixed))
        start_all(end[4:])
        wait_all(middle_out, end)


def middle_rows(
    at, xp, first_set, tables, own, state, x, cot, back, grad2, out_set, norm_set, fc1_set, down2, groups
):
    rows, width = x.shape
    peers = xp.shape[0] // rows
    w1 = fc1_set[0]
    ff = w1.shape[1]
    tile = 1024
    second = 3 * peers
    third = second + HEADS // 2 // STEP_PAIRS
    steps = third + ff // tile
    one = lambda j: jnp.minimum(j, second - 1) // peers
    peer = lambda j: lax.rem(jnp.minimum(j, second - 1), peers)
    two = lambda j: clip(j - second, 0, third - second - 1)
    three = lambda j: clip(j - third, 0, steps - third - 1)
    stat = (HEADS // 2, 2, rows)
    count = ff // tile
    vmem = pltpu.VMEM
    return pl.pallas_call(
        functools.partial(middle_kernel, starts=(second, third), peers=peers),
        grid_spec=pltpu.PrefetchScalarGridSpec(
            num_scalar_prefetch=2,
            grid=(steps,),
            in_specs=[
                pl.BlockSpec((rows, width), lambda j, adapter, at: (jnp.minimum(j, peers - 1), 0)),
                pl.BlockSpec((width, width), lambda j, adapter, at: (0, one(j))),
                pl.BlockSpec((width, tile), lambda j, adapter, at: (0, three(j))),
                pl.BlockSpec((rows, tile), lambda j, adapter, at: (0, three(j))),
            ]
            + [ANY] * 24,
            out_specs=[
                pl.BlockSpec((8, rows, LANES), lambda j, adapter, at: (3 * peer(j) + one(j), 0, 0)),
                pl.BlockSpec((rows, tile), lambda j, adapter, at: (0, three(j))),
            ]
            + [ANY] * 8,
            scratch_shapes=[
                vmem((peers, rows, width), BF16),
                vmem((peers, rows, RANK), BF16),
                vmem((24 * peers, rows, LANES), BF16),
                vmem((HEADS // 2, rows, LANES), BF16),
                vmem((rows, width), BF16),
                vmem((rows, width), F32),
                vmem((rows, RANK), BF16),
                vmem((rows, RANK), BF16),
                vmem((RANK, rows), BF16),
                vmem((RANK, rows), BF16),
                vmem((rows, RANK), F32),
                vmem((rows, RANK), F32),
                vmem((1, width), F32),
                vmem((1, width), F32),
                vmem((3, 1, width), F32),
                vmem((RANK, width), BF16),
                vmem((3, RANK, width), BF16),
                vmem((peers, rows, LANES), F32),
                vmem((peers, rows, LANES), F32),
                vmem((8, rows, LANES), BF16),
                vmem((width, rows), F32),
                vmem(stat, F32),
                vmem(stat, F32),
                vmem((rows, width), BF16),
                vmem((rows, width), BF16),
                vmem((rows, RANK), BF16),
                vmem((width, width), BF16),
                vmem((1, width), F32),
                vmem((RANK, width), BF16),
                vmem((RANK, width), BF16),
                vmem((1, width), F32),
                vmem((1, width), F32),
                vmem((count, 1, tile), F32),
                vmem((RANK, width), BF16),
                vmem((count, RANK, tile), BF16),
                vmem((count, RANK, tile), BF16),
                vmem((rows, width), F32),
                vmem((rows, RANK), BF16),
                vmem((rows, width), F32),
                vmem((EXTRA + rows, width), BF16),
                vmem((HEADS, rows), F32),
                vmem(stat, F32),
                vmem((groups, 3, RANK, LANES), BF16),
                pltpu.SemaphoreType.DMA((9 + 2 * peers,)),
                pltpu.SemaphoreType.DMA((4,)),
                pltpu.SemaphoreType.DMA((10 + 3 * count,)),
                pltpu.SemaphoreType.DMA((2,)),
                pltpu.SemaphoreType.DMA((6,)),
            ],
        ),
        out_shape=[
            pltpu.HBM((24 * peers, rows, LANES), BF16),
            pltpu.HBM((rows, ff), BF16),
            pltpu.HBM((rows, width), F32),
            pltpu.HBM((rows, RANK), BF16),
            pltpu.HBM((rows, width), F32),
            pltpu.HBM((EXTRA + rows, width), BF16),
            pltpu.HBM((HEADS, rows), F32),
            pltpu.HBM(stat, F32),
            pltpu.HBM((groups // 2, 3, RANK, LANES), BF16),
            pltpu.HBM((groups // 2, 3, RANK, LANES), BF16),
        ],
        compiler_params=params(56),
        cost_estimate=cost(
            4 * rows * width * ff + (4 + 6 * peers) * rows * width * width, 40 << 20, rows * ff
        ),
        name="middle_rows",
    )(
        *at, xp, first_set[2], w1, back,
        first_set[0], first_set[1], first_set[3], first_set[4], first_set[5], *tables, own, *state,
        x, cot, grad2, *out_set, *norm_set, *fc1_set[1:], down2,
    )


def output_kernel(_adapter, at, act, w2, x1, b2, low2, up2, *refs):
    out, y = refs[-2:]
    j = pl.program_id(0)
    last = pl.num_programs(0) - 1

    @pl.when(j == 0)
    def _():
        y[...] = dot(act[...], w2[...])

    @pl.when((j > 0) & (j < last))
    def _():
        y[...] += dot(act[...], w2[...])

    @pl.when(j == last)
    def _():
        side = b2[...] + dot(low2[...], up2[0])
        out[...] = (x1[...] + (y[...] + dot(act[...], w2[...]) + side)).astype(BF16)


def output_rows(at, act, w2, x1, b2, low2, up2, half, before=()):
    rows, ff = act.shape
    width = x1.shape[1]
    wide = width // 2
    tile = 1024
    part = pl.BlockSpec((rows, wide), lambda j, adapter, at: (0, half))
    return pl.pallas_call(
        output_kernel,
        grid_spec=pltpu.PrefetchScalarGridSpec(
            num_scalar_prefetch=2,
            grid=(ff // tile,),
            in_specs=[
                pl.BlockSpec((rows, tile), lambda j, adapter, at: (0, j)),
                pl.BlockSpec((tile, wide), lambda j, adapter, at: (j, half)),
                part,
                pl.BlockSpec((1, wide), lambda j, adapter, at: (0, half)),
                fixed((rows, RANK)),
                pl.BlockSpec((1, RANK, wide), lambda j, adapter, at: (adapter[0], 0, half)),
            ]
            + [ANY] * len(before),
            out_specs=part,
            scratch_shapes=[pltpu.VMEM((rows, wide), F32)],
        ),
        out_shape=jax.ShapeDtypeStruct((rows, width), BF16),
        input_output_aliases={8 + n: n for n in range(len(before))},
        compiler_params=params(24),
        cost_estimate=cost(rows * width * ff, width * ff + 2 * rows * ff),
        name="output_rows",
    )(*at, act, w2, x1, b2, low2, up2, *before)


def unrotate(values, cos, sin):
    return values * cos[...] - swap_halves(values) * sin[...]


def score_grads(s, dp, lse, delta):
    prob = jnp.exp(s - lse)
    return prob.astype(BF16), (prob * (dp - delta)).astype(BF16)


def own_back_kernel(_adapter, at, q0, k0, v0, go, lse0, delta0, cos, sin, *refs, first_pair, peers):
    k1, v1 = refs[:peers], refs[peers : 2 * peers]
    dq, dk, dv = refs[-3:]
    i = pl.program_id(0) + first_pair
    rows = q0.shape[1]
    keys = jnp.concatenate([k0[0]] + [k[0] for k in k1], axis=0)
    values = jnp.concatenate([v0[0]] + [v[0] for v in v1], axis=0)
    keys_t = keys.T

    def first(head):
        q = head_mask(q0[0], head)
        g = head_mask(go[EXTRA : EXTRA + rows, :], head)
        return dot(keys, q, NT), dot(values, g, NT), q, g

    grad_q = []
    now = first(0)
    for head in range(2):
        later = first(1) if head == 0 else None
        s, dp, q, g = now
        row = pl.ds(2 * i + head, 1)
        prob, ds = score_grads(s, dp, lse0[i, head : head + 1, :], delta0[row, :])
        grad_q.append(dot(keys_t[head * HD : (head + 1) * HD], ds))
        more_v = dot(prob[:rows], g)
        more_k = dot(ds[:rows], q)
        if head == 0:
            dv[...] = more_v
            dk[...] = more_k
        else:
            dv[...] += more_v
            dk[...] += more_k
        now = later
    dq[0] = unrotate(jnp.concatenate(grad_q, axis=0).T * (HD**-0.5), cos, sin).astype(BF16)


def peer_back_kernel(_adapter, at, k0, v0, gp, stats, cos, sin, dk_in, dv_in, *refs, first_pair, peers):
    q1 = refs[:peers]
    out, lse1, delta1 = refs[-3:]
    i = pl.program_id(0) + first_pair
    rows = k0.shape[1]
    half = stats.shape[2] // 2

    @pl.when(i == first_pair)
    def _():
        for n in range(peers):
            for side, ref in enumerate((lse1, delta1)):
                cut = slice(side * half, side * half + rows)
                ref[n] = (
                    stats[n, 0:16, cut].astype(F32)
                    + stats[n, 16:32, cut].astype(F32)
                    + stats[n, 32:48, cut].astype(F32)
                )

    def first(item):
        head, peer = item
        q = head_mask(q1[peer][0], head)
        g = head_mask(gp[peer, EXTRA : EXTRA + rows, :], head)
        return dot(k0[0], q, NT), dot(v0[0], g, NT), q, g

    items = [(head, peer) for peer in range(peers) for head in range(2)]
    grad_k, grad_v = dk_in[...], dv_in[...]
    now = first(items[0])
    for n, (head, peer) in enumerate(items):
        later = first(items[n + 1]) if n + 1 < len(items) else None
        s, dp, q, g = now
        row = pl.ds(2 * i + head, 1)
        prob, ds = score_grads(s, dp, lse1[peer, row, :], delta1[peer, row, :])
        grad_v = grad_v + dot(prob, g)
        grad_k = grad_k + dot(ds, q)
        now = later
    out[0] = unrotate(grad_k, cos, sin).astype(BF16)
    out[1] = grad_v.astype(BF16)


def attend_back(limit, kernel, at, args, specs, outs, blocks, before, pairs, peers, scratch, flops, name):
    first, count = pairs
    before = () if before is None else tuple(before)
    steps = HEADS // 2
    return pl.pallas_call(
        functools.partial(kernel, first_pair=first, peers=peers),
        grid_spec=pltpu.PrefetchScalarGridSpec(
            num_scalar_prefetch=2,
            grid=(count,),
            in_specs=specs + [pl.BlockSpec(memory_space=pl.ANY)] * len(before),
            out_specs=[pl.BlockSpec((blocks[0], outs[0].shape[1], LANES), lambda i, adapter, at: (blocks[1], 0, i + first))]
            + [pl.BlockSpec((o.shape[0], LANES), lambda i, adapter, at: (0, i + first)) for o in outs[1:]],
            scratch_shapes=scratch,
        ),
        out_shape=outs,
        input_output_aliases={2 + len(args) + n: n for n in range(len(before))},
        compiler_params=params(limit),
        cost_estimate=cost(
            flops * count // steps,
            4 * sum(a.size for a in args[:4]) * count // steps,
            flops * count // steps // 512,
        ),
        name=name,
    )(*at, *args, *before)


def own_back(at, own, peer, go, lse, delta, cos, sin, pairs, before):
    rows = own.shape[1]
    peers = peer.shape[0] // 24
    width = own.shape[0] // 3 * LANES
    first = pairs[0]

    def part(which):
        return pl.BlockSpec((1, rows, LANES), lambda i, adapter, at: (8 * which + first + i, 0, 0))

    table = pl.BlockSpec((rows, LANES), lambda i, adapter, at: (at[0], 0), pipeline_mode=pl.Buffered(1))
    return attend_back(
        24,
        own_back_kernel,
        at,
        (own, own, own, go, lse, delta, cos, sin) + (peer,) * (2 * peers),
        [part(0), part(1), part(2)]
        + [pl.BlockSpec((rows + EXTRA, LANES), lambda i, adapter, at: (0, i + first))]
        + [fixed((HEADS // 2, 2, rows)), fixed((HEADS, rows)), table, table]
        + [part(3 * p + 1) for p in range(peers)]
        + [part(3 * p + 2) for p in range(peers)],
        [jax.ShapeDtypeStruct((3, rows, width), BF16)] + [pltpu.HBM((rows, width), F32)] * 2,
        (1, 2),
        before,
        pairs,
        peers,
        [],
        2 * rows * width * 4 * rows * (5 + 3 * peers),
        "own_back",
    )


def peer_back(at, own, peer, gp, cos, sin, dk, dv, pairs, before):
    rows = own.shape[1]
    peers = gp.shape[0]
    width = own.shape[0] // 3 * LANES
    first = pairs[0]

    def part(which):
        return pl.BlockSpec((1, rows, LANES), lambda i, adapter, at: (8 * which + first + i, 0, 0))

    column = pl.BlockSpec((rows, LANES), lambda i, adapter, at: (0, i + first))
    table = pl.BlockSpec((rows, LANES), lambda i, adapter, at: (at[0], 0), pipeline_mode=pl.Buffered(1))
    return attend_back(
        24,
        peer_back_kernel,
        at,
        (own, own, gp, gp, cos, sin, dk, dv) + (peer,) * peers,
        [
            part(1), part(2),
            pl.BlockSpec((peers, rows + EXTRA, LANES), lambda i, adapter, at: (0, 0, i + first)),
            fixed((peers, EXTRA, width)),
            table, table, column, column,
        ]
        + [part(3 * p) for p in range(peers)],
        [jax.ShapeDtypeStruct((3, rows, width), BF16)],
        (2, 0),
        before,
        pairs,
        peers,
        [pltpu.VMEM((peers, HEADS, rows), F32), pltpu.VMEM((peers, HEADS, rows), F32)],
        2 * rows * width * 4 * 4 * rows * peers,
        "peer_back",
    )


def qkv_grad_kernel(
    _adapter, at, g, low, x, gain, shift, up, stay_out, leave_out, rank_grad, pieces, sems
):
    width = x.shape[1]
    low_t = low[...].T
    total = None
    def put(first, grad):
        for p in range(width // LANES):
            cut = slice(p * LANES, (p + 1) * LANES)
            pieces[position(jnp.int32(first + p), at, 6), 0] = grad[:, cut].astype(BF16)

    for n in range(3):
        grad = g[(n + 2) % 3]
        put(n * (width // LANES), dot(low_t, grad))
        more = dot(grad, up[0, :, n * width : (n + 1) * width], NT)
        total = more if total is None else total + more
    rank = total.astype(BF16)
    rank_grad[...] = rank
    normed, _s = norm_rows(x[...].astype(F32))
    h1 = (normed * gain[...] + shift[...]).astype(BF16)
    put(3 * (width // LANES), dot(rank.T, h1))
    leave = group(
        sems, [(pieces.at[pl.ds(0, 16)], stay_out), (pieces.at[pl.ds(16, 16)], leave_out)]
    )
    start_all(leave)
    wait_all(leave)


def qkv_grad(at, g, low, x, gain, shift, up, groups):
    rows, width = x.shape
    return pl.pallas_call(
        qkv_grad_kernel,
        grid_spec=pltpu.PrefetchScalarGridSpec(
            num_scalar_prefetch=2,
            grid=(1,),
            in_specs=[
                whole((3, rows, width)),
                whole((rows, RANK)),
                whole((rows, width)),
                whole((1, width)),
                whole((1, width)),
                chosen((RANK, 3 * width)),
            ],
            out_specs=[ANY, ANY, whole((rows, RANK))],
            scratch_shapes=[
                pltpu.VMEM((groups, 1, RANK, LANES), BF16),
                pltpu.SemaphoreType.DMA((2,)),
            ],
        ),
        out_shape=[
            jax.ShapeDtypeStruct((groups // 2, 1, RANK, LANES), BF16),
            jax.ShapeDtypeStruct((groups // 2, 1, RANK, LANES), BF16),
            jax.ShapeDtypeStruct((rows, RANK), BF16),
        ],
        compiler_params=params(16),
        cost_estimate=cost(2 * rows * 16 * 3 * width * 4, 8 * rows * width),
        name="qkv_grad",
    )(*at, g, low, x, gain, shift, up)


def input_grad_kernel(_adapter, at, g, w, rank_grad, down, x, gain, dx1, *refs):
    out, total = refs[-2:]
    j = pl.program_id(0)

    @pl.when(j == 0)
    def _():
        total[...] = dot(rank_grad[...], down[0]) + dot(g[0], w[...], NT)

    @pl.when(j == 1)
    def _():
        total[...] += dot(g[0], w[...], NT)

    @pl.when(j == 2)
    def _():
        grad = total[...] + dot(g[0], w[...], NT)
        normed, spread = norm_rows(x[...].astype(F32))
        out[...] = dx1[...] + norm_back(grad, normed, spread, gain[...])


def input_grad(at, g, w, rank_grad, down, x, gain, dx1, half, before=()):
    rows, width = x.shape
    cut = rows // 2
    part = pl.BlockSpec((cut, width), lambda j, adapter, at: (half, 0))
    order = lambda j: lax.rem(j + 1, 3)
    return pl.pallas_call(
        input_grad_kernel,
        grid_spec=pltpu.PrefetchScalarGridSpec(
            num_scalar_prefetch=2,
            grid=(3,),
            in_specs=[
                pl.BlockSpec((1, cut, width), lambda j, adapter, at: (j, half, 0)),
                pl.BlockSpec((width, width), lambda j, adapter, at: (0, order(j))),
                pl.BlockSpec((cut, RANK), lambda j, adapter, at: (half, 0)),
                chosen((RANK, width)),
                part,
                fixed((1, width)),
                part,
            ]
            + [ANY] * len(before),
            out_specs=part,
            scratch_shapes=[pltpu.VMEM((cut, width), F32)],
        ),
        out_shape=jax.ShapeDtypeStruct((rows, width), F32),
        input_output_aliases={9 + n: n for n in range(len(before))},
        compiler_params=params(20),
        cost_estimate=cost(3 * rows * width * width, 6 * width * width + 8 * rows * width),
        name="input_grad",
    )(*at, g, w, rank_grad, down, x, gain, dx1, *before)


def swap_order():
    bits = []
    n = 4
    while n < lax.axis_size("dp"):
        bits.append((n, 0))
        n *= 2
    n = 1
    while n < lax.axis_size("seq"):
        bits.append((0, n))
        n *= 2
    bits.append((2, 0))
    first = bits[:4]
    second = [first[1], first[0], first[3], first[2]]
    return (first, second), bits[4:]


def swap(values, step):
    size, ways = lax.axis_size("dp"), lax.axis_size("seq")
    perm = []
    for d in range(size):
        flip_d, flip_s = step[d & 1]
        for s in range(ways):
            perm.append((d * ways + s, (d ^ flip_d) * ways + (s ^ flip_s)))
    return lax.ppermute(values, ("dp", "seq"), perm)


def device_codes():
    orders, _rest = swap_order()
    size, ways = lax.axis_size("dp"), lax.axis_size("seq")
    table = np.zeros((size * ways, 9 + ways), np.int32)
    for d in range(size):
        for s in range(ways):
            codes = []
            for order in orders:
                on = [((d & bit_d) | (s & bit_s)) != 0 for bit_d, bit_s in order]
                codes.append(
                    (
                        sum(8 >> n for n in range(4) if on[n]),
                        sum(1 << n for n in range(4) if on[n]),
                        8 * on[2] + 4 * on[3],
                    )
                )
            mine, theirs = codes[d & 1], codes[1 - (d & 1)]
            row = [s, d & 1, mine[0], theirs[0], mine[1], theirs[1], mine[2], theirs[2], d]
            table[d * ways + s] = row + [(s + n) % ways for n in range(1, ways)] + [0]
    place = lax.axis_index("dp") * ways + lax.axis_index("seq")
    return lax.dynamic_slice_in_dim(jnp.asarray(table), place, 1, 0)[0]


def slot_masks(sequence):
    orders, _rest = swap_order()
    masks = []
    for order in orders:
        slots = [0, 1]
        for n in sequence:
            slots = slots + [slot ^ order[n][0] for slot in slots]
        masks.append(slots)
    return masks


def scatter_steps():
    orders, _rest = swap_order()
    return [((1, 0), (1, 0))] + list(zip(*orders))


def scatter_stage(held, step):
    half = held.shape[1] // 2
    return jnp.concatenate([held[:, :half], swap(held[:, half:], step)], axis=0)


def owner_sum_kernel(owners, at, held, out, total, *, masks):
    total[...] = jnp.zeros_like(total)
    for n, (even, odd) in enumerate(zip(*masks)):
        mask = even if even == odd else jnp.where(at[1] == 0, even, odd)
        total[owners[at[8] ^ mask]] += held[n].astype(F32)
    for a in range(NADAPT):
        out[:, a] = total[a].astype(BF16)


def owner_sum(at, owners, held, masks):
    slots, groups, parts, rank, lanes = held.shape
    pieces = groups * parts
    held = held.reshape(slots, pieces, rank, lanes)
    step = min(pieces, 4)
    out = pl.pallas_call(
        functools.partial(owner_sum_kernel, masks=masks),
        grid_spec=pltpu.PrefetchScalarGridSpec(
            num_scalar_prefetch=2,
            grid=(pieces // step,),
            in_specs=[pl.BlockSpec((slots, step, rank, lanes), lambda i, *_: (0, i, 0, 0))],
            out_specs=pl.BlockSpec((step, NADAPT, rank, lanes), lambda i, *_: (i, 0, 0, 0)),
            scratch_shapes=[pltpu.VMEM((NADAPT, step, rank, lanes), F32)],
        ),
        out_shape=jax.ShapeDtypeStruct((pieces, NADAPT, rank, lanes), BF16),
        compiler_params=params(12),
        cost_estimate=cost(held.size, 2 * held.size),
        name="owner_sum",
    )(owners, at[1], held)
    out = out.reshape(groups, parts, NADAPT, rank, lanes)
    _orders, rest = swap_order()
    for bits in rest:
        out = (out.astype(F32) + swap(out, (bits, bits)).astype(F32)).astype(BF16)
    return out


def spread_kernel(_adapter, at, mine, theirs, *outs, plan, straight):
    for core in range(2):

        @pl.when(at[1] == core)
        def _():
            for ref, part, first, count in zip(outs, *plan):
                for p in range(count):
                    piece = first + p
                    near = piece >> 4 == core
                    held = mine if near else theirs
                    if straight:
                        low = (piece & 15) ^ (at[6] if near else at[7])
                    else:
                        low = int(f"{piece & 15:04b}"[::-1], 2) ^ (at[4] if near else at[5])
                    ref[:, :, p * LANES : (p + 1) * LANES] = held[low, part].astype(F32)


def spread(at, mine, theirs, plan, straight=False):
    parts, firsts, counts = plan
    shapes = [(NADAPT, RANK, count * LANES) for count in counts]
    return pl.pallas_call(
        functools.partial(spread_kernel, plan=plan, straight=straight),
        grid_spec=pltpu.PrefetchScalarGridSpec(
            num_scalar_prefetch=2,
            grid=(1,),
            in_specs=[whole(mine.shape), whole(theirs.shape)],
            out_specs=[whole(shape) for shape in shapes],
        ),
        out_shape=[jax.ShapeDtypeStruct(shape, F32) for shape in shapes],
        compiler_params=params(20),
        cost_estimate=cost(1, 12 * mine.size),
        name="spread",
    )(*at, mine, theirs)


def tie(*values):
    flat, tree = jax.tree.flatten(values)
    return jax.tree.unflatten(tree, lax.optimization_barrier(flat))


def body(
    clip_tokens, adapter_index, ln1_gain, ln1_bias, qkv_weight, qkv_bias, qkv_down, qkv_up,
    out_weight, out_bias, out_down, out_up, ln2_gain, ln2_bias, fc1_weight, fc1_bias, fc1_down,
    fc1_up, fc2_weight, fc2_bias, fc2_down, fc2_up, cotangent,
):
    _one, rows, width = clip_tokens.shape
    devices = lax.axis_size("seq")
    groups = 32
    pin = lambda v: pltpu.with_memory_space_constraint(v, pltpu.HBM)
    row = lambda v: pin(v.reshape(1, -1))
    x = pin(clip_tokens[0])
    cot = cotangent[0]
    free_qkv, free_fc2 = qkv_weight, fc2_weight
    qkv_weight, qkv_down, qkv_up = pin(qkv_weight), pin(qkv_down), pin(qkv_up)
    out_weight, out_down, out_up = pin(out_weight), pin(out_down), pin(out_up)
    fc1_weight, fc1_down, fc1_up = pin(fc1_weight), pin(fc1_down), pin(fc1_up)
    fc2_weight, fc2_down, fc2_up = pin(fc2_weight), pin(fc2_down), pin(fc2_up)
    peers = range(1, devices)
    at = (adapter_index, device_codes())
    tagged = jnp.broadcast_to(adapter_index.astype(BF16)[:, None], (256, LANES))
    tagged, cot = tie(tagged, cot)
    tags = lax.all_gather(tagged, "dp", axis=0, tiled=True)
    masks_a, masks_b = slot_masks((0, 1, 2, 3)), slot_masks((2, 3, 0, 1))

    def from_peer(values, shift):
        return lax.ppermute(values, "seq", [((n + shift) % devices, n) for n in range(devices)])

    tables = tuple(pin(jnp.asarray(t)) for t in rotary_tables(rows * devices))
    cos, sin = tables
    x_peer = jnp.concatenate([from_peer(clip_tokens[0], n) for n in peers], axis=0)
    first_set = (row(ln1_gain), row(ln1_bias), qkv_weight, row(qkv_bias), qkv_down, qkv_up)
    own, mixed, back, low_qkv, top, total, grad2 = front_rows(
        at, x, pin(cot), first_set, tables, fc2_weight, fc2_down, fc2_up
    )
    peer, act, x1, low2, dx1, go, delta, lse, *pieces_a = middle_rows(
        at, x_peer, first_set, tables, own, (mixed, top, total), x, pin(cot), back, grad2,
        (out_weight, row(out_bias), out_down, out_up),
        (row(ln2_gain), row(ln2_bias)),
        (fc1_weight, row(fc1_bias), fc1_down, fc1_up),
        fc2_down, groups,
    )
    own, peer, lse = pin(own), pin(peer), pin(lse)
    go_sent, kept, sent, delta, tags = tie(go, pieces_a[0][None], pieces_a[1][None], delta, tags)
    index_all = tags[::256, 0].astype(jnp.int32)
    go_peer = jnp.stack([from_peer(go_sent, n) for n in peers])
    steps = scatter_steps()

    def halves(held):
        half = held.shape[1] // 2
        return held[:, :half], held[:, half:]

    def join(*parts):
        return jnp.concatenate(parts, axis=0)

    arrived = swap(sent, steps[0])
    kept, sent = halves(join(kept, arrived))
    sent, delta = tie(sent, delta)
    arrived = swap(sent, steps[1])
    back = functools.partial(own_back, at, own, peer, pin(go), lse, pin(delta), cos, sin)
    grads = back((0, 4), None)
    arrived, grads = tie(arrived, grads)
    kept, sent = halves(join(kept, arrived))
    sent, grads = tie(sent, grads)
    arrived = swap(sent, steps[2])
    grads, dk, dv = back((4, 4), grads)
    arrived, dk, go_peer = tie(arrived, dk, go_peer)
    dk, dv = pin(dk), pin(dv)
    kept, sent = halves(join(kept, arrived))
    sent, go_peer = tie(sent, go_peer)
    arrived = swap(sent, steps[3])
    grads = peer_back(at, own, peer, go_peer, cos, sin, dk, dv, (0, 8), (grads,))[0]
    arrived, grads = tie(arrived, grads)
    kept_a, sent = halves(join(kept, arrived))
    sent, grads = tie(sent, grads)
    arrived_a = swap(sent, steps[4])
    kept, sent, rank_grad = qkv_grad(
        at, grads, low_qkv, x, row(ln1_gain), row(ln1_bias), qkv_up, groups
    )
    arrived_a, sent, rank_grad = tie(arrived_a, sent, rank_grad)
    held = join(kept[None], swap(sent[None], steps[0]))
    total_a = owner_sum(at, index_all, join(kept_a, arrived_a), masks_a)

    def grad_half(half, rank_grad, before=()):
        return input_grad(
            at, grads, free_qkv, rank_grad, qkv_down, x, row(ln1_gain), pin(dx1), half, before
        )

    def output_half(half, low2, before=()):
        return output_rows(at, pin(act), free_fc2, pin(x1), row(fc2_bias), low2, fc2_up, half, before)

    kept, sent = halves(held)
    arrived = swap(sent, steps[3])
    sent, total_a, rank_grad = tie(sent, total_a, rank_grad)
    arrived_a = swap(total_a, steps[1])
    grad_in = grad_half(0, rank_grad)
    arrived, arrived_a, rank_grad, grad_in = tie(arrived, arrived_a, rank_grad, grad_in)
    kept, sent = halves(join(kept, arrived))
    total_a = join(total_a, arrived_a)
    sent, total_a, rank_grad = tie(sent, total_a, rank_grad)
    arrived = swap(sent, steps[4])
    arrived_a = swap(total_a, steps[2])
    grad_in = grad_half(1, rank_grad, (grad_in,))
    arrived, arrived_a, grad_in = tie(arrived, arrived_a, grad_in)
    held, total_a = join(kept, arrived), join(total_a, arrived_a)
    held, total_a, low2 = tie(held, total_a, low2)
    arrived = swap(held, steps[1])
    arrived_a = swap(total_a, steps[3])
    block_output = output_half(0, low2)
    arrived, arrived_a, low2, block_output = tie(arrived, arrived_a, low2, block_output)
    held, total_a = join(held, arrived), join(total_a, arrived_a)
    held, total_a, low2 = tie(held, total_a, low2)
    arrived = swap(held, steps[2])
    arrived_a = swap(total_a, steps[4])
    block_output = output_half(1, low2, (block_output,))
    arrived, block_output = tie(arrived, block_output)
    total_b = owner_sum(at, index_all, join(held, arrived), masks_b)
    total_b, arrived_a = tie(total_b, arrived_a)
    total_a = join(total_a, arrived_a)
    arrived = swap(total_b, steps[4])
    theirs_a = swap(total_a, steps[0])
    total_b = join(total_b, arrived)
    total_b, total_a, theirs_a = tie(total_b, total_a, theirs_a)
    arrived = swap(total_b, steps[3])
    per = width // LANES
    spread_a = spread(
        at, total_a, theirs_a,
        ((0, 1, 2, 2, 2, 2), (0, 0, 0, per, 2 * per, 3 * per), (32, 32, per, per, per, per)),
    )
    arrived, spread_a = tie(arrived, spread_a)
    up1, down2, up2, down1, up_o, down_o = spread_a
    total_b = join(total_b, arrived)
    up_qkv, down_qkv = spread(
        at, total_b, swap(total_b, steps[0]), ((0, 0), (0, 3 * per), (3 * per, per)), straight=True
    )
    return (
        block_output[None], grad_in[None], down_qkv, up_qkv, down_o, up_o, down1, up1, down2, up2,
    )


def solution(mesh):
    split = P("dp", "seq", None)
    return jax.shard_map(
        body,
        mesh=mesh,
        in_specs=(split, P("dp")) + (P(),) * 20 + (split,),
        out_specs=(split, split) + (P(),) * 8,
        check_vma=False,
    )
```

```python
import functools

import jax
import jax.numpy as jnp
import numpy as np
from jax import lax
from jax.experimental import pallas as pl
from jax.experimental.pallas import tpu as pltpu
from jax.sharding import PartitionSpec as P

HEADS = 16
HD = 64
GRID = 16
NADAPT = 8
RANK = 16
EPSILON = 1e-06
LANES = 128
EXTRA = 48

F32 = jnp.float32
BF16 = jnp.bfloat16
NN = (((1,), (0,)), ((), ()))
NT = (((1,), (1,)), ((), ()))

ERFC = (
    0.16918800211151383,
    0.1707152747822528,
    0.14833885959986734,
    0.21492717178376733,
    -0.09465313901935662,
    0.5477232747113128,
    -0.5122807406271995,
    0.48556441585520754,
    -0.1295231387829952,
)


def dot(a, b, dims=NN):
    return lax.dot_general(a, b, dims, preferred_element_type=F32)


def params(megabytes):
    return pltpu.CompilerParams(
        dimension_semantics=("arbitrary",), vmem_limit_bytes=megabytes << 20
    )


def cost(flops, moved, exps=0):
    return pl.CostEstimate(flops=int(flops), bytes_accessed=int(moved), transcendentals=int(exps))


def norm_rows(values):
    centre = values - jnp.mean(values, axis=-1, keepdims=True)
    spread = lax.rsqrt(jnp.mean(centre * centre, axis=-1, keepdims=True) + EPSILON)
    return centre * spread, spread


def norm_back(grad_rows, normed, spread, gain):
    scaled = grad_rows * gain
    first = jnp.mean(scaled, axis=-1, keepdims=True)
    second = jnp.mean(scaled * normed, axis=-1, keepdims=True)
    return spread * (scaled - first - normed * second)


def rotary_tables(length):
    half = HD // 2
    side = half // 3
    lead = half - 2 * side
    token = np.arange(length)
    pair = np.arange(half)
    kind = np.where(pair < lead, 0, np.where(pair < lead + side, 1, 2))
    local = np.where(kind == 0, pair, np.where(kind == 1, pair - lead, pair - lead - side))
    total = np.where(kind == 0, lead, side)
    frequency = np.power(
        np.float32(10000.0), -local.astype(np.float32) / total.astype(np.float32)
    ).astype(np.float32)
    place = np.where(
        kind[None] == 0,
        (token // (GRID * GRID))[:, None],
        np.where(kind[None] == 1, (token // GRID % GRID)[:, None], (token % GRID)[:, None]),
    ).astype(np.float32)
    angle = place * frequency[None]
    cosine, sine = np.cos(angle), np.sin(angle)
    cos_rows = np.concatenate([cosine] * 4, axis=1).astype(np.float32)
    sin_rows = np.concatenate([-sine, sine, -sine, sine], axis=1).astype(np.float32)
    return cos_rows, sin_rows


def swap_halves(values):
    lane = lax.broadcasted_iota(jnp.int32, (1, LANES), 1)
    low = (lane & (HD // 2)) == 0
    return jnp.where(
        low, pltpu.roll(values, LANES - HD // 2, 1), pltpu.roll(values, HD // 2, 1)
    )


def head_mask(values, head):
    lane = lax.broadcasted_iota(jnp.int32, (1, LANES), 1)
    keep = (lane < HD) if head == 0 else (lane >= HD)
    return jnp.where(keep, values, jnp.zeros_like(values))


def whole(shape):
    return pl.BlockSpec(shape, lambda *_: (0,) * len(shape))


def fixed(shape):
    return pl.BlockSpec(shape, lambda *_: (0,) * len(shape), pipeline_mode=pl.Buffered(1))


def chosen(shape):
    return pl.BlockSpec((1,) + shape, lambda *ids: (ids[-2][0], 0, 0))


def chosen_tile(tile, which):
    return pl.BlockSpec((1, RANK, tile), lambda j, adapter, at: (adapter[0], 0, which(j)))


def position(piece, at, first=2):
    top = (piece >> 4) ^ at[1]
    return 16 * top + ((piece & 15) ^ jnp.where(top == 0, at[first], at[first + 1]))


CHUNK = 256


def qkv_tile(tile, h1, low, w, bias, up, cos, sin, out_ref, keep, first):
    scale = jnp.where(tile == 0, HD**-0.5, 1.0).astype(F32)
    turn = jnp.where(tile == 2, 0.0, 1.0).astype(F32)
    c = (cos[...] * turn + (1.0 - turn)) * scale
    s = sin[...] * (turn * scale)

    def chunk(n):
        cut = slice(n * CHUNK, (n + 1) * CHUNK)
        return dot(h1, w[:, cut]) + bias[:, cut] + dot(low, up[:, cut])

    count = w.shape[1] // CHUNK
    now = chunk(0)
    parts = []
    for n in range(count):
        later = chunk(n + 1) if n + 1 < count else None
        for g in range(CHUNK // LANES):
            part = now[:, g * LANES : (g + 1) * LANES]
            parts.append((part * c + swap_halves(part) * s).astype(BF16))
        now = later
    for n, part in enumerate(parts):
        out_ref[n] = part
        keep[first + n] = part


def attend_pairs(count, load, finish):
    loaded = [load(pair) for pair in range(count)]
    values_t = [v.T for _q, _k, v in loaded]

    def scores(item):
        pair, head = item
        q, k, _v = loaded[pair]
        return dot(k, head_mask(q, head), NT)

    items = [(pair, head) for pair in range(count) for head in range(2)]
    now = scores(items[0])
    for n, (pair, head) in enumerate(items):
        later = scores(items[n + 1]) if n + 1 < len(items) else None
        finish(pair, head, now, values_t[pair][head * HD : (head + 1) * HD])
        now = later


STEP_PAIRS = 4


def start_all(*groups):
    for group in groups:
        for copy in group:
            copy.start()


def wait_all(*groups):
    for group in groups:
        for copy in group:
            copy.wait()


def group(sems, pairs):
    return [pltpu.make_async_copy(a, b, sems.at[n]) for n, (a, b) in enumerate(pairs)]


def tiles(source, kept, size):
    return [(source.at[:, pl.ds(n * size, size)], kept.at[n]) for n in range(kept.shape[0])]


def front_kernel(
    adapter, at, x, w, w2,
    gain, shift, bias, down, up, cos, sin, cot, down2, up2,
    qkv, mixed_out, back, low, top_out, total_out, grad2,
    h1, keep, gain_k, shift_k, bias_k, down_k, up_k, cos_k, sin_k, cot_k, down2_k, up2_k,
    low_k, top_k, total_k, grad2_k, sem_a, sem_b, sem_c, sem_d,
    *, starts,
):
    j = pl.program_id(0)
    second, third = starts
    last = pl.num_programs(0) - 1
    mine = adapter[0]
    rows, width = x.shape
    place = pl.ds(pl.multiple_of(at[0] * rows, rows), rows)
    early = group(
        sem_a,
        [
            (gain, gain_k), (shift, shift_k), (down.at[mine], down_k),
            (cos.at[place], cos_k), (sin.at[place], sin_k),
        ]
        + tiles(bias, bias_k, width)
        + tiles(up.at[mine], up_k, width),
    )
    late = group(
        sem_b, [(cot, cot_k), (up2.at[mine], up2_k)] + tiles(down2.at[mine], down2_k, w2.shape[0])
    )
    stats = group(sem_c, [(low_k, low), (top_k, top_out), (total_k, total_out)])
    end = group(sem_d, [(grad2_k, grad2)])

    @pl.when(j == 0)
    def _():
        start_all(early, late)
        normed, _s = norm_rows(x[...].astype(F32))
        wait_all(early)
        held = (normed * gain_k[...] + shift_k[...]).astype(BF16)
        h1[...] = held
        low_k[...] = dot(held, down_k[...], NT).astype(BF16)

    @pl.when(j < second)
    def _():
        qkv_tile(j, h1[...], low_k[...], w, bias_k[j], up_k[j], cos_k, sin_k, qkv, keep, 8 * j)

    @pl.when((j >= second) & (j < third))
    def _():
        first = (j - second) * STEP_PAIRS

        def load(pair):
            return keep[first + pair], keep[8 + first + pair], keep[16 + first + pair]

        def finish(pair, head, scores, values_t):
            top = jnp.max(scores, axis=0, keepdims=True)
            weights = jnp.exp(scores - top)
            start = pair * LANES + head * HD
            mixed_out[start : start + HD, :] = dot(values_t, weights.astype(BF16))
            top_k[first + pair, head : head + 1, :] = top
            total_k[first + pair, head : head + 1, :] = jnp.sum(weights, axis=0, keepdims=True)

        attend_pairs(STEP_PAIRS, load, finish)

    @pl.when(j == third)
    def _():
        start_all(stats)
        wait_all(late)
        grad2_k[...] = dot(cot_k[...], up2_k[...], NT).astype(BF16)
        start_all(end)

    @pl.when(j >= third)
    def _():
        side = dot(grad2_k[...], down2_k[j - third])
        back[...] = (dot(cot_k[...], w2[...], NT) + side).astype(BF16)

    @pl.when(j == last)
    def _():
        wait_all(stats, end)


def clip(value, low, high):
    return jnp.minimum(jnp.maximum(value, low), high)


ANY = pl.BlockSpec(memory_space=pl.ANY)


def front_rows(at, x, cot, first_set, tables, w2, down2, up2):
    gain, shift, w, bias, down, up = first_set
    rows, width = x.shape
    ff = w2.shape[0]
    tile = 1024
    second = w.shape[1] // width
    third = second + HEADS // 2 // STEP_PAIRS
    steps = third + ff // tile
    one = lambda j: jnp.minimum(j, second - 1)
    two = lambda j: clip(j - second, 0, third - second - 1)
    three = lambda j: clip(j - third, 0, steps - third - 1)
    stat = (HEADS // 2, 2, rows)
    return pl.pallas_call(
        functools.partial(front_kernel, starts=(second, third)),
        grid_spec=pltpu.PrefetchScalarGridSpec(
            num_scalar_prefetch=2,
            grid=(steps,),
            in_specs=[
                fixed((rows, width)),
                pl.BlockSpec((width, width), lambda j, adapter, at: (0, one(j))),
                pl.BlockSpec((tile, width), lambda j, adapter, at: (three(j), 0)),
            ]
            + [ANY] * 10,
            out_specs=[
                pl.BlockSpec((8, rows, LANES), lambda j, adapter, at: (one(j), 0, 0)),
                pl.BlockSpec((STEP_PAIRS * LANES, rows), lambda j, adapter, at: (two(j), 0)),
                pl.BlockSpec((rows, tile), lambda j, adapter, at: (0, three(j))),
            ]
            + [ANY] * 4,
            scratch_shapes=[
                pltpu.VMEM((rows, width), BF16),
                pltpu.VMEM((24, rows, LANES), BF16),
                pltpu.VMEM((1, width), F32),
                pltpu.VMEM((1, width), F32),
                pltpu.VMEM((second, 1, width), F32),
                pltpu.VMEM((RANK, width), BF16),
                pltpu.VMEM((second, RANK, width), BF16),
                pltpu.VMEM((rows, LANES), F32),
                pltpu.VMEM((rows, LANES), F32),
                pltpu.VMEM((rows, width), BF16),
                pltpu.VMEM((ff // tile, RANK, tile), BF16),
                pltpu.VMEM((RANK, width), BF16),
                pltpu.VMEM((rows, RANK), BF16),
                pltpu.VMEM(stat, F32),
                pltpu.VMEM(stat, F32),
                pltpu.VMEM((rows, RANK), BF16),
                pltpu.SemaphoreType.DMA((5 + 2 * second,)),
                pltpu.SemaphoreType.DMA((2 + ff // tile,)),
                pltpu.SemaphoreType.DMA((3,)),
                pltpu.SemaphoreType.DMA((1,)),
            ],
        ),
        out_shape=[
            pltpu.HBM((24, rows, LANES), BF16),
            pltpu.HBM((width, rows), F32),
            pltpu.HBM((rows, ff), BF16),
            pltpu.HBM((rows, RANK), BF16),
            pltpu.HBM(stat, F32),
            pltpu.HBM(stat, F32),
            pltpu.HBM((rows, RANK), BF16),
        ],
        compiler_params=params(44),
        cost_estimate=cost(
            2 * rows * width * (3 * width + ff) + 16 * rows * rows * width, 20 << 20, 16 * rows * rows
        ),
        name="front_rows",
    )(*at, x, w, w2, gain, shift, bias, down, up, *tables, cot, down2, up2)


def gelu_both(f):
    z = jnp.abs(f) * (0.5**0.5)
    t = 1.0 / (1.0 + 0.3 * z)
    poly = ERFC[-1]
    for c in ERFC[-2::-1]:
        poly = poly * t + c
    bell = jnp.exp(f * f * -0.5)
    tail = (0.5 * poly) * t * bell
    phi = jnp.where(f < 0, tail, 1.0 - tail)
    return f * phi, phi + f * (bell * 0.3989422804014327)


def middle_kernel(
    adapter, at, xp, wq, w1, back,
    gain1, shift1, bq, downq, upq, cos, sin, own, mixed, top, total,
    x, cot, grad2, w_out, b_out, out_down, out_up, gain, shift, b1, down1, up1, down2,
    qkv, act_out, x1_out, low2_out, dx1_out, go_out, delta_out, lse_out, stay_out, leave_out,
    h1, lowq, keep, o, h2, dh2, low_o, low1, low1_t, grad2_t, low2, grad1,
    gain1_k, shift1_k, bq_k, downq_k, upq_k, cos_k, sin_k, q_own, mixed_in, top_in, total_in,
    x_k, cot_k, grad2_k, w_out_k, b_out_k, out_down_k, out_up_k, gain_k, shift_k, b1_k, down1_k, up1_k, down2_k,
    x1, low2_k, dx1_k, go, delta_k, lse, pieces,
    sem_a, sem_b, sem_c, sem_d, sem_e,
    *, starts, peers,
):
    j = pl.program_id(0)
    second, third = starts
    last = pl.num_programs(0) - 1
    rows, width = xp.shape
    tile = w1.shape[1]
    mine = adapter[0]
    places = [pl.ds(pl.multiple_of(at[9 + p] * rows, rows), rows) for p in range(peers)]
    early = group(
        sem_a,
        [(gain1, gain1_k), (shift1, shift1_k), (downq.at[mine], downq_k)]
        + [(cos.at[places[p]], cos_k.at[p]) for p in range(peers)]
        + [(sin.at[places[p]], sin_k.at[p]) for p in range(peers)]
        + tiles(bq, bq_k, width)
        + tiles(upq.at[mine], upq_k, width),
    )
    later = group(
        sem_b, [(own.at[pl.ds(0, 8)], q_own), (mixed, mixed_in), (top, top_in), (total, total_in)]
    )
    late = group(
        sem_c,
        [
            (x, x_k), (cot, cot_k), (grad2, grad2_k), (w_out, w_out_k), (b_out, b_out_k),
            (out_down.at[mine], out_down_k), (out_up.at[mine], out_up_k), (gain, gain_k),
            (shift, shift_k), (down1.at[mine], down1_k),
        ]
        + tiles(b1, b1_k, tile)
        + tiles(up1.at[mine], up1_k, tile)
        + tiles(down2.at[mine], down2_k, tile),
    )
    middle_out = group(sem_d, [(x1, x1_out), (lse, lse_out)])
    end = group(
        sem_e,
        [(low2_k, low2_out), (dx1_k, dx1_out), (go, go_out), (delta_k, delta_out)]
        + [(pieces.at[pl.ds(0, 16)], stay_out), (pieces.at[pl.ds(16, 16)], leave_out)],
    )

    @pl.when(j == 0)
    def _():
        start_all(early, later, late)

    @pl.when(j < second)
    def _():
        which, p = j // peers, lax.rem(j, peers)

        @pl.when(which == 0)
        def _():
            normed, _s = norm_rows(xp[...].astype(F32))

            @pl.when(j == 0)
            def _():
                wait_all(early)

            normed = (normed * gain1_k[...] + shift1_k[...]).astype(BF16)
            h1[p] = normed
            lowq[p] = dot(normed, downq_k[...], NT).astype(BF16)

        qkv_tile(
            which, h1[p], lowq[p], wq, bq_k[which], upq_k[which], cos_k.at[p], sin_k.at[p],
            qkv, keep, 24 * p + 8 * which,
        )

    @pl.when(j == second)
    def _():
        wait_all(later)

    @pl.when((j >= second) & (j < third))
    def _():
        first = (j - second) * STEP_PAIRS
        held = []

        def load(pair):
            n = first + pair
            k = [keep[24 * p + 8 + n] for p in range(peers)]
            v = [keep[24 * p + 16 + n] for p in range(peers)]
            if peers > 1:
                k, v = [jnp.concatenate(k, axis=0)], [jnp.concatenate(v, axis=0)]
            return q_own[n], k[0], v[0]

        def finish(pair, head, scores, values_t):
            n = first + pair
            before = top_in[n, head : head + 1, :]
            top = jnp.maximum(jnp.max(scores, axis=0, keepdims=True), before)
            scale = jnp.exp(before - top)
            weights = jnp.exp(scores - top)
            total = jnp.sum(weights, axis=0, keepdims=True)
            total = total + scale * total_in[n, head : head + 1, :]
            start = pl.ds(pl.multiple_of(n * LANES + head * HD, HD), HD)
            mixed = dot(values_t, weights.astype(BF16)) + scale * mixed_in[start, :]
            held.append(mixed * (1.0 / total))
            lse[n, head : head + 1, :] = top + jnp.log(total)
            if head == 1:
                o[n] = jnp.concatenate(held[-2:], axis=0).T.astype(BF16)

        attend_pairs(STEP_PAIRS, load, finish)

    def put(first, slot, grad):
        for p in range(grad.shape[1] // LANES):
            cut = slice(p * LANES, (p + 1) * LANES)
            pieces[position(first + p, at), slot] = grad[:, cut].astype(BF16)

    @pl.when(j == third)
    def _():
        wait_all(late)
        mixed = jnp.concatenate([o[n] for n in range(HEADS // 2)], axis=1)
        low = dot(mixed, out_down_k[...], NT).astype(BF16)
        low_o[...] = low
        branch = dot(mixed, w_out_k[...]) + b_out_k[...] + dot(low, out_up_k[...])
        mid = x_k[...].astype(F32) + branch
        x1[...] = mid
        normed, _s = norm_rows(mid)
        rows2 = (normed * gain_k[...] + shift_k[...]).astype(BF16)
        h2[...] = rows2
        low_1 = dot(rows2, down1_k[...], NT).astype(BF16)
        low1[...] = low_1
        low1_t[...] = low_1.T
        grad2_t[...] = grad2_k[...].T
        dh2[...] = jnp.zeros_like(dh2)
        low2[...] = jnp.zeros_like(low2)
        grad1[...] = jnp.zeros_like(grad1)
        start_all(middle_out)

    @pl.when(j >= third)
    def _():
        n_tile = j - third

        def hidden(n):
            cut = slice(n * CHUNK, (n + 1) * CHUNK)
            return dot(h2[...], w1[:, cut]) + b1_k[n_tile, :, cut] + dot(low1[...], up1_k[n_tile, :, cut])

        first = n_tile * (tile // LANES)
        count = tile // CHUNK
        now = hidden(0)
        acts, dfs = [], []
        for n in range(count):
            later = hidden(n + 1) if n + 1 < count else None
            cut = slice(n * CHUNK, (n + 1) * CHUNK)
            act, slope = gelu_both(now)
            acts.append(act.astype(BF16))
            dfs.append((back[:, cut].astype(F32) * slope).astype(BF16))
            now = later
        act, df = jnp.concatenate(acts, axis=1), jnp.concatenate(dfs, axis=1)
        dh2[...] += dot(df, w1[...], NT)
        low2[...] += dot(act, down2_k[n_tile], NT)
        grad1[...] += dot(df, up1_k[n_tile], NT)
        act_out[...] = act
        put(first, 0, dot(low1_t[...], df))
        put(first, 1, dot(grad2_t[...], act))

    @pl.when(j == last)
    def _():
        low_2 = low2[...].astype(BF16)
        low2_k[...] = low_2
        g1 = grad1[...].astype(BF16)
        back2 = dh2[...] + dot(g1, down1_k[...])
        normed, spread = norm_rows(x1[...])
        dx1 = cot_k[...].astype(F32) + norm_back(back2, normed, spread, gain_k[...])
        dx1_k[...] = dx1
        da = dx1.astype(BF16)
        g_o = dot(da, out_up_k[...], NT).astype(BF16)
        new_go = (dot(da, w_out_k[...], NT) + dot(g_o, out_down_k[...])).astype(BF16)
        go[EXTRA : EXTRA + rows, :] = new_go
        mixed = jnp.concatenate([o[n] for n in range(HEADS // 2)], axis=1)
        product = new_go.astype(F32) * mixed.astype(F32)
        high = product.astype(BF16)
        rest = (product - high.astype(F32)).astype(BF16)
        lane = lax.broadcasted_iota(jnp.int32, (HEADS, width), 1)
        head = lax.broadcasted_iota(jnp.int32, (HEADS, width), 0)
        pick = (lane // HD == head).astype(BF16)
        delta = dot(pick, high, NT) + dot(pick, rest, NT)
        delta_k[...] = delta
        if rows < width // 2:
            go[0:EXTRA, :] = jnp.zeros((EXTRA, width), BF16)
        logs = jnp.concatenate([lse[n] for n in range(HEADS // 2)], axis=0)
        for side, stat in enumerate((logs, delta)):
            left = stat
            for n in range(3):
                part = left.astype(BF16)
                go[16 * n : 16 * n + 16, side * (width // 2) : side * (width // 2) + rows] = part
                left = left - part.astype(F32)
        start_all(end[:4])
        per = width // LANES
        put(jnp.int32(0), 2, dot(low_2.T, cot_k[...]))
        put(jnp.int32(per), 2, dot(g1.T, h2[...]))
        put(jnp.int32(2 * per), 2, dot(low_o[...].T, da))
        put(jnp.int32(3 * per), 2, dot(g_o.T, mixed))
        start_all(end[4:])
        wait_all(middle_out, end)


def middle_rows(
    at, xp, first_set, tables, own, state, x, cot, back, grad2, out_set, norm_set, fc1_set, down2, groups
):
    rows, width = x.shape
    peers = xp.shape[0] // rows
    w1 = fc1_set[0]
    ff = w1.shape[1]
    tile = 1024
    second = 3 * peers
    third = second + HEADS // 2 // STEP_PAIRS
    steps = third + ff // tile
    one = lambda j: jnp.minimum(j, second - 1) // peers
    peer = lambda j: lax.rem(jnp.minimum(j, second - 1), peers)
    two = lambda j: clip(j - second, 0, third - second - 1)
    three = lambda j: clip(j - third, 0, steps - third - 1)
    stat = (HEADS // 2, 2, rows)
    count = ff // tile
    vmem = pltpu.VMEM
    return pl.pallas_call(
        functools.partial(middle_kernel, starts=(second, third), peers=peers),
        grid_spec=pltpu.PrefetchScalarGridSpec(
            num_scalar_prefetch=2,
            grid=(steps,),
            in_specs=[
                pl.BlockSpec((rows, width), lambda j, adapter, at: (jnp.minimum(j, peers - 1), 0)),
                pl.BlockSpec((width, width), lambda j, adapter, at: (0, one(j))),
                pl.BlockSpec((width, tile), lambda j, adapter, at: (0, three(j))),
                pl.BlockSpec((rows, tile), lambda j, adapter, at: (0, three(j))),
            ]
            + [ANY] * 24,
            out_specs=[
                pl.BlockSpec((8, rows, LANES), lambda j, adapter, at: (3 * peer(j) + one(j), 0, 0)),
                pl.BlockSpec((rows, tile), lambda j, adapter, at: (0, three(j))),
            ]
            + [ANY] * 8,
            scratch_shapes=[
                vmem((peers, rows, width), BF16),
                vmem((peers, rows, RANK), BF16),
                vmem((24 * peers, rows, LANES), BF16),
                vmem((HEADS // 2, rows, LANES), BF16),
                vmem((rows, width), BF16),
                vmem((rows, width), F32),
                vmem((rows, RANK), BF16),
                vmem((rows, RANK), BF16),
                vmem((RANK, rows), BF16),
                vmem((RANK, rows), BF16),
                vmem((rows, RANK), F32),
                vmem((rows, RANK), F32),
                vmem((1, width), F32),
                vmem((1, width), F32),
                vmem((3, 1, width), F32),
                vmem((RANK, width), BF16),
                vmem((3, RANK, width), BF16),
                vmem((peers, rows, LANES), F32),
                vmem((peers, rows, LANES), F32),
                vmem((8, rows, LANES), BF16),
                vmem((width, rows), F32),
                vmem(stat, F32),
                vmem(stat, F32),
                vmem((rows, width), BF16),
                vmem((rows, width), BF16),
                vmem((rows, RANK), BF16),
                vmem((width, width), BF16),
                vmem((1, width), F32),
                vmem((RANK, width), BF16),
                vmem((RANK, width), BF16),
                vmem((1, width), F32),
                vmem((1, width), F32),
                vmem((count, 1, tile), F32),
                vmem((RANK, width), BF16),
                vmem((count, RANK, tile), BF16),
                vmem((count, RANK, tile), BF16),
                vmem((rows, width), F32),
                vmem((rows, RANK), BF16),
                vmem((rows, width), F32),
                vmem((EXTRA + rows, width), BF16),
                vmem((HEADS, rows), F32),
                vmem(stat, F32),
                vmem((groups, 3, RANK, LANES), BF16),
                pltpu.SemaphoreType.DMA((9 + 2 * peers,)),
                pltpu.SemaphoreType.DMA((4,)),
                pltpu.SemaphoreType.DMA((10 + 3 * count,)),
                pltpu.SemaphoreType.DMA((2,)),
                pltpu.SemaphoreType.DMA((6,)),
            ],
        ),
        out_shape=[
            pltpu.HBM((24 * peers, rows, LANES), BF16),
            pltpu.HBM((rows, ff), BF16),
            pltpu.HBM((rows, width), F32),
            pltpu.HBM((rows, RANK), BF16),
            pltpu.HBM((rows, width), F32),
            pltpu.HBM((EXTRA + rows, width), BF16),
            pltpu.HBM((HEADS, rows), F32),
            pltpu.HBM(stat, F32),
            pltpu.HBM((groups // 2, 3, RANK, LANES), BF16),
            pltpu.HBM((groups // 2, 3, RANK, LANES), BF16),
        ],
        compiler_params=params(52),
        cost_estimate=cost(
            4 * rows * width * ff + (4 + 6 * peers) * rows * width * width, 40 << 20, rows * ff
        ),
        name="middle_rows",
    )(
        *at, xp, first_set[2], w1, back,
        first_set[0], first_set[1], first_set[3], first_set[4], first_set[5], *tables, own, *state,
        x, cot, grad2, *out_set, *norm_set, *fc1_set[1:], down2,
    )


def output_kernel(_adapter, at, act, w2, x1, b2, low2, up2, *refs):
    out, y = refs[-2:]
    j = pl.program_id(0)
    last = pl.num_programs(0) - 1

    @pl.when(j == 0)
    def _():
        y[...] = dot(act[...], w2[...])

    @pl.when((j > 0) & (j < last))
    def _():
        y[...] += dot(act[...], w2[...])

    @pl.when(j == last)
    def _():
        side = b2[...] + dot(low2[...], up2[0])
        out[...] = (x1[...] + (y[...] + dot(act[...], w2[...]) + side)).astype(BF16)


def output_rows(at, act, w2, x1, b2, low2, up2, half, before=()):
    rows, ff = act.shape
    width = x1.shape[1]
    wide = width // 2
    tile = 1024
    part = pl.BlockSpec((rows, wide), lambda j, adapter, at: (0, half))
    return pl.pallas_call(
        output_kernel,
        grid_spec=pltpu.PrefetchScalarGridSpec(
            num_scalar_prefetch=2,
            grid=(ff // tile,),
            in_specs=[
                pl.BlockSpec((rows, tile), lambda j, adapter, at: (0, j)),
                pl.BlockSpec((tile, wide), lambda j, adapter, at: (j, half)),
                part,
                pl.BlockSpec((1, wide), lambda j, adapter, at: (0, half)),
                fixed((rows, RANK)),
                pl.BlockSpec((1, RANK, wide), lambda j, adapter, at: (adapter[0], 0, half)),
            ]
            + [ANY] * len(before),
            out_specs=part,
            scratch_shapes=[pltpu.VMEM((rows, wide), F32)],
        ),
        out_shape=jax.ShapeDtypeStruct((rows, width), BF16),
        input_output_aliases={8 + n: n for n in range(len(before))},
        compiler_params=params(24),
        cost_estimate=cost(rows * width * ff, width * ff + 2 * rows * ff),
        name="output_rows",
    )(*at, act, w2, x1, b2, low2, up2, *before)


def unrotate(values, cos, sin):
    return values * cos[...] - swap_halves(values) * sin[...]


def score_grads(s, dp, lse, delta):
    prob = jnp.exp(s - lse)
    return prob.astype(BF16), (prob * (dp - delta)).astype(BF16)


def own_back_kernel(_adapter, at, q0, k0, v0, go, lse0, delta0, cos, sin, *refs, first_pair, peers):
    k1, v1 = refs[:peers], refs[peers : 2 * peers]
    dq, dk, dv = refs[-3:]
    i = pl.program_id(0) + first_pair
    rows = q0.shape[1]
    keys = jnp.concatenate([k0[0]] + [k[0] for k in k1], axis=0)
    values = jnp.concatenate([v0[0]] + [v[0] for v in v1], axis=0)
    keys_t = keys.T

    def first(head):
        q = head_mask(q0[0], head)
        g = head_mask(go[EXTRA : EXTRA + rows, :], head)
        return dot(keys, q, NT), dot(values, g, NT), q, g

    grad_q = []
    now = first(0)
    for head in range(2):
        later = first(1) if head == 0 else None
        s, dp, q, g = now
        row = pl.ds(2 * i + head, 1)
        prob, ds = score_grads(s, dp, lse0[i, head : head + 1, :], delta0[row, :])
        grad_q.append(dot(keys_t[head * HD : (head + 1) * HD], ds))
        more_v = dot(prob[:rows], g)
        more_k = dot(ds[:rows], q)
        if head == 0:
            dv[...] = more_v
            dk[...] = more_k
        else:
            dv[...] += more_v
            dk[...] += more_k
        now = later
    dq[0] = unrotate(jnp.concatenate(grad_q, axis=0).T * (HD**-0.5), cos, sin).astype(BF16)


def peer_back_kernel(_adapter, at, k0, v0, gp, stats, cos, sin, dk_in, dv_in, *refs, first_pair, peers):
    q1 = refs[:peers]
    out, lse1, delta1 = refs[-3:]
    i = pl.program_id(0) + first_pair
    rows = k0.shape[1]
    half = stats.shape[2] // 2

    @pl.when(i == first_pair)
    def _():
        for n in range(peers):
            for side, ref in enumerate((lse1, delta1)):
                cut = slice(side * half, side * half + rows)
                ref[n] = (
                    stats[n, 0:16, cut].astype(F32)
                    + stats[n, 16:32, cut].astype(F32)
                    + stats[n, 32:48, cut].astype(F32)
                )

    def first(item):
        head, peer = item
        q = head_mask(q1[peer][0], head)
        g = head_mask(gp[peer, EXTRA : EXTRA + rows, :], head)
        return dot(k0[0], q, NT), dot(v0[0], g, NT), q, g

    items = [(head, peer) for peer in range(peers) for head in range(2)]
    grad_k, grad_v = dk_in[...], dv_in[...]
    now = first(items[0])
    for n, (head, peer) in enumerate(items):
        later = first(items[n + 1]) if n + 1 < len(items) else None
        s, dp, q, g = now
        row = pl.ds(2 * i + head, 1)
        prob, ds = score_grads(s, dp, lse1[peer, row, :], delta1[peer, row, :])
        grad_v = grad_v + dot(prob, g)
        grad_k = grad_k + dot(ds, q)
        now = later
    out[0] = unrotate(grad_k, cos, sin).astype(BF16)
    out[1] = grad_v.astype(BF16)


def attend_back(limit, kernel, at, args, specs, outs, blocks, before, pairs, peers, scratch, flops, name):
    first, count = pairs
    before = () if before is None else tuple(before)
    steps = HEADS // 2
    return pl.pallas_call(
        functools.partial(kernel, first_pair=first, peers=peers),
        grid_spec=pltpu.PrefetchScalarGridSpec(
            num_scalar_prefetch=2,
            grid=(count,),
            in_specs=specs + [pl.BlockSpec(memory_space=pl.ANY)] * len(before),
            out_specs=[pl.BlockSpec((blocks[0], outs[0].shape[1], LANES), lambda i, adapter, at: (blocks[1], 0, i + first))]
            + [pl.BlockSpec((o.shape[0], LANES), lambda i, adapter, at: (0, i + first)) for o in outs[1:]],
            scratch_shapes=scratch,
        ),
        out_shape=outs,
        input_output_aliases={2 + len(args) + n: n for n in range(len(before))},
        compiler_params=params(limit),
        cost_estimate=cost(
            flops * count // steps,
            4 * sum(a.size for a in args[:4]) * count // steps,
            flops * count // steps // 512,
        ),
        name=name,
    )(*at, *args, *before)


def own_back(at, own, peer, go, lse, delta, cos, sin, pairs, before):
    rows = own.shape[1]
    peers = peer.shape[0] // 24
    width = own.shape[0] // 3 * LANES
    first = pairs[0]

    def part(which):
        return pl.BlockSpec((1, rows, LANES), lambda i, adapter, at: (8 * which + first + i, 0, 0))

    table = pl.BlockSpec((rows, LANES), lambda i, adapter, at: (at[0], 0), pipeline_mode=pl.Buffered(1))
    return attend_back(
        24,
        own_back_kernel,
        at,
        (own, own, own, go, lse, delta, cos, sin) + (peer,) * (2 * peers),
        [part(0), part(1), part(2)]
        + [pl.BlockSpec((rows + EXTRA, LANES), lambda i, adapter, at: (0, i + first))]
        + [fixed((HEADS // 2, 2, rows)), fixed((HEADS, rows)), table, table]
        + [part(3 * p + 1) for p in range(peers)]
        + [part(3 * p + 2) for p in range(peers)],
        [jax.ShapeDtypeStruct((3, rows, width), BF16)] + [pltpu.HBM((rows, width), F32)] * 2,
        (1, 2),
        before,
        pairs,
        peers,
        [],
        2 * rows * width * 4 * rows * (5 + 3 * peers),
        "own_back",
    )


def peer_back(at, own, peer, gp, cos, sin, dk, dv, pairs, before):
    rows = own.shape[1]
    peers = gp.shape[0]
    width = own.shape[0] // 3 * LANES
    first = pairs[0]

    def part(which):
        return pl.BlockSpec((1, rows, LANES), lambda i, adapter, at: (8 * which + first + i, 0, 0))

    column = pl.BlockSpec((rows, LANES), lambda i, adapter, at: (0, i + first))
    table = pl.BlockSpec((rows, LANES), lambda i, adapter, at: (at[0], 0), pipeline_mode=pl.Buffered(1))
    return attend_back(
        24,
        peer_back_kernel,
        at,
        (own, own, gp, gp, cos, sin, dk, dv) + (peer,) * peers,
        [
            part(1), part(2),
            pl.BlockSpec((peers, rows + EXTRA, LANES), lambda i, adapter, at: (0, 0, i + first)),
            fixed((peers, EXTRA, width)),
            table, table, column, column,
        ]
        + [part(3 * p) for p in range(peers)],
        [jax.ShapeDtypeStruct((3, rows, width), BF16)],
        (2, 0),
        before,
        pairs,
        peers,
        [pltpu.VMEM((peers, HEADS, rows), F32), pltpu.VMEM((peers, HEADS, rows), F32)],
        2 * rows * width * 4 * 4 * rows * peers,
        "peer_back",
    )


def qkv_grad_kernel(
    _adapter, at, g, low, x, gain, shift, up, stay_out, leave_out, rank_grad, pieces, sems
):
    width = x.shape[1]
    low_t = low[...].T
    total = None
    def put(first, grad):
        for p in range(width // LANES):
            cut = slice(p * LANES, (p + 1) * LANES)
            pieces[position(jnp.int32(first + p), at, 6), 0] = grad[:, cut].astype(BF16)

    for n in range(3):
        grad = g[(n + 2) % 3]
        put(n * (width // LANES), dot(low_t, grad))
        more = dot(grad, up[0, :, n * width : (n + 1) * width], NT)
        total = more if total is None else total + more
    rank = total.astype(BF16)
    rank_grad[...] = rank
    normed, _s = norm_rows(x[...].astype(F32))
    h1 = (normed * gain[...] + shift[...]).astype(BF16)
    put(3 * (width // LANES), dot(rank.T, h1))
    leave = group(
        sems, [(pieces.at[pl.ds(0, 16)], stay_out), (pieces.at[pl.ds(16, 16)], leave_out)]
    )
    start_all(leave)
    wait_all(leave)


def qkv_grad(at, g, low, x, gain, shift, up, groups):
    rows, width = x.shape
    return pl.pallas_call(
        qkv_grad_kernel,
        grid_spec=pltpu.PrefetchScalarGridSpec(
            num_scalar_prefetch=2,
            grid=(1,),
            in_specs=[
                whole((3, rows, width)),
                whole((rows, RANK)),
                whole((rows, width)),
                whole((1, width)),
                whole((1, width)),
                chosen((RANK, 3 * width)),
            ],
            out_specs=[ANY, ANY, whole((rows, RANK))],
            scratch_shapes=[
                pltpu.VMEM((groups, 1, RANK, LANES), BF16),
                pltpu.SemaphoreType.DMA((2,)),
            ],
        ),
        out_shape=[
            jax.ShapeDtypeStruct((groups // 2, 1, RANK, LANES), BF16),
            jax.ShapeDtypeStruct((groups // 2, 1, RANK, LANES), BF16),
            jax.ShapeDtypeStruct((rows, RANK), BF16),
        ],
        compiler_params=params(16),
        cost_estimate=cost(2 * rows * 16 * 3 * width * 4, 8 * rows * width),
        name="qkv_grad",
    )(*at, g, low, x, gain, shift, up)


def input_grad_kernel(_adapter, at, g, w, rank_grad, down, x, gain, dx1, *refs):
    out, total = refs[-2:]
    j = pl.program_id(0)

    @pl.when(j == 0)
    def _():
        total[...] = dot(rank_grad[...], down[0]) + dot(g[0], w[...], NT)

    @pl.when(j == 1)
    def _():
        total[...] += dot(g[0], w[...], NT)

    @pl.when(j == 2)
    def _():
        grad = total[...] + dot(g[0], w[...], NT)
        normed, spread = norm_rows(x[...].astype(F32))
        out[...] = dx1[...] + norm_back(grad, normed, spread, gain[...])


def input_grad(at, g, w, rank_grad, down, x, gain, dx1, half, before=()):
    rows, width = x.shape
    cut = rows // 2
    part = pl.BlockSpec((cut, width), lambda j, adapter, at: (half, 0))
    order = lambda j: lax.rem(j + 1, 3)
    return pl.pallas_call(
        input_grad_kernel,
        grid_spec=pltpu.PrefetchScalarGridSpec(
            num_scalar_prefetch=2,
            grid=(3,),
            in_specs=[
                pl.BlockSpec((1, cut, width), lambda j, adapter, at: (j, half, 0)),
                pl.BlockSpec((width, width), lambda j, adapter, at: (0, order(j))),
                pl.BlockSpec((cut, RANK), lambda j, adapter, at: (half, 0)),
                chosen((RANK, width)),
                part,
                fixed((1, width)),
                part,
            ]
            + [ANY] * len(before),
            out_specs=part,
            scratch_shapes=[pltpu.VMEM((cut, width), F32)],
        ),
        out_shape=jax.ShapeDtypeStruct((rows, width), F32),
        input_output_aliases={9 + n: n for n in range(len(before))},
        compiler_params=params(20),
        cost_estimate=cost(3 * rows * width * width, 6 * width * width + 8 * rows * width),
        name="input_grad",
    )(*at, g, w, rank_grad, down, x, gain, dx1, *before)


def swap_order():
    bits = []
    n = 4
    while n < lax.axis_size("dp"):
        bits.append((n, 0))
        n *= 2
    n = 1
    while n < lax.axis_size("seq"):
        bits.append((0, n))
        n *= 2
    bits.append((2, 0))
    first = bits[:4]
    second = [first[1], first[0], first[3], first[2]]
    return (first, second), bits[4:]


def swap(values, step):
    size, ways = lax.axis_size("dp"), lax.axis_size("seq")
    perm = []
    for d in range(size):
        flip_d, flip_s = step[d & 1]
        for s in range(ways):
            perm.append((d * ways + s, (d ^ flip_d) * ways + (s ^ flip_s)))
    return lax.ppermute(values, ("dp", "seq"), perm)


def device_codes():
    orders, _rest = swap_order()
    size, ways = lax.axis_size("dp"), lax.axis_size("seq")
    table = np.zeros((size * ways, 9 + ways), np.int32)
    for d in range(size):
        for s in range(ways):
            codes = []
            for order in orders:
                on = [((d & bit_d) | (s & bit_s)) != 0 for bit_d, bit_s in order]
                codes.append(
                    (
                        sum(8 >> n for n in range(4) if on[n]),
                        sum(1 << n for n in range(4) if on[n]),
                        8 * on[2] + 4 * on[3],
                    )
                )
            mine, theirs = codes[d & 1], codes[1 - (d & 1)]
            row = [s, d & 1, mine[0], theirs[0], mine[1], theirs[1], mine[2], theirs[2], d]
            table[d * ways + s] = row + [(s + n) % ways for n in range(1, ways)] + [0]
    place = lax.axis_index("dp") * ways + lax.axis_index("seq")
    return lax.dynamic_slice_in_dim(jnp.asarray(table), place, 1, 0)[0]


def slot_masks(sequence):
    orders, _rest = swap_order()
    masks = []
    for order in orders:
        slots = [0, 1]
        for n in sequence:
            slots = slots + [slot ^ order[n][0] for slot in slots]
        masks.append(slots)
    return masks


def scatter_steps():
    orders, _rest = swap_order()
    return [((1, 0), (1, 0))] + list(zip(*orders))


def scatter_stage(held, step):
    half = held.shape[1] // 2
    return jnp.concatenate([held[:, :half], swap(held[:, half:], step)], axis=0)


def owner_sum_kernel(owners, at, held, out, total, *, masks):
    total[...] = jnp.zeros_like(total)
    for n, (even, odd) in enumerate(zip(*masks)):
        mask = even if even == odd else jnp.where(at[1] == 0, even, odd)
        total[owners[at[8] ^ mask]] += held[n].astype(F32)
    for a in range(NADAPT):
        out[:, a] = total[a].astype(BF16)


def owner_sum(at, owners, held, masks):
    slots, groups, parts, rank, lanes = held.shape
    pieces = groups * parts
    held = held.reshape(slots, pieces, rank, lanes)
    step = min(pieces, 4)
    out = pl.pallas_call(
        functools.partial(owner_sum_kernel, masks=masks),
        grid_spec=pltpu.PrefetchScalarGridSpec(
            num_scalar_prefetch=2,
            grid=(pieces // step,),
            in_specs=[pl.BlockSpec((slots, step, rank, lanes), lambda i, *_: (0, i, 0, 0))],
            out_specs=pl.BlockSpec((step, NADAPT, rank, lanes), lambda i, *_: (i, 0, 0, 0)),
            scratch_shapes=[pltpu.VMEM((NADAPT, step, rank, lanes), F32)],
        ),
        out_shape=jax.ShapeDtypeStruct((pieces, NADAPT, rank, lanes), BF16),
        compiler_params=params(12),
        cost_estimate=cost(held.size, 2 * held.size),
        name="owner_sum",
    )(owners, at[1], held)
    out = out.reshape(groups, parts, NADAPT, rank, lanes)
    _orders, rest = swap_order()
    for bits in rest:
        out = (out.astype(F32) + swap(out, (bits, bits)).astype(F32)).astype(BF16)
    return out


def spread_kernel(_adapter, at, mine, theirs, *outs, plan, straight):
    for core in range(2):

        @pl.when(at[1] == core)
        def _():
            for ref, part, first, count in zip(outs, *plan):
                for p in range(count):
                    piece = first + p
                    near = piece >> 4 == core
                    held = mine if near else theirs
                    if straight:
                        low = (piece & 15) ^ (at[6] if near else at[7])
                    else:
                        low = int(f"{piece & 15:04b}"[::-1], 2) ^ (at[4] if near else at[5])
                    ref[:, :, p * LANES : (p + 1) * LANES] = held[low, part].astype(F32)


def spread(at, mine, theirs, plan, straight=False):
    parts, firsts, counts = plan
    shapes = [(NADAPT, RANK, count * LANES) for count in counts]
    return pl.pallas_call(
        functools.partial(spread_kernel, plan=plan, straight=straight),
        grid_spec=pltpu.PrefetchScalarGridSpec(
            num_scalar_prefetch=2,
            grid=(1,),
            in_specs=[whole(mine.shape), whole(theirs.shape)],
            out_specs=[whole(shape) for shape in shapes],
        ),
        out_shape=[jax.ShapeDtypeStruct(shape, F32) for shape in shapes],
        compiler_params=params(20),
        cost_estimate=cost(1, 12 * mine.size),
        name="spread",
    )(*at, mine, theirs)


def tie(*values):
    flat, tree = jax.tree.flatten(values)
    return jax.tree.unflatten(tree, lax.optimization_barrier(flat))


def body(
    clip_tokens, adapter_index, ln1_gain, ln1_bias, qkv_weight, qkv_bias, qkv_down, qkv_up,
    out_weight, out_bias, out_down, out_up, ln2_gain, ln2_bias, fc1_weight, fc1_bias, fc1_down,
    fc1_up, fc2_weight, fc2_bias, fc2_down, fc2_up, cotangent,
):
    _one, rows, width = clip_tokens.shape
    devices = lax.axis_size("seq")
    groups = 32
    pin = lambda v: pltpu.with_memory_space_constraint(v, pltpu.HBM)
    row = lambda v: pin(v.reshape(1, -1))
    x = pin(clip_tokens[0])
    cot = cotangent[0]
    free_qkv, free_fc2 = qkv_weight, fc2_weight
    qkv_weight, qkv_down, qkv_up = pin(qkv_weight), pin(qkv_down), pin(qkv_up)
    out_weight, out_down, out_up = pin(out_weight), pin(out_down), pin(out_up)
    fc1_weight, fc1_down, fc1_up = pin(fc1_weight), pin(fc1_down), pin(fc1_up)
    fc2_weight, fc2_down, fc2_up = pin(fc2_weight), pin(fc2_down), pin(fc2_up)
    peers = range(1, devices)
    at = (adapter_index, device_codes())
    tagged = jnp.broadcast_to(adapter_index.astype(BF16)[:, None], (256, LANES))
    tagged, cot = tie(tagged, cot)
    tags = lax.all_gather(tagged, "dp", axis=0, tiled=True)
    masks_a, masks_b = slot_masks((0, 1, 2, 3)), slot_masks((2, 3, 0, 1))

    def from_peer(values, shift):
        return lax.ppermute(values, "seq", [((n + shift) % devices, n) for n in range(devices)])

    tables = tuple(pin(jnp.asarray(t)) for t in rotary_tables(rows * devices))
    cos, sin = tables
    x_peer = jnp.concatenate([from_peer(clip_tokens[0], n) for n in peers], axis=0)
    first_set = (row(ln1_gain), row(ln1_bias), qkv_weight, row(qkv_bias), qkv_down, qkv_up)
    own, mixed, back, low_qkv, top, total, grad2 = front_rows(
        at, x, pin(cot), first_set, tables, fc2_weight, fc2_down, fc2_up
    )
    peer, act, x1, low2, dx1, go, delta, lse, *pieces_a = middle_rows(
        at, x_peer, first_set, tables, pin(own), (pin(mixed), pin(top), pin(total)), x, pin(cot), pin(back), pin(grad2),
        (out_weight, row(out_bias), out_down, out_up),
        (row(ln2_gain), row(ln2_bias)),
        (fc1_weight, row(fc1_bias), fc1_down, fc1_up),
        fc2_down, groups,
    )
    own, peer, lse = pin(own), pin(peer), pin(lse)
    go_sent, kept, sent, delta, tags = tie(go, pieces_a[0][None], pieces_a[1][None], delta, tags)
    index_all = tags[::256, 0].astype(jnp.int32)
    go_peer = jnp.stack([from_peer(go_sent, n) for n in peers])
    steps = scatter_steps()

    def halves(held):
        half = held.shape[1] // 2
        return held[:, :half], held[:, half:]

    def join(*parts):
        return jnp.concatenate(parts, axis=0)

    arrived = swap(sent, steps[0])
    kept, sent = halves(join(kept, arrived))
    sent, delta = tie(sent, delta)
    arrived = swap(sent, steps[1])
    back = functools.partial(own_back, at, own, peer, pin(go), lse, pin(delta), cos, sin)
    grads = back((0, 4), None)
    arrived, grads = tie(arrived, grads)
    kept, sent = halves(join(kept, arrived))
    sent, grads = tie(sent, grads)
    arrived = swap(sent, steps[2])
    grads, dk, dv = back((4, 4), grads)
    arrived, dk, go_peer = tie(arrived, dk, go_peer)
    dk, dv = pin(dk), pin(dv)
    kept, sent = halves(join(kept, arrived))
    sent, go_peer = tie(sent, go_peer)
    arrived = swap(sent, steps[3])
    grads = peer_back(at, own, peer, go_peer, cos, sin, dk, dv, (0, 8), (grads,))[0]
    arrived, grads = tie(arrived, grads)
    kept_a, sent = halves(join(kept, arrived))
    sent, grads = tie(sent, grads)
    arrived_a = swap(sent, steps[4])
    kept, sent, rank_grad = qkv_grad(
        at, grads, low_qkv, x, row(ln1_gain), row(ln1_bias), qkv_up, groups
    )
    arrived_a, sent, rank_grad = tie(arrived_a, sent, rank_grad)
    held = join(kept[None], swap(sent[None], steps[0]))
    total_a = owner_sum(at, index_all, join(kept_a, arrived_a), masks_a)

    def grad_half(half, rank_grad, before=()):
        return input_grad(
            at, grads, free_qkv, rank_grad, qkv_down, x, row(ln1_gain), pin(dx1), half, before
        )

    def output_half(half, low2, before=()):
        return output_rows(at, pin(act), free_fc2, pin(x1), row(fc2_bias), low2, fc2_up, half, before)

    kept, sent = halves(held)
    arrived = swap(sent, steps[3])
    sent, total_a, rank_grad = tie(sent, total_a, rank_grad)
    arrived_a = swap(total_a, steps[1])
    grad_in = grad_half(0, rank_grad)
    arrived, arrived_a, rank_grad, grad_in = tie(arrived, arrived_a, rank_grad, grad_in)
    kept, sent = halves(join(kept, arrived))
    total_a = join(total_a, arrived_a)
    sent, total_a, rank_grad = tie(sent, total_a, rank_grad)
    arrived = swap(sent, steps[4])
    arrived_a = swap(total_a, steps[2])
    grad_in = grad_half(1, rank_grad, (grad_in,))
    arrived, arrived_a, grad_in = tie(arrived, arrived_a, grad_in)
    held, total_a = join(kept, arrived), join(total_a, arrived_a)
    held, total_a, low2 = tie(held, total_a, low2)
    arrived = swap(held, steps[1])
    arrived_a = swap(total_a, steps[3])
    block_output = output_half(0, low2)
    arrived, arrived_a, low2, block_output = tie(arrived, arrived_a, low2, block_output)
    held, total_a = join(held, arrived), join(total_a, arrived_a)
    held, total_a, low2 = tie(held, total_a, low2)
    arrived = swap(held, steps[2])
    arrived_a = swap(total_a, steps[4])
    block_output = output_half(1, low2, (block_output,))
    arrived, block_output = tie(arrived, block_output)
    total_b = owner_sum(at, index_all, join(held, arrived), masks_b)
    total_b, arrived_a = tie(total_b, arrived_a)
    total_a = join(total_a, arrived_a)
    arrived = swap(total_b, steps[4])
    theirs_a = swap(total_a, steps[0])
    total_b = join(total_b, arrived)
    total_b, total_a, theirs_a = tie(total_b, total_a, theirs_a)
    arrived = swap(total_b, steps[3])
    per = width // LANES
    spread_a = spread(
        at, total_a, theirs_a,
        ((0, 1, 2, 2, 2, 2), (0, 0, 0, per, 2 * per, 3 * per), (32, 32, per, per, per, per)),
    )
    arrived, spread_a = tie(arrived, spread_a)
    up1, down2, up2, down1, up_o, down_o = spread_a
    total_b = join(total_b, arrived)
    up_qkv, down_qkv = spread(
        at, total_b, swap(total_b, steps[0]), ((0, 0), (0, 3 * per), (3 * per, per)), straight=True
    )
    return (
        block_output[None], grad_in[None], down_qkv, up_qkv, down_o, up_o, down1, up1, down2, up2,
    )


def solution(mesh):
    split = P("dp", "seq", None)
    return jax.shard_map(
        body,
        mesh=mesh,
        in_specs=(split, P("dp")) + (P(),) * 20 + (split,),
        out_specs=(split, split) + (P(),) * 8,
        check_vma=False,
    )
```
